32 devices in a mesh: lat: 4 (over y, x), lon: 8 (over z, core).
Axes of the slice: x: 2, y: 2, z: 4, core: 2. Of those that a mesh axis runs over, the one named last changes fastest.
Arguments:
- background: bfloat16 [64, 256, 512], P('lat', 'lon'), may hold values from -6 to 6
- obs_rows: bfloat16 [16384, 256], P(('lat', 'lon')), may hold values from -6 to 6
- obs_pixel: int32 [16384], P(('lat', 'lon')), may hold values from 0 to 16383, as said below
- obs_count: int32 [32], P(('lat', 'lon')), may hold values from 256 to 512, as said below
- block_pattern: int32 [8, 32, 4], P('lat', 'lon'), may hold values 0 or 1
- w_enc: bfloat16 [256, 512], replicated, may hold values from -0.375 to 0.375
- w_qkv: bfloat16 [512, 1536], replicated, may hold values from -0.375 to 0.375
- w_out: bfloat16 [512, 512], replicated, may hold values from -0.25 to 0.25
- cotangent: bfloat16 [64, 256, 512], P('lat', 'lon'), may hold values from -6 to 6
Outputs:
- updated: bfloat16 [64, 256, 512], P('lat', 'lon')
- grad_background: bfloat16 [64, 256, 512], P('lat', 'lon')
- grad_obs: bfloat16 [16384, 256], P(('lat', 'lon'))
The draws below stay inside these ranges and needn't reach their ends.
Inputs may be any that keep to these rules, and one draw needn't show every extreme that they name: obs_count[d] counts the live rows of device d of lat+lon; its rows are the 512 rows starting at d * 512. `obs_pixel`: each entry names a pixel as latitude_row * 256 + column, with latitude_row its row index in the slab and column its index along the row. Among the live rows of one device, at most 18 name pixels of one device of lat+lon; in every draw one device receives exactly 18 live rows from every device.
All inputs are finite; a program needn't handle non-finite values. No bound on the sum of `block_pattern` on one device may be relied on, other than what follows from the above.
Results may differ from the reference program's by a relative error of at most 0.018.
Values may be sent and summed in bfloat16 or wider, within the bound.
No kernel may reach another device: no remote copies, remote signals or barrier semaphores. Data moves between devices by JAX's collectives and lax.ppermute only.
A program may use at most 192 MiB of HBM per device.

```python
import math
import jax
import jax.numpy as jnp
from jax import lax

C = 512
HEADS = 8
F_OBS = 256
BLOCK = 8
R_DEV = 16
L_DEV = 32
OBS_DEV = 512
NRING = 64
NLON = 256
NOBS = 16384
N_LAT = 4
N_LON = 8


def draw_obs_pixel(key, part):
    dev_count = N_LAT * N_LON
    capacity = (OBS_DEV + dev_count - 1) // dev_count + 2
    half_slots = OBS_DEV // 2
    hot_owner = jax.random.randint(jax.random.fold_in(key, 11), (), 0, dev_count)

    def one_device(device):
        dev_key = jax.random.fold_in(jax.random.fold_in(key, 12), device)
        key_offset, key_first, key_second, key_local = jax.random.split(dev_key, 4)
        offset = jax.random.randint(key_offset, (), 0, dev_count - 1)
        position = jnp.arange(OBS_DEV - capacity, dtype=jnp.int32)
        others = (hot_owner + 1 + (position + offset) % (dev_count - 1)) % dev_count
        destination = jnp.concatenate([jnp.full((capacity,), hot_owner, jnp.int32), others.astype(jnp.int32)])
        first_half = jax.random.permutation(key_first, destination[:half_slots])
        second_half = jax.random.permutation(key_second, destination[half_slots:])
        owner_dev = jnp.concatenate([first_half, second_half])
        local_pixel = jax.random.randint(key_local, (OBS_DEV,), 0, R_DEV * L_DEV)
        lat_row = owner_dev // N_LON * R_DEV + local_pixel // L_DEV
        lon_col = owner_dev % N_LON * L_DEV + local_pixel % L_DEV
        return (lat_row * (L_DEV * N_LON) + lon_col).astype(jnp.int32)
    return jax.vmap(one_device)(jnp.arange(dev_count, dtype=jnp.int32)).reshape(-1)


def draw_obs_count(key, part):
    dev_count = N_LAT * N_LON
    counts = jax.random.randint(jax.random.fold_in(key, 21), (dev_count,), OBS_DEV // 2, OBS_DEV + 1)
    full_dev = jax.random.randint(jax.random.fold_in(key, 22), (), 0, dev_count)
    half_dev = (full_dev + 1 + jax.random.randint(jax.random.fold_in(key, 23), (), 0, dev_count - 1)) % dev_count
    device = jnp.arange(dev_count, dtype=jnp.int32)
    counts = jnp.where(device == full_dev, OBS_DEV, counts)
    counts = jnp.where(device == half_dev, OBS_DEV // 2, counts)
    return counts.astype(jnp.int32)


def set_ends(values, key, smallest, high):
    spot = [jax.random.randint(jax.random.fold_in(key, axis), (), 0, length) for axis, length in enumerate(values.shape)]
    main_axis = values.shape.index(max(values.shape))
    neighbour = spot[:main_axis] + [(spot[main_axis] + 1) % values.shape[main_axis]] + spot[main_axis + 1:]
    return values.at[tuple(spot)].set(smallest).at[tuple(neighbour)].set(high)


def block_levels(rng, dims, cuts, smallest, top_value):
    level = 1.0
    for dim, shards_of in cuts:
        heights = jax.random.uniform(jax.random.fold_in(jax.random.fold_in(rng, 6), dim), (shards_of,), jnp.float32, smallest / len(cuts), top_value / len(cuts))
        level = level * jnp.repeat(jnp.exp(heights), dims[dim] // shards_of).reshape((-1,) + (1,) * (len(dims) - 1 - dim))
    return level


def bell_draw(own_key, shape, scale, most, cuts=(), kind=jnp.bfloat16):
    entries = jax.random.normal(own_key, shape, jnp.float32) * scale
    if len(cuts) > 0:
        entries = block_levels(own_key, shape, cuts, -0.22, 0.18) * entries
    return jnp.clip(entries, min=-most, max=most).astype(kind)


def setup_inputs(seed: int = 0) -> dict:
    seeds = jax.random.split(jax.random.key(seed), 10)
    background = bell_draw(seeds[0], (NRING, NLON, C), 1.0, 6.0, ((0, 4), (1, 8)))
    obs_rows = bell_draw(seeds[1], (NOBS, F_OBS), 1.0, 6.0, ((0, 32),))
    obs_pixel = draw_obs_pixel(jax.random.fold_in(seeds[9], 71), 0)
    obs_count = draw_obs_count(jax.random.fold_in(seeds[9], 71), 0)
    block_pattern = set_ends((jax.random.randint(seeds[4], (NRING // BLOCK, NLON // BLOCK, 4), 0, 4) < 3).astype(jnp.int32), jax.random.fold_in(seeds[4], 1), 0, 1)
    w_enc = bell_draw(seeds[5], (F_OBS, C), F_OBS ** -0.5, 0.375)
    w_qkv = bell_draw(seeds[6], (C, 3 * C), (C // 2) ** -0.5, 0.375)
    w_out = bell_draw(seeds[7], (C, C), C ** -0.5, 0.25)
    cotangent = bell_draw(seeds[8], (NRING, NLON, C), 1.0, 6.0, ((0, 4), (1, 8)))
    return {"background": background, "obs_rows": obs_rows, "obs_pixel": obs_pixel, "obs_count": obs_count, "block_pattern": block_pattern, "w_enc": w_enc, "w_qkv": w_qkv, "w_out": w_out, "cotangent": cotangent}


norm_eps = 1e-06
gelu_coef = 0.7978845608028654

def gelu_tanh(inputs):
    inner_arg = gelu_coef * (inputs + 0.044715 * inputs * inputs * inputs)
    return 0.5 * inputs * (1.0 + jnp.tanh(inner_arg))

def gelu_slope(inputs):
    inner_arg = gelu_coef * (inputs + 0.044715 * inputs * inputs * inputs)
    tangent = jnp.tanh(inner_arg)
    return 0.5 * (1.0 + tangent) + 0.5 * inputs * (1.0 - tangent * tangent) * gelu_coef * (1.0 + 3.0 * 0.044715 * inputs * inputs)

def to_blocks(field_grid):
    rows_all, cols_all, depth_dim = field_grid.shape
    shaped = field_grid.reshape(rows_all // BLOCK, BLOCK, cols_all // BLOCK, BLOCK, depth_dim)
    return shaped.transpose(0, 2, 1, 3, 4).reshape(rows_all // BLOCK, cols_all // BLOCK, BLOCK * BLOCK, depth_dim)

def from_blocks(blocks):
    row_blocks, col_blocks, block_area, depth_dim = blocks.shape
    shaped = blocks.reshape(row_blocks, col_blocks, BLOCK, BLOCK, depth_dim)
    return shaped.transpose(0, 2, 1, 3, 4).reshape(row_blocks * BLOCK, col_blocks * BLOCK, depth_dim)

def attend(queries, key_rows, grad_heads, key_mask):
    row_blocks, col_blocks, block_area, channels = queries.shape
    head_dim = channels // HEADS
    query_shape = (row_blocks, col_blocks, block_area, HEADS, head_dim)
    key_shape = (row_blocks, col_blocks, 5, block_area, HEADS, head_dim)
    query_heads = queries.reshape(query_shape).astype(jnp.float32)
    key_heads = key_rows[..., :channels].reshape(key_shape).astype(jnp.float32)
    value_heads = key_rows[..., channels:].reshape(key_shape).astype(jnp.float32)
    grad_split = grad_heads.reshape(query_shape).astype(jnp.float32)
    score_scale = 1.0 / math.sqrt(head_dim)
    scores = jnp.einsum('abqhd,abokhd->abhqok', query_heads, key_heads)
    live_keys = lax.optimization_barrier(jnp.sum(key_mask, axis=-1)) * float(block_area)
    offset_bias = -jnp.log(live_keys)[:, :, None, None, None, None]
    gate_mask = key_mask[:, :, None, None, :, None]
    weights = jax.nn.sigmoid(scores * score_scale + offset_bias) * gate_mask
    weights_bf = weights.astype(jnp.bfloat16)
    mixed_heads = jnp.einsum('abhqok,abokhd->abqhd', weights_bf.astype(jnp.float32), value_heads)
    mixed_heads = mixed_heads.astype(jnp.bfloat16).reshape(row_blocks, col_blocks, block_area, channels)
    grad_weights = jnp.einsum('abqhd,abokhd->abhqok', grad_split, value_heads)
    grad_scores = (grad_weights * weights * (1.0 - weights) * score_scale).astype(jnp.bfloat16).astype(jnp.float32)
    grad_query = jnp.einsum('abhqok,abokhd->abqhd', grad_scores, key_heads)
    grad_query = grad_query.astype(jnp.bfloat16).reshape(row_blocks, col_blocks, block_area, channels)
    grad_key = jnp.einsum('abhqok,abqhd->abokhd', grad_scores, query_heads)
    grad_value = jnp.einsum('abhqok,abqhd->abokhd', weights_bf.astype(jnp.float32), grad_split)
    flat_shape = (row_blocks, col_blocks, 5, block_area, channels)
    contrib = jnp.concatenate([grad_key.reshape(flat_shape), grad_value.reshape(flat_shape)], axis=-1)
    return (mixed_heads, grad_query, contrib)

def reference(background, obs_rows, obs_pixel, obs_count, block_pattern, w_enc, w_qkv, w_out, cotangent):
    lat_rows = R_DEV * N_LAT
    lon_all = L_DEV * N_LON
    pixels = lat_rows * lon_all
    position = jnp.arange(NOBS, dtype=jnp.int32) % OBS_DEV
    is_live = position < jnp.repeat(obs_count, OBS_DEV)
    live_float = is_live.astype(jnp.float32)
    obs_pre = jnp.dot(obs_rows, w_enc, preferred_element_type=jnp.float32)
    encoded = gelu_tanh(obs_pre).astype(jnp.bfloat16)
    obs_sum = jax.ops.segment_sum(encoded.astype(jnp.float32) * live_float[:, None], obs_pixel, num_segments=pixels)
    obs_number = jax.ops.segment_sum(live_float, obs_pixel, num_segments=pixels)
    denominator = 1.0 + obs_number
    state_in = (background.reshape(pixels, C).astype(jnp.float32) + obs_sum / denominator[:, None]).astype(jnp.bfloat16)
    state_f32 = state_in.astype(jnp.float32)
    inv_rms = lax.rsqrt(lax.optimization_barrier(jnp.mean(state_f32 * state_f32, axis=1, keepdims=True)) + norm_eps)
    normed = state_f32 * inv_rms
    normed_bf = normed.astype(jnp.bfloat16)
    projected = jnp.dot(normed_bf, w_qkv, preferred_element_type=jnp.float32).astype(jnp.bfloat16)
    grad_out = jnp.dot(cotangent.reshape(pixels, C), w_out.T, preferred_element_type=jnp.float32).astype(jnp.bfloat16)
    query_blocks = to_blocks(projected[:, :C].reshape(lat_rows, lon_all, C))
    keyval_blocks = to_blocks(projected[:, C:].reshape(lat_rows, lon_all, 2 * C))
    grad_blocks = to_blocks(grad_out.reshape(lat_rows, lon_all, C))
    pattern_float = block_pattern.astype(jnp.float32)
    self_column = jnp.ones(pattern_float.shape[:2] + (1,), jnp.float32)
    key_mask = jnp.concatenate([pattern_float[..., :2], self_column, pattern_float[..., 2:]], axis=-1)
    col_blocks = lon_all // BLOCK
    dev_blocks = L_DEV // BLOCK
    key_block = jnp.arange(col_blocks, dtype=jnp.int32)
    key_sector = key_block // dev_blocks

    def per_row(packed):
        queries, key_vals, grad_heads, row_mask = packed
        key_rows = jnp.stack([jnp.roll(key_vals, -shift, axis=0) for shift in range(-2, 3)], axis=1)
        mixed_heads, grad_query, contrib = attend(queries[None], key_rows[None], grad_heads[None], row_mask[None])
        own_sum = jnp.zeros(key_vals.shape, jnp.float32)
        west_sum = jnp.zeros(key_vals.shape, jnp.float32)
        east_sum = jnp.zeros(key_vals.shape, jnp.float32)
        for index, shift in enumerate(range(-2, 3)):
            moved = jnp.roll(contrib[0, :, index], shift, axis=0)
            source_sector = (key_block - shift) % col_blocks // dev_blocks
            relation = ((source_sector - key_sector) % N_LON)[:, None, None]
            own_sum = own_sum + jnp.where(relation == 0, moved, 0.0)
            west_sum = west_sum + jnp.where(relation == N_LON - 1, moved, 0.0)
            east_sum = east_sum + jnp.where(relation == 1, moved, 0.0)
        own_round = lax.optimization_barrier(own_sum.astype(jnp.bfloat16)).astype(jnp.float32)
        west_round = lax.optimization_barrier(west_sum.astype(jnp.bfloat16)).astype(jnp.float32)
        east_round = lax.optimization_barrier(east_sum.astype(jnp.bfloat16)).astype(jnp.float32)
        grad_total = own_round + west_round + east_round
        return (mixed_heads[0], grad_query[0], grad_total.astype(jnp.bfloat16))
    mixed_all, grad_q_all, grad_kv_all = lax.map(per_row, (query_blocks, keyval_blocks, grad_blocks, key_mask))
    mixed_grid = from_blocks(mixed_all).reshape(pixels, C)
    attn_out = jnp.dot(mixed_grid, w_out, preferred_element_type=jnp.float32)
    updated = (state_f32 + attn_out).astype(jnp.bfloat16).reshape(lat_rows, lon_all, C)
    grad_proj = jnp.concatenate([from_blocks(grad_q_all).reshape(pixels, C), from_blocks(grad_kv_all).reshape(pixels, 2 * C)], axis=1)
    grad_normed = jnp.dot(grad_proj, w_qkv.T, preferred_element_type=jnp.float32)
    cot_float = cotangent.reshape(pixels, C).astype(jnp.float32)
    grad_state = cot_float + inv_rms * (grad_normed - normed * lax.optimization_barrier(jnp.mean(grad_normed * normed, axis=1, keepdims=True)))
    grad_background = grad_state.astype(jnp.bfloat16).reshape(lat_rows, lon_all, C)
    grad_scaled = grad_state / denominator[:, None]
    grad_enc = (jnp.take(grad_scaled, obs_pixel, axis=0) * live_float[:, None]).astype(jnp.bfloat16)
    grad_pre = (grad_enc.astype(jnp.float32) * gelu_slope(obs_pre)).astype(jnp.bfloat16)
    grad_obs = jnp.dot(grad_pre, w_enc.T, preferred_element_type=jnp.float32).astype(jnp.bfloat16)
    return (updated, grad_background, grad_obs)
```

```python
import functools
import math

import jax
import jax.numpy as jnp
from jax import lax
from jax.experimental import pallas as pl
from jax.experimental.pallas import tpu as pltpu
from jax.sharding import PartitionSpec as P

HEADS = 8
BLOCK = 8
HALF = 2 * BLOCK
TILE = BLOCK * HALF
SLAB = 128
MASKED = -1e30

norm_eps = 1e-06
gelu_coef = 0.7978845608028654

bf16 = jnp.bfloat16
f32 = jnp.float32
i32 = jnp.int32


def iota(shape, dim):
    return lax.broadcasted_iota(i32, shape, dim)


def mm(lhs, rhs, lhs_dim=1, rhs_dim=0):
    return lax.dot_general(
        lhs, rhs, (((lhs_dim,), (rhs_dim,)), ((), ())), preferred_element_type=f32
    )


def one_hot(cond):
    return jnp.where(cond, 1.0, 0.0).astype(bf16)


def gelu_parts(inputs):
    square = inputs * inputs
    tangent = jnp.tanh(gelu_coef * inputs * (1.0 + 0.044715 * square))
    return square, tangent


def call(body, outs, scratch=(), flops=0, n_smem=(), n_in=0, size=1 << 20):
    in_specs = [
        pl.BlockSpec(memory_space=pltpu.SMEM if k in n_smem else pltpu.VMEM) for k in range(n_in)
    ]
    return pl.pallas_call(
        body,
        out_shape=[jax.ShapeDtypeStruct(s, d) for s, d in outs],
        in_specs=in_specs,
        out_specs=[pl.BlockSpec(memory_space=pltpu.VMEM) for _ in outs],
        scratch_shapes=list(scratch),
        compiler_params=pltpu.CompilerParams(vmem_limit_bytes=40 << 20),
        cost_estimate=pl.CostEstimate(flops=flops, bytes_accessed=size, transcendentals=0),
    )


def chunk(ref, row_block, half):
    part = ref[
        row_block * BLOCK : (row_block + 1) * BLOCK, half * HALF : (half + 1) * HALF, :
    ]
    return part.reshape(TILE, part.shape[-1])


def halves():
    return [(i, u) for i in range(2) for u in range(2)]


def rows_of(i, u):
    return slice((i * 2 + u) * TILE, (i * 2 + u + 1) * TILE)


def key_count(pat, i, b):
    return 1 + pat[i, b, 0] + pat[i, b, 1] + pat[i, b, 2] + pat[i, b, 3]


def mask_value(pat, i, b, shift):
    if abs(shift) > 2:
        return jnp.int32(0)
    if shift == 0:
        return jnp.int32(1)
    return pat[i, b, shift + 2 if shift < 0 else shift + 1]


def half_bias(count):
    bias = jnp.float32(-0.5 * math.log(64.0))
    for n in range(2, 6):
        bias = jnp.where(count == n, jnp.float32(-0.5 * math.log(64.0 * n)), bias)
    return bias


def own_bias(pat, i, u, turn):
    second_q = iota((TILE, TILE), 0) % HALF >= BLOCK
    second_k = iota((TILE, TILE), 1) % HALF >= BLOCK
    parts = []
    for qb in range(2):
        bias = half_bias(key_count(pat, i, 2 * u + qb))
        pair = [
            jnp.where(mask_value(pat, i, 2 * u + qb, 2 * turn + kb - qb) > 0, bias, MASKED)
            for kb in range(2)
        ]
        parts.append(jnp.where(second_k, pair[1], pair[0]))
    return jnp.where(second_q, parts[1], parts[0])


def pack_body(geo, pix_ref, cnt_ref, pat_ref, rows_ref, cot_ref, pay_ref, slot_ref, east_ref, west_ref):
    devs, cap, span, lon_bits, lon_devs = geo
    slots = pix_ref.shape[1]
    pix = pix_ref[...]
    lat = lax.shift_right_logical(pix, lon_bits)
    lon = lax.bitwise_and(pix, (1 << lon_bits) - 1)
    owner = lax.shift_right_logical(lat, 4) * lon_devs + lax.shift_right_logical(lon, 5)
    row = lax.bitwise_and(lat, 15)
    col = lax.bitwise_and(lon, 31)
    code = (
        lax.shift_right_logical(row, 3) * (2 * TILE)
        + lax.shift_right_logical(col, 4) * TILE
        + lax.bitwise_and(row, 7) * HALF
        + lax.bitwise_and(col, 15)
        + 1
    )
    live = iota((1, slots), 1) < cnt_ref[0]
    table = (iota((devs, slots), 0) == owner) & live
    table_f = jnp.where(table, 1.0, 0.0)
    table_b = table_f.astype(bf16)
    upper = one_hot(iota((slots, slots), 0) <= iota((slots, slots), 1))
    running = mm(table_b, upper)
    rank = (jnp.sum(running * table_f, axis=0, keepdims=True) - 1.0).astype(i32)
    slot = jnp.where(live, owner * span + rank, -1)
    slot_ref[...] = slot
    spread = one_hot(iota((devs * span, slots), 0) == slot)
    high = lax.shift_right_logical(code, 5).astype(f32)
    low = lax.bitwise_and(code, 31).astype(f32)
    place = iota((256, slots), 0)
    codes = jnp.where(place == rank, high, 0.0) + jnp.where(place == rank + 128, low, 0.0)
    meta = mm(table_b, codes.astype(bf16), 1, 1)
    lift = one_hot(iota((devs * span, devs), 0) == iota((devs * span, devs), 1) * span + cap)
    pay_ref[...] = (mm(spread, rows_ref[...]) + mm(lift, meta.astype(bf16))).astype(bf16)
    lane = iota((HALF, 4 * TILE), 1)
    line = iota((HALF, 4 * TILE), 0)
    second_k = lane % HALF >= BLOCK
    for ref, u, turn in ((east_ref, 1, 1), (west_ref, 0, -1)):
        extra = jnp.zeros((HALF, 4 * TILE), f32)
        for i in range(2):
            ref[i * TILE : (i + 1) * TILE, :] = chunk(cot_ref, i, u)
            for qb in range(2):
                pair = [
                    mask_value(pat_ref, i, 2 * u + qb, 2 * turn + kb - qb).astype(f32)
                    for kb in range(2)
                ]
                mask = jnp.where(second_k, pair[1], pair[0])
                count = key_count(pat_ref, i, 2 * u + qb).astype(f32)
                here = (line == i) & (lane >= qb * TILE) & (lane < (qb + 1) * TILE)
                there = (line == i) & (lane >= (qb + 2) * TILE) & (lane < (qb + 3) * TILE)
                extra = jnp.where(here, mask, jnp.where(there, count, extra))
        ref[2 * TILE : 2 * TILE + HALF, :] = extra.astype(bf16)


def grad_body(cot_ref, west_ref, east_ref, wout_ref, gm_ref, gmt_ref, gw_ref, gwt_ref, ge_ref, get_ref, bw_ref, be_ref):
    wout = wout_ref[...]
    for i, u in halves():
        part = mm(chunk(cot_ref, i, u), wout, 1, 1)
        gm_ref[rows_of(i, u), :] = part.astype(bf16)
        gmt_ref[:, rows_of(i, u)] = part.T.astype(bf16)
    second_q = iota((TILE, TILE), 0) % HALF >= BLOCK
    for src, dst, dst_t, bias_ref in ((west_ref, gw_ref, gwt_ref, bw_ref), (east_ref, ge_ref, get_ref, be_ref)):
        part = mm(src[0 : 2 * TILE, :], wout, 1, 1)
        dst[...] = part.astype(bf16)
        dst_t[...] = part.T.astype(bf16)
        extra = src[2 * TILE : 2 * TILE + HALF, :].astype(f32)
        for i in range(2):
            line = extra[i : i + 1, :]
            mask = jnp.where(second_q, line[:, TILE : 2 * TILE], line[:, 0:TILE])
            count = jnp.where(second_q, line[:, 3 * TILE : 4 * TILE], line[:, 2 * TILE : 3 * TILE])
            bias = -0.5 * jnp.log(count * 64.0)
            bias_ref[i * TILE : (i + 1) * TILE, :] = jnp.where(mask > 0.5, bias, MASKED)


def state_body(geo, arr_ref, wenc_ref, bg_ref, state_ref, n_ref, n0_ref, n1_ref, inv_ref, oht_ref):
    devs, cap, span = geo
    slots = devs * span
    arr = arr_ref[...]
    pick = one_hot(iota((devs, slots), 1) == iota((devs, slots), 0) * span + cap)
    meta = mm(pick, arr).astype(bf16)
    owner = one_hot(iota((devs, span, devs), 0) == iota((devs, span, devs), 2)).reshape(slots, devs)
    wide = mm(owner, meta)
    here = (iota((devs, span, 128), 1) == iota((devs, span, 128), 2)).reshape(slots, 128)
    code = jnp.sum(
        jnp.where(here, wide[:, 0:128] * 32.0 + wide[:, 128:256], 0.0), axis=1, keepdims=True
    ).astype(i32)
    pixels = n_ref.shape[0]
    oht = one_hot(code == iota((slots, pixels), 1) + 1)
    oht_ref[...] = oht
    pre = mm(arr, wenc_ref[...])
    _, tangent = gelu_parts(pre)
    encoded = (0.5 * pre * (1.0 + tangent)).astype(bf16)
    obs_sum = mm(oht, encoded, 0, 0)
    number = mm(oht, jnp.ones((slots, 128), bf16), 0, 0)
    inverse = 1.0 / (1.0 + number)
    inv_ref[...] = inverse
    for i, u in halves():
        rows = rows_of(i, u)
        fresh = obs_sum[rows] * inverse[rows, 0:1]
        state = (chunk(bg_ref, i, u).astype(f32) + fresh).astype(bf16)
        state_ref[rows, :] = state
        wide_state = state.astype(f32)
        inv_rms = lax.rsqrt(jnp.mean(wide_state * wide_state, axis=1, keepdims=True) + norm_eps)
        normed = (wide_state * inv_rms).astype(bf16)
        n_ref[rows, :] = normed
        side = n1_ref if u else n0_ref
        side[i * TILE : (i + 1) * TILE, :] = normed


def head_lanes(shape, head, dim=1):
    return lax.shift_right_logical(iota(shape, dim), 6) == head


def split_heads(slab):
    return [jnp.where(head_lanes(slab.shape, h), slab, jnp.zeros((), slab.dtype)) for h in range(2)]


def weigh(q2, g2, km, vm, bias):
    tangent = jnp.tanh(mm(q2, km, 1, 1) + bias)
    weight = tangent + 1.0
    slope = mm(g2, vm, 1, 1) * weight * (2.0 - weight)
    return weight.astype(bf16), slope.astype(bf16)


def own_body(
    n_ref, wqkv_ref, gm_ref, gmt_ref, pat_ref, arr_ref, wenc_ref,
    q_ref, qt_ref, k_ref, v_ref, mixed_ref, dq_ref, dkt_ref, dvt_ref, slope_ref,
):
    normed = n_ref[...]
    chans = normed.shape[1]
    queries = mm(normed, wqkv_ref[:, 0:chans]).astype(bf16).astype(f32) * 0.0625
    q_ref[...] = queries.astype(bf16)
    qt_ref[...] = queries.T.astype(bf16)
    k_ref[...] = mm(normed, wqkv_ref[:, chans : 2 * chans]).astype(bf16)
    v_ref[...] = mm(normed, wqkv_ref[:, 2 * chans : 3 * chans]).astype(bf16)
    for i in range(2):
        keys = slice(i * 2 * TILE, (i + 1) * 2 * TILE)
        bias = [
            jnp.concatenate([own_bias(pat_ref, i, u, -u), own_bias(pat_ref, i, u, 1 - u)], axis=1)
            for u in range(2)
        ]
        bias = jnp.concatenate(bias, axis=0)
        for s in range(chans // SLAB):
            lanes = slice(s * SLAB, (s + 1) * SLAB)
            km = split_heads(k_ref[keys, lanes])
            vm = split_heads(v_ref[keys, lanes])
            mixed = jnp.zeros((2 * TILE, SLAB), f32)
            grad_q = jnp.zeros((2 * TILE, SLAB), f32)
            for h in range(2):
                weight, slope = weigh(q_ref[keys, lanes], gm_ref[keys, lanes], km[h], vm[h], bias)
                mixed = mixed + mm(weight, vm[h])
                grad_q = grad_q + mm(slope, km[h])
                chan = slice(s * SLAB + h * 64, s * SLAB + (h + 1) * 64)
                dkt_ref[chan, keys] = mm(qt_ref[chan, keys], slope)
                dvt_ref[chan, keys] = mm(gmt_ref[chan, keys], weight)
            mixed_ref[keys, lanes] = mixed
            dq_ref[keys, lanes] = grad_q
    pre = mm(arr_ref[...], wenc_ref[...])
    square, tangent = gelu_parts(pre)
    slope_ref[...] = 0.5 * (1.0 + tangent) + 0.5 * pre * (1.0 - tangent * tangent) * gelu_coef * (
        1.0 + 3.0 * 0.044715 * square
    )


def rim_body(
    nw_ref, ne_ref, wqkv_ref, q_ref, k_ref, v_ref, gm_ref, gw_ref, gwt_ref, ge_ref, get_ref,
    bw_ref, be_ref, pat_ref, mixed_ref, dq_ref, dkt_ref, dvt_ref, state_ref, cot_ref, inv_ref,
    oht_ref, slope_ref, wenc_ref,
    mout_ref, gback_ref, reply_ref,
    rim_q, rim_qt, rim_k, rim_v, gq, gkt, gvt,
):
    chans = q_ref.shape[1]
    for side, src in enumerate((nw_ref, ne_ref)):
        rows = slice(side * 2 * TILE, (side + 1) * 2 * TILE)
        normed = src[...]
        queries = mm(normed, wqkv_ref[:, 0:chans]).astype(bf16).astype(f32) * 0.0625
        rim_q[rows, :] = queries.astype(bf16)
        rim_qt[:, rows] = queries.T.astype(bf16)
        rim_k[rows, :] = mm(normed, wqkv_ref[:, chans : 2 * chans]).astype(bf16)
        rim_v[rows, :] = mm(normed, wqkv_ref[:, 2 * chans : 3 * chans]).astype(bf16)
    for i in range(2):
        for side, (gh_ref, ght_ref, bias_ref) in enumerate(
            ((gw_ref, gwt_ref, bw_ref), (ge_ref, get_ref, be_ref))
        ):
            own = rows_of(i, side)
            far = slice((side * 2 + i) * TILE, (side * 2 + i + 1) * TILE)
            near = slice(i * TILE, (i + 1) * TILE)
            out_bias = own_bias(pat_ref, i, side, 2 * side - 1)
            in_bias = bias_ref[near, :]
            for s in range(chans // SLAB):
                lanes = slice(s * SLAB, (s + 1) * SLAB)
                km = split_heads(rim_k[far, lanes])
                vm = split_heads(rim_v[far, lanes])
                kin = split_heads(k_ref[own, lanes])
                vin = split_heads(v_ref[own, lanes])
                mixed = mixed_ref[own, lanes]
                grad_q = dq_ref[own, lanes]
                for h in range(2):
                    weight, slope = weigh(q_ref[own, lanes], gm_ref[own, lanes], km[h], vm[h], out_bias)
                    mixed = mixed + mm(weight, vm[h])
                    grad_q = grad_q + mm(slope, km[h])
                    weight, slope = weigh(rim_q[far, lanes], gh_ref[near, lanes], kin[h], vin[h], in_bias)
                    chan = slice(s * SLAB + h * 64, s * SLAB + (h + 1) * 64)
                    gkt[chan, own] = (
                        (dkt_ref[chan, own] + mm(rim_qt[chan, far], slope)) * 0.5
                    ).astype(bf16)
                    gvt[chan, own] = (
                        (dvt_ref[chan, own] + mm(ght_ref[chan, near], weight)) * 0.5
                    ).astype(bf16)
                mout_ref[own, lanes] = (mixed * 0.5).astype(bf16)
                gq[own, lanes] = (grad_q * 0.03125).astype(bf16)
    grad_normed = (
        mm(gq[...], wqkv_ref[:, 0:chans], 1, 1)
        + mm(gkt[...], wqkv_ref[:, chans : 2 * chans], 0, 1)
        + mm(gvt[...], wqkv_ref[:, 2 * chans : 3 * chans], 0, 1)
    )
    scaled = []
    for i, u in halves():
        rows = rows_of(i, u)
        state = state_ref[rows, :].astype(f32)
        inv_rms = lax.rsqrt(jnp.mean(state * state, axis=1, keepdims=True) + norm_eps)
        normed = state * inv_rms
        grad = grad_normed[rows]
        grad_state = chunk(cot_ref, i, u).astype(f32) + inv_rms * (
            grad - normed * jnp.mean(grad * normed, axis=1, keepdims=True)
        )
        gback_ref[i * BLOCK : (i + 1) * BLOCK, u * HALF : (u + 1) * HALF, :] = grad_state.astype(
            bf16
        ).reshape(BLOCK, HALF, chans)
        scaled.append((grad_state * inv_ref[rows, 0:1]).astype(bf16))
    grad_enc = mm(oht_ref[...], jnp.concatenate(scaled, axis=0))
    grad_pre = (grad_enc * slope_ref[...]).astype(bf16)
    reply_ref[...] = mm(grad_pre, wenc_ref[...], 1, 1).astype(bf16)


def out_body(mixed_ref, wout_ref, state_ref, out_ref):
    chans = wout_ref.shape[0]
    for i, u in halves():
        rows = rows_of(i, u)
        total = state_ref[rows, :].astype(f32) + mm(mixed_ref[rows, :], wout_ref[...])
        out_ref[i * BLOCK : (i + 1) * BLOCK, u * HALF : (u + 1) * HALF, :] = total.astype(
            bf16
        ).reshape(BLOCK, HALF, chans)


def unpack_body(back_ref, slot_ref, out_ref):
    total = back_ref.shape[0]
    slots = slot_ref.shape[1]
    spread = one_hot(iota((total, slots), 0) == slot_ref[...])
    out_ref[...] = mm(spread, back_ref[...], 0, 0).astype(bf16)


def shards(
    background, obs_rows, obs_pixel, obs_count, block_pattern, w_enc, w_qkv, w_out, cotangent
):
    lat_rows, lon_cols, chans = background.shape
    pixels = lat_rows * lon_cols
    slots, feats = obs_rows.shape
    lon_devs = lax.axis_size("lon")
    devs = lax.axis_size("lat") * lon_devs
    cap = (slots + devs - 1) // devs + 2
    span = (cap + 1 + 7) // 8 * 8
    total = devs * span
    lon_bits = (lon_cols * lon_devs).bit_length() - 1
    side = pixels // 2
    up = [(i, (i + 1) % lon_devs) for i in range(lon_devs)]
    down = [(j, i) for i, j in up]

    payload, slot, cot_east, cot_west = call(
        functools.partial(pack_body, (devs, cap, span, lon_bits, lon_devs)),
        [
            ((total, feats), bf16),
            ((1, slots), i32),
            ((side + HALF, chans), bf16),
            ((side + HALF, chans), bf16),
        ],
        n_in=5,
        n_smem=(1, 2),
        flops=400 << 20,
    )(obs_pixel.reshape(1, slots), obs_count, block_pattern, obs_rows, cotangent)
    arrived = lax.all_to_all(
        payload.reshape(devs, span, feats), ("lat", "lon"), split_axis=0, concat_axis=0, tiled=True
    ).reshape(total, feats)
    west_cot = lax.ppermute(cot_east, "lon", up)
    east_cot = lax.ppermute(cot_west, "lon", down)
    gm, gmt, gw, gwt, ge, get, bias_w, bias_e = call(
        grad_body,
        [
            ((pixels, chans), bf16),
            ((chans, pixels), bf16),
            ((side, chans), bf16),
            ((chans, side), bf16),
            ((side, chans), bf16),
            ((chans, side), bf16),
            ((side, TILE), f32),
            ((side, TILE), f32),
        ],
        n_in=4,
        flops=1 << 30,
    )(cotangent, west_cot, east_cot, w_out)
    state, normed, n0, n1, inverse, oht = call(
        functools.partial(state_body, (devs, cap, span)),
        [
            ((pixels, chans), bf16),
            ((pixels, chans), bf16),
            ((side, chans), bf16),
            ((side, chans), bf16),
            ((pixels, 128), f32),
            ((total, pixels), bf16),
        ],
        n_in=3,
        flops=1 << 30,
    )(arrived, w_enc, background)
    n_west = lax.ppermute(n1, "lon", up)
    n_east = lax.ppermute(n0, "lon", down)
    q, qt, k, v, mixed, dq, dkt, dvt, slope = call(
        own_body,
        [
            ((pixels, chans), bf16),
            ((chans, pixels), bf16),
            ((pixels, chans), bf16),
            ((pixels, chans), bf16),
            ((pixels, chans), f32),
            ((pixels, chans), f32),
            ((chans, pixels), f32),
            ((chans, pixels), f32),
            ((total, chans), f32),
        ],
        n_in=7,
        n_smem=(4,),
        flops=4 << 30,
    )(normed, w_qkv, gm, gmt, block_pattern, arrived, w_enc)
    mixed, grad_background, reply = call(
        rim_body,
        [
            ((pixels, chans), bf16),
            ((lat_rows, lon_cols, chans), bf16),
            ((total, feats), bf16),
        ],
        scratch=[
            pltpu.VMEM((pixels, chans), bf16),
            pltpu.VMEM((chans, pixels), bf16),
            pltpu.VMEM((pixels, chans), bf16),
            pltpu.VMEM((pixels, chans), bf16),
            pltpu.VMEM((pixels, chans), bf16),
            pltpu.VMEM((chans, pixels), bf16),
            pltpu.VMEM((chans, pixels), bf16),
        ],
        n_in=24,
        n_smem=(13,),
        flops=4 << 30,
    )(
        n_west, n_east, w_qkv, q, k, v, gm, gw, gwt, ge, get, bias_w, bias_e, block_pattern,
        mixed, dq, dkt, dvt, state, cotangent, inverse, oht, slope, w_enc,
    )
    returned = lax.all_to_all(
        reply.reshape(devs, span, feats), ("lat", "lon"), split_axis=0, concat_axis=0, tiled=True
    ).reshape(total, feats)
    (updated,) = call(out_body, [((lat_rows, lon_cols, chans), bf16)], n_in=3, flops=1 << 30)(
        mixed, w_out, state
    )
    (grad_obs,) = call(unpack_body, [((slots, feats), bf16)], n_in=2, flops=1 << 28)(returned, slot)
    return (updated, grad_background, grad_obs)


def solution(mesh):
    return jax.shard_map(
        shards,
        mesh=mesh,
        in_specs=(
            P("lat", "lon", None),
            P(("lat", "lon"), None),
            P(("lat", "lon")),
            P(("lat", "lon")),
            P("lat", "lon", None),
            P(),
            P(),
            P(),
            P("lat", "lon", None),
        ),
        out_specs=(P("lat", "lon", None), P("lat", "lon", None), P(("lat", "lon"), None)),
        check_vma=False,
    )
```

```python
import functools
import math

import jax
import jax.numpy as jnp
from jax import lax
from jax.experimental import pallas as pl
from jax.experimental.pallas import tpu as pltpu
from jax.sharding import PartitionSpec as P

HEADS = 8
BLOCK = 8
HALF = 2 * BLOCK
TILE = BLOCK * HALF
SLAB = 128
MASKED = -1e30
GRAD_COST = 1 << 37

norm_eps = 1e-06
gelu_coef = 0.7978845608028654

bf16 = jnp.bfloat16
f32 = jnp.float32
i32 = jnp.int32


def iota(shape, dim):
    return lax.broadcasted_iota(i32, shape, dim)


def mm(lhs, rhs, lhs_dim=1, rhs_dim=0):
    return lax.dot_general(
        lhs, rhs, (((lhs_dim,), (rhs_dim,)), ((), ())), preferred_element_type=f32
    )


def one_hot(cond):
    return jnp.where(cond, 1.0, 0.0).astype(bf16)


def gelu_parts(inputs):
    square = inputs * inputs
    tangent = jnp.tanh(gelu_coef * inputs * (1.0 + 0.044715 * square))
    return square, tangent


def call(
    body, outs, scratch=(), flops=0, n_smem=(), n_hbm=(), out_hbm=(), n_in=0, size=1 << 20, vmem=16
):
    def spec(k, smem, hbm):
        if k in hbm:
            return pl.BlockSpec(memory_space=pltpu.HBM)
        return pl.BlockSpec(memory_space=pltpu.SMEM if k in smem else pltpu.VMEM)

    kernel = pl.pallas_call(
        body,
        out_shape=[
            pltpu.HBM(s, d) if k in out_hbm else jax.ShapeDtypeStruct(s, d)
            for k, (s, d) in enumerate(outs)
        ],
        in_specs=[spec(k, n_smem, n_hbm) for k in range(n_in)],
        out_specs=[spec(k, (), out_hbm) for k in range(len(outs))],
        scratch_shapes=list(scratch),
        compiler_params=pltpu.CompilerParams(vmem_limit_bytes=vmem << 20),
        cost_estimate=pl.CostEstimate(flops=flops, bytes_accessed=size, transcendentals=0),
    )

    def run(*args):
        return kernel(
            *[
                pltpu.with_memory_space_constraint(x, pltpu.HBM) if k in n_hbm else x
                for k, x in enumerate(args)
            ]
        )

    return run


def chunk(ref, row_block, half):
    part = ref[
        row_block * BLOCK : (row_block + 1) * BLOCK, half * HALF : (half + 1) * HALF, :
    ]
    return part.reshape(TILE, part.shape[-1])


def halves():
    return [(i, u) for i in range(2) for u in range(2)]


def rows_of(i, u):
    return slice((i * 2 + u) * TILE, (i * 2 + u + 1) * TILE)


def key_count(pat, i, b):
    return 1 + pat[i, b, 0] + pat[i, b, 1] + pat[i, b, 2] + pat[i, b, 3]


def mask_value(pat, i, b, shift):
    if abs(shift) > 2:
        return jnp.int32(0)
    if shift == 0:
        return jnp.int32(1)
    return pat[i, b, shift + 2 if shift < 0 else shift + 1]


def half_bias(count):
    bias = jnp.float32(-0.5 * math.log(64.0))
    for n in range(2, 6):
        bias = jnp.where(count == n, jnp.float32(-0.5 * math.log(64.0 * n)), bias)
    return bias


def own_bias(pat, i, u, turn):
    second_q = iota((TILE, TILE), 0) % HALF >= BLOCK
    second_k = iota((TILE, TILE), 1) % HALF >= BLOCK
    parts = []
    for qb in range(2):
        bias = half_bias(key_count(pat, i, 2 * u + qb))
        pair = [
            jnp.where(mask_value(pat, i, 2 * u + qb, 2 * turn + kb - qb) > 0, bias, MASKED)
            for kb in range(2)
        ]
        parts.append(jnp.where(second_k, pair[1], pair[0]))
    return jnp.where(second_q, parts[1], parts[0])


def start_copy(src, dst, sem):
    copy = pltpu.make_async_copy(src, dst, sem)
    copy.start()
    return copy


def halo_rows(pat_ref, u, turn, width):
    lane = iota((HALF, width), 1)
    line = iota((HALF, width), 0)
    second_k = lane % HALF >= BLOCK
    extra = jnp.zeros((HALF, width), f32)
    for i in range(2):
        for qb in range(2):
            pair = [
                mask_value(pat_ref, i, 2 * u + qb, 2 * turn + kb - qb).astype(f32)
                for kb in range(2)
            ]
            mask = jnp.where(second_k, pair[1], pair[0])
            count = key_count(pat_ref, i, 2 * u + qb).astype(f32)
            here = (line == i) & (lane >= qb * TILE) & (lane < (qb + 1) * TILE)
            there = (line == i) & (lane >= (qb + 2) * TILE) & (lane < (qb + 3) * TILE)
            extra = jnp.where(here, mask, jnp.where(there, count, extra))
    return extra.astype(bf16)


class Geometry:
    def __init__(self, slots, devs, lon_devs, lon_cols):
        self.devs, self.lon_devs = devs, lon_devs
        self.cap = (slots + devs - 1) // devs + 2
        self.full = self.cap // 8 * 8
        self.rest = self.cap - self.full
        self.shift = 4 if self.rest <= 3 else 8
        self.tail = 2 * self.shift
        self.mark = self.shift - 1
        self.rows = 2 * self.full + self.tail
        self.bulk = devs * self.full
        self.total = self.bulk + devs * self.tail
        self.lon_bits = (lon_cols * lon_devs).bit_length() - 1


def join_slots(geo, ref, feats):
    half = feats // 2
    tail = ref[:, 2 * geo.full : geo.rows, :].reshape(geo.devs * geo.tail, half)
    wide = tail.astype(f32)
    moved = pltpu.roll(wide, wide.shape[0] - geo.shift, 0)
    tail_rows = jnp.concatenate([wide, moved], axis=1).astype(bf16)
    if not geo.full:
        return tail, tail_rows
    first = ref[:, 0 : geo.full, :].reshape(geo.bulk, half)
    second = ref[:, geo.full : 2 * geo.full, :].reshape(geo.bulk, half)
    return tail, jnp.concatenate([jnp.concatenate([first, second], axis=1), tail_rows], axis=0)


def store_bulk(geo, ref, values):
    half = values.shape[1] // 2
    if geo.full:
        ref[:, 0 : geo.full, :] = values[:, 0:half].reshape(geo.devs, geo.full, half)
        ref[:, geo.full : 2 * geo.full, :] = values[:, half:].reshape(geo.devs, geo.full, half)


def slot_index(geo, owner, rank, live):
    place = jnp.where(
        rank < geo.full,
        owner * geo.full + rank,
        geo.bulk + owner * geo.tail + rank - geo.full,
    )
    return jnp.where(live, place, -1)


def pack_body(
    geo, pix_hbm, cnt_ref, rows_hbm, pat_hbm, cot_hbm,
    pay_hbm, slot_ref, east_hbm, west_hbm,
    pix_ref, rows_ref, pat_ref, pay_ref, east_ref, west_ref, sems,
):
    pix_copy = start_copy(pix_hbm, pix_ref, sems.at[0])
    rows_copy = start_copy(rows_hbm, rows_ref, sems.at[1])
    pat_copy = start_copy(pat_hbm, pat_ref, sems.at[2])
    lats = cot_hbm.shape[0]
    sides = ((east_ref, 1, 1), (west_ref, 0, -1))
    cot_copies = [
        start_copy(cot_hbm.at[:, u * HALF : (u + 1) * HALF, :], ref.at[0:lats], sems.at[3 + u])
        for ref, u, _ in sides
    ]
    slots = pix_ref.shape[1]
    upper = one_hot(iota((slots, slots), 0) <= iota((slots, slots), 1))
    pix_copy.wait()
    pix = pix_ref[...]
    lat = lax.shift_right_logical(pix, geo.lon_bits)
    lon = lax.bitwise_and(pix, (1 << geo.lon_bits) - 1)
    owner = lax.shift_right_logical(lat, 4) * geo.lon_devs + lax.shift_right_logical(lon, 5)
    row = lax.bitwise_and(lat, 15)
    col = lax.bitwise_and(lon, 31)
    code = (
        lax.shift_right_logical(row, 3) * (2 * TILE)
        + lax.shift_right_logical(col, 4) * TILE
        + lax.bitwise_and(row, 7) * HALF
        + lax.bitwise_and(col, 15)
        + 1
    )
    live = iota((1, slots), 1) < cnt_ref[0]
    table = (iota((geo.devs, slots), 0) == owner) & live
    table_f = jnp.where(table, 1.0, 0.0)
    table_b = table_f.astype(bf16)
    running = mm(table_b, upper)
    rank = (jnp.sum(running * table_f, axis=0, keepdims=True) - 1.0).astype(i32)
    slot = slot_index(geo, owner, rank, live)
    slot_ref[...] = slot
    high = lax.shift_right_logical(code, 5).astype(f32)
    low = lax.bitwise_and(code, 31).astype(f32)
    place = iota((128, slots), 0)
    codes = jnp.where(place == rank, high, 0.0) + jnp.where(place == rank + 64, low, 0.0)
    meta = mm(table_b, codes.astype(bf16), 1, 1)
    tails = geo.devs * geo.tail
    lift = one_hot(
        iota((tails, geo.devs), 0) == iota((tails, geo.devs), 1) * geo.tail + geo.mark
    )
    lifted = mm(lift, meta.astype(bf16))
    pat_copy.wait()
    for copy, (ref, u, turn) in zip(cot_copies, sides):
        ref[lats] = halo_rows(pat_ref, u, turn, cot_hbm.shape[2])
        copy.wait()
    outs = [
        start_copy(east_ref, east_hbm, sems.at[5]),
        start_copy(west_ref, west_hbm, sems.at[6]),
    ]
    place = iota((tails, slots), 0)
    first = one_hot(place == slot - geo.bulk)
    second = one_hot((place == slot - geo.bulk + geo.shift) & (slot >= geo.bulk))
    rows_copy.wait()
    half = rows_ref.shape[1] // 2
    if geo.full:
        spread = one_hot(iota((geo.bulk, slots), 0) == slot)
        store_bulk(geo, pay_ref, mm(spread, rows_ref[...]).astype(bf16))
    tail = mm(first, rows_ref[:, 0:half]) + mm(second, rows_ref[:, half:]) + lifted
    pay_ref[:, 2 * geo.full : geo.rows, :] = tail.astype(bf16).reshape(geo.devs, geo.tail, half)
    outs.append(start_copy(pay_ref, pay_hbm, sems.at[7]))
    for copy in outs:
        copy.wait()


def grad_body(
    cot_hbm, west_ref, east_ref, wout_hbm,
    gm_hbm, gmt_hbm, gw_hbm, gwt_hbm, ge_hbm, get_hbm, bw_hbm, be_hbm,
    cot_ref, wout_ref,
    gm_ref, gmt_ref, gw_ref, gwt_ref, ge_ref, get_ref, bw_ref, be_ref, in_sems, out_sems,
):
    wout_copy = start_copy(wout_hbm, wout_ref, in_sems.at[0])
    cot_copy = start_copy(cot_hbm, cot_ref, in_sems.at[1])
    wout_copy.wait()
    cot_copy.wait()
    wout = wout_ref[...]
    for i, u in halves():
        part = mm(chunk(cot_ref, i, u), wout, 1, 1)
        gm_ref[rows_of(i, u), :] = part.astype(bf16)
        gmt_ref[:, rows_of(i, u)] = part.T.astype(bf16)
    outs = [
        start_copy(gm_ref, gm_hbm, out_sems.at[0]),
        start_copy(gmt_ref, gmt_hbm, out_sems.at[1]),
    ]
    second_q = iota((TILE, TILE), 0) % HALF >= BLOCK
    for n, (src, dst, dst_t, bias_ref, dst_hbm, dst_t_hbm, bias_hbm) in enumerate(
        (
            (west_ref, gw_ref, gwt_ref, bw_ref, gw_hbm, gwt_hbm, bw_hbm),
            (east_ref, ge_ref, get_ref, be_ref, ge_hbm, get_hbm, be_hbm),
        )
    ):
        rows = src.shape[0] - 1
        part = mm(src[0:rows].reshape(2 * TILE, wout.shape[0]), wout, 1, 1)
        dst[...] = part.astype(bf16)
        dst_t[...] = part.T.astype(bf16)
        extra = src[rows].astype(f32)
        for i in range(2):
            line = extra[i : i + 1, :]
            mask = jnp.where(second_q, line[:, TILE : 2 * TILE], line[:, 0:TILE])
            count = jnp.where(second_q, line[:, 3 * TILE : 4 * TILE], line[:, 2 * TILE : 3 * TILE])
            bias = -0.5 * jnp.log(count * 64.0)
            bias_ref[i * TILE : (i + 1) * TILE, :] = jnp.where(mask > 0.5, bias, MASKED)
        outs += [
            start_copy(dst, dst_hbm, out_sems.at[2 + 3 * n]),
            start_copy(dst_t, dst_t_hbm, out_sems.at[3 + 3 * n]),
            start_copy(bias_ref, bias_hbm, out_sems.at[4 + 3 * n]),
        ]
    for copy in outs:
        copy.wait()


def state_body(geo, arr_ref, wenc_ref, bg_ref, state_ref, n_ref, n0_ref, n1_ref, inv_ref, oht_ref):
    devs, feats = geo.devs, wenc_ref.shape[0]
    tails, arr = join_slots(geo, arr_ref, feats)
    pick = one_hot(
        iota((devs, devs * geo.tail), 1) == iota((devs, devs * geo.tail), 0) * geo.tail + geo.mark
    )
    meta = mm(pick, tails).astype(bf16)
    codes = []
    for base, count in ((0, geo.full), (geo.full, geo.tail)):
        if count:
            owner = one_hot(
                iota((devs, count, devs), 0) == iota((devs, count, devs), 2)
            ).reshape(devs * count, devs)
            wide = mm(owner, meta)
            place = iota((devs, count, 128), 1).reshape(devs * count, 128) + base
            lane = iota((devs * count, 128), 1)
            scale = jnp.where(lane == place, 32.0, 0.0) + jnp.where(lane == place + 64, 1.0, 0.0)
            codes.append(jnp.sum(wide * scale, axis=1, keepdims=True))
    code = jnp.concatenate(codes, axis=0).astype(i32)
    pixels = n_ref.shape[0]
    oht = one_hot(code == iota((geo.total, pixels), 1) + 1)
    oht_ref[...] = oht
    pre = mm(arr, wenc_ref[...])
    _, tangent = gelu_parts(pre)
    encoded = (0.5 * pre * (1.0 + tangent)).astype(bf16)
    obs_sum = mm(oht, encoded, 0, 0)
    number = mm(oht, jnp.ones((geo.total, 128), bf16), 0, 0)
    inverse = 1.0 / (1.0 + number)
    inv_ref[...] = inverse
    for i, u in halves():
        rows = rows_of(i, u)
        fresh = obs_sum[rows] * inverse[rows, 0:1]
        state = (chunk(bg_ref, i, u).astype(f32) + fresh).astype(bf16)
        state_ref[rows, :] = state
        wide_state = state.astype(f32)
        inv_rms = lax.rsqrt(jnp.mean(wide_state * wide_state, axis=1, keepdims=True) + norm_eps)
        normed = (wide_state * inv_rms).astype(bf16)
        n_ref[rows, :] = normed
        side = n1_ref if u else n0_ref
        side[i * TILE : (i + 1) * TILE, :] = normed


def head_lanes(shape, head, dim=1):
    return lax.shift_right_logical(iota(shape, dim), 6) == head


def split_heads(slab):
    return [jnp.where(head_lanes(slab.shape, h), slab, jnp.zeros((), slab.dtype)) for h in range(2)]


def weigh(q2, g2, km, vm, bias):
    tangent = jnp.tanh(mm(q2, km, 1, 1) + bias)
    weight = tangent + 1.0
    slope = mm(g2, vm, 1, 1) * weight * (2.0 - weight)
    return weight.astype(bf16), slope.astype(bf16)


def stack_heads(slab):
    return jnp.concatenate(split_heads(slab), axis=0)


def project(src, wqkv_ref, q_ref, qt_ref, k_ref, v_ref, rows):
    chans = src.shape[1]
    queries = mm(src, wqkv_ref[:, 0:chans]).astype(bf16).astype(f32) * 0.0625
    q_ref[rows, :] = queries.astype(bf16)
    qt_ref[:, rows] = queries.T.astype(bf16)
    k_ref[rows, :] = mm(src, wqkv_ref[:, chans : 2 * chans]).astype(bf16)
    v_ref[rows, :] = mm(src, wqkv_ref[:, 2 * chans : 3 * chans]).astype(bf16)


def own_body(
    geo, n_ref, wqkv_ref, gm_ref, gmt_ref, pat_hbm, arr_ref, wenc_ref, state_ref,
    q_ref, k_ref, v_ref, dq_ref, dkt_ref, dvt_ref, slope_ref, weight_hbm, v_hbm, state_hbm,
    pat_ref, qt_ref, weight_ref, sems,
):
    chans = n_ref.shape[1]
    pat_copy = start_copy(pat_hbm, pat_ref, sems.at[0])
    state_copy = start_copy(state_ref, state_hbm, sems.at[1])
    project(n_ref[...], wqkv_ref, q_ref, qt_ref, k_ref, v_ref, slice(0, n_ref.shape[0]))
    v_copy = start_copy(v_ref, v_hbm, sems.at[2])
    pat_copy.wait()
    for i in range(2):
        keys = slice(i * 2 * TILE, (i + 1) * 2 * TILE)
        bias = [
            jnp.concatenate([own_bias(pat_ref, i, u, -u), own_bias(pat_ref, i, u, 1 - u)], axis=1)
            for u in range(2)
        ]
        bias = jnp.concatenate(bias, axis=0)
        for s in range(chans // SLAB):
            lanes = slice(s * SLAB, (s + 1) * SLAB)
            km = split_heads(k_ref[keys, lanes])
            vm = split_heads(v_ref[keys, lanes])
            grad_q = jnp.zeros((2 * TILE, SLAB), f32)
            for h in range(2):
                weight, slope = weigh(q_ref[keys, lanes], gm_ref[keys, lanes], km[h], vm[h], bias)
                weight_ref[i, 2 * s + h] = weight
                grad_q = grad_q + mm(slope, km[h])
                chan = slice(s * SLAB + h * 64, s * SLAB + (h + 1) * 64)
                dkt_ref[chan, keys] = mm(qt_ref[chan, keys], slope)
                dvt_ref[chan, keys] = mm(gmt_ref[chan, keys], weight)
            dq_ref[keys, lanes] = grad_q
    weight_copy = start_copy(weight_ref, weight_hbm, sems.at[3])
    pre = mm(join_slots(geo, arr_ref, wenc_ref.shape[0])[1], wenc_ref[...])
    square, tangent = gelu_parts(pre)
    slope_ref[...] = 0.5 * (1.0 + tangent) + 0.5 * pre * (1.0 - tangent * tangent) * gelu_coef * (
        1.0 + 3.0 * 0.044715 * square
    )
    for copy in (state_copy, v_copy, weight_copy):
        copy.wait()


def rim_body(
    geo, nw_ref, ne_ref, wqkv_ref, q_ref, k_ref, v_ref, gm_ref, gw_ref, gwt_ref, ge_ref, get_ref,
    bw_ref, be_ref, pat_hbm, dq_ref, dkt_ref, dvt_ref, state_ref, cot_ref, inv_ref,
    oht_ref, slope_ref, wenc_ref,
    v_hbm, weight_hbm, gback_hbm, reply_ref,
    pat_ref, rim_q, rim_qt, rim_k, rim_v, weight_ref, gback_ref, gq, gkt, gvt, sems,
):
    chans = q_ref.shape[1]
    pat_copy = start_copy(pat_hbm, pat_ref, sems.at[0])
    for side, src in enumerate((nw_ref, ne_ref)):
        rows = slice(side * 2 * TILE, (side + 1) * 2 * TILE)
        project(src[...], wqkv_ref, rim_q, rim_qt, rim_k, rim_v, rows)
    v_copy = start_copy(rim_v, v_hbm, sems.at[1])
    pat_copy.wait()
    for i in range(2):
        for side, (gh_ref, ght_ref, bias_ref) in enumerate(
            ((gw_ref, gwt_ref, bw_ref), (ge_ref, get_ref, be_ref))
        ):
            own = rows_of(i, side)
            far = slice((side * 2 + i) * TILE, (side * 2 + i + 1) * TILE)
            near = slice(i * TILE, (i + 1) * TILE)
            out_bias = own_bias(pat_ref, i, side, 2 * side - 1)
            out_bias = jnp.concatenate([out_bias, out_bias], axis=1)
            in_bias = bias_ref[near, :]
            in_bias = jnp.concatenate([in_bias, in_bias], axis=1)
            for s in range(chans // SLAB):
                lanes = slice(s * SLAB, (s + 1) * SLAB)
                km = stack_heads(rim_k[far, lanes])
                vm = stack_heads(rim_v[far, lanes])
                weight, slope = weigh(q_ref[own, lanes], gm_ref[own, lanes], km, vm, out_bias)
                weight_ref[i * 2 + side, s] = weight
                gq[own, lanes] = ((dq_ref[own, lanes] + mm(slope, km)) * 0.03125).astype(bf16)
                km = stack_heads(k_ref[own, lanes])
                vm = stack_heads(v_ref[own, lanes])
                weight, slope = weigh(rim_q[far, lanes], gh_ref[near, lanes], km, vm, in_bias)
                grad_k = mm(rim_qt[lanes, far], slope)
                grad_v = mm(ght_ref[lanes, near], weight)
                for h in range(2):
                    part = slice(h * 64, (h + 1) * 64)
                    cols = slice(h * TILE, (h + 1) * TILE)
                    chan = slice(s * SLAB + h * 64, s * SLAB + (h + 1) * 64)
                    gkt[chan, own] = ((dkt_ref[chan, own] + grad_k[part, cols]) * 0.5).astype(bf16)
                    gvt[chan, own] = ((dvt_ref[chan, own] + grad_v[part, cols]) * 0.5).astype(bf16)
    weight_copy = start_copy(weight_ref, weight_hbm, sems.at[2])
    grad_normed = (
        mm(gq[...], wqkv_ref[:, 0:chans], 1, 1)
        + mm(gkt[...], wqkv_ref[:, chans : 2 * chans], 0, 1)
        + mm(gvt[...], wqkv_ref[:, 2 * chans : 3 * chans], 0, 1)
    )
    scaled = []
    for i, u in halves():
        rows = rows_of(i, u)
        state = state_ref[rows, :].astype(f32)
        inv_rms = lax.rsqrt(jnp.mean(state * state, axis=1, keepdims=True) + norm_eps)
        normed = state * inv_rms
        grad = grad_normed[rows]
        grad_state = chunk(cot_ref, i, u).astype(f32) + inv_rms * (
            grad - normed * jnp.mean(grad * normed, axis=1, keepdims=True)
        )
        gback_ref[rows, :] = grad_state.astype(bf16)
        scaled.append((grad_state * inv_ref[rows, 0:1]).astype(bf16))
    gback_copy = start_copy(gback_ref, gback_hbm, sems.at[3])
    grad_enc = mm(oht_ref[...], jnp.concatenate(scaled, axis=0))
    grad_pre = (grad_enc * slope_ref[...]).astype(bf16)
    reply = mm(grad_pre, wenc_ref[...], 1, 1)
    store_bulk(geo, reply_ref, reply[0 : geo.bulk].astype(bf16))
    tail = reply[geo.bulk :]
    half = tail.shape[1] // 2
    moved = pltpu.roll(tail[:, half:], geo.shift, 0)
    lower = iota((geo.devs * geo.tail, half), 0) % geo.tail < geo.shift
    tail = jnp.where(lower, tail[:, 0:half], moved)
    reply_ref[:, 2 * geo.full : geo.rows, :] = tail.astype(bf16).reshape(geo.devs, geo.tail, half)
    for copy in (v_copy, weight_copy, gback_copy):
        copy.wait()


def out_body(*refs):
    hbm, (out_ref, back_ref), local, (mixed_ref, sems) = refs[:7], refs[7:9], refs[9:16], refs[16:]
    copies = [start_copy(src, dst, sems.at[n]) for n, (src, dst) in enumerate(zip(hbm, local))]
    for copy in copies:
        copy.wait()
    weight_ref, far_ref, v_ref, rim_v, wout_ref, state_ref, gback_ref = local
    chans = wout_ref.shape[0]
    for i in range(2):
        keys = slice(i * 2 * TILE, (i + 1) * 2 * TILE)
        for s in range(chans // SLAB):
            lanes = slice(s * SLAB, (s + 1) * SLAB)
            vm = split_heads(v_ref[keys, lanes])
            mixed = mm(weight_ref[i, 2 * s], vm[0]) + mm(weight_ref[i, 2 * s + 1], vm[1])
            for side in range(2):
                far = slice((side * 2 + i) * TILE, (side * 2 + i + 1) * TILE)
                total = mixed[side * TILE : (side + 1) * TILE] + mm(
                    far_ref[i * 2 + side, s], stack_heads(rim_v[far, lanes])
                )
                mixed_ref[rows_of(i, side), lanes] = (total * 0.5).astype(bf16)
    for i, u in halves():
        rows = rows_of(i, u)
        place = (slice(i * BLOCK, (i + 1) * BLOCK), slice(u * HALF, (u + 1) * HALF))
        total = state_ref[rows, :].astype(f32) + mm(mixed_ref[rows, :], wout_ref[...])
        out_ref[place[0], place[1], :] = total.astype(bf16).reshape(BLOCK, HALF, chans)
        back_ref[place[0], place[1], :] = gback_ref[rows, :].reshape(BLOCK, HALF, chans)


def unpack_body(geo, back_ref, slot_ref, out_ref):
    feats = out_ref.shape[1]
    slots = slot_ref.shape[1]
    spread = one_hot(iota((geo.total, slots), 0) == slot_ref[...])
    out_ref[...] = mm(spread, join_slots(geo, back_ref, feats)[1], 0, 0).astype(bf16)


def shards(
    background, obs_rows, obs_pixel, obs_count, block_pattern, w_enc, w_qkv, w_out, cotangent
):
    lat_rows, lon_cols, chans = background.shape
    pixels = lat_rows * lon_cols
    slots, feats = obs_rows.shape
    lon_devs = lax.axis_size("lon")
    geo = Geometry(slots, lax.axis_size("lat") * lon_devs, lon_devs, lon_cols)
    side = pixels // 2
    half = feats // 2
    up = [(i, (i + 1) % lon_devs) for i in range(lon_devs)]
    down = [(j, i) for i, j in up]

    rim = (lat_rows + 1, HALF, chans)
    wide, tall, edge, edge_t = (pixels, chans), (chans, pixels), (side, chans), (chans, side)
    weights_own = (2, HEADS, 2 * TILE, 2 * TILE)
    weights_far = (4, chans // SLAB, TILE, 2 * TILE)
    dma = pltpu.SemaphoreType.DMA
    pattern = pltpu.SMEM(block_pattern.shape, i32)

    def vmem(*shapes):
        return [pltpu.VMEM(shape, bf16) for shape in shapes]

    payload, slot, cot_east, cot_west = call(
        functools.partial(pack_body, geo),
        [((geo.devs, geo.rows, half), bf16), ((1, slots), i32), (rim, bf16), (rim, bf16)],
        scratch=[pltpu.VMEM((1, slots), i32), pltpu.VMEM((slots, feats), bf16), pattern]
        + vmem((geo.devs, geo.rows, half), rim, rim)
        + [dma((8,))],
        n_in=5,
        n_smem=(1,),
        n_hbm=(0, 2, 3, 4),
        out_hbm=(0, 2, 3),
        flops=400 << 20,
    )(obs_pixel.reshape(1, slots), obs_count, obs_rows, block_pattern, cotangent)
    west_cot = lax.ppermute(cot_east, "lon", up)
    east_cot = lax.ppermute(cot_west, "lon", down)
    arrived = lax.all_to_all(payload, ("lat", "lon"), split_axis=0, concat_axis=0, tiled=True)
    gm, gmt, gw, gwt, ge, get, bias_w, bias_e = call(
        grad_body,
        [
            (wide, bf16),
            (tall, bf16),
            (edge, bf16),
            (edge_t, bf16),
            (edge, bf16),
            (edge_t, bf16),
            ((side, TILE), f32),
            ((side, TILE), f32),
        ],
        scratch=vmem((lat_rows, lon_cols, chans), (chans, chans))
        + vmem(wide, tall, edge, edge_t, edge, edge_t)
        + [pltpu.VMEM((side, TILE), f32)] * 2
        + [dma((2,)), dma((8,))],
        n_in=4,
        n_hbm=(0, 3),
        out_hbm=range(8),
        flops=GRAD_COST,
    )(cotangent, west_cot, east_cot, w_out)
    state, normed, n0, n1, inverse, oht = call(
        functools.partial(state_body, geo),
        [
            (wide, bf16),
            (wide, bf16),
            (edge, bf16),
            (edge, bf16),
            ((pixels, 128), f32),
            ((geo.total, pixels), bf16),
        ],
        n_in=3,
        flops=1 << 30,
    )(arrived, w_enc, background)
    n_west = lax.ppermute(n1, "lon", up)
    n_east = lax.ppermute(n0, "lon", down)
    q, k, v, dq, dkt, dvt, slope, weight, v_far, state_far = call(
        functools.partial(own_body, geo),
        [
            (wide, bf16),
            (wide, bf16),
            (wide, bf16),
            (wide, f32),
            (tall, f32),
            (tall, f32),
            ((geo.total, chans), f32),
            (weights_own, bf16),
            (wide, bf16),
            (wide, bf16),
        ],
        scratch=[pattern] + vmem(tall, weights_own) + [dma((4,))],
        n_in=8,
        n_hbm=(4,),
        out_hbm=(7, 8, 9),
        flops=4 << 30,
    )(normed, w_qkv, gm, gmt, block_pattern, arrived, w_enc, state)
    rim_v, far, gback, reply = call(
        functools.partial(rim_body, geo),
        [
            (wide, bf16),
            (weights_far, bf16),
            (wide, bf16),
            ((geo.devs, geo.rows, half), bf16),
        ],
        scratch=[pattern] + vmem(wide, tall, wide, wide, weights_far, wide, wide, tall, tall) + [dma((4,))],
        n_in=23,
        n_hbm=(13,),
        out_hbm=(0, 1, 2),
        flops=4 << 30,
    )(
        n_west, n_east, w_qkv, q, k, v, gm, gw, gwt, ge, get, bias_w, bias_e, block_pattern,
        dq, dkt, dvt, state, cotangent, inverse, oht, slope, w_enc,
    )
    returned = lax.all_to_all(reply, ("lat", "lon"), split_axis=0, concat_axis=0, tiled=True)
    updated, grad_background = call(
        out_body,
        [((lat_rows, lon_cols, chans), bf16), ((lat_rows, lon_cols, chans), bf16)],
        scratch=vmem(weights_own, weights_far, wide, wide, (chans, chans), wide, wide, wide)
        + [dma((7,))],
        n_in=7,
        n_hbm=range(7),
        flops=1 << 30,
    )(weight, far, v_far, rim_v, w_out, state_far, gback)
    (grad_obs,) = call(
        functools.partial(unpack_body, geo), [((slots, feats), bf16)], n_in=2, flops=1 << 28
    )(returned, slot)
    return (updated, grad_background, grad_obs)


def solution(mesh):
    return jax.shard_map(
        shards,
        mesh=mesh,
        in_specs=(
            P("lat", "lon", None),
            P(("lat", "lon"), None),
            P(("lat", "lon")),
            P(("lat", "lon")),
            P("lat", "lon", None),
            P(),
            P(),
            P(),
            P("lat", "lon", None),
        ),
        out_specs=(P("lat", "lon", None), P("lat", "lon", None), P(("lat", "lon"), None)),
        check_vma=False,
    )
```

```python
import functools
import math

import jax
import jax.numpy as jnp
from jax import lax
from jax.experimental import pallas as pl
from jax.experimental.pallas import tpu as pltpu
from jax.sharding import PartitionSpec as P

HEADS = 8
BLOCK = 8
HALF = 2 * BLOCK
TILE = BLOCK * HALF
SLAB = 128
MASKED = -1e30
GRAD_COST = 1 << 37

norm_eps = 1e-06
gelu_coef = 0.7978845608028654

bf16 = jnp.bfloat16
f32 = jnp.float32
i32 = jnp.int32


def iota(shape, dim):
    return lax.broadcasted_iota(i32, shape, dim)


def mm(lhs, rhs, lhs_dim=1, rhs_dim=0):
    return lax.dot_general(
        lhs, rhs, (((lhs_dim,), (rhs_dim,)), ((), ())), preferred_element_type=f32
    )


def one_hot(cond):
    return jnp.where(cond, 1.0, 0.0).astype(bf16)


def gelu_parts(inputs):
    square = inputs * inputs
    tangent = jnp.tanh(gelu_coef * inputs * (1.0 + 0.044715 * square))
    return square, tangent


def call(
    body, outs, scratch=(), flops=0, n_smem=(), n_hbm=(), out_hbm=(), n_in=0, size=1 << 20, vmem=16
):
    def spec(k, smem, hbm):
        if k in hbm:
            return pl.BlockSpec(memory_space=pltpu.HBM)
        return pl.BlockSpec(memory_space=pltpu.SMEM if k in smem else pltpu.VMEM)

    kernel = pl.pallas_call(
        body,
        out_shape=[
            pltpu.HBM(s, d) if k in out_hbm else jax.ShapeDtypeStruct(s, d)
            for k, (s, d) in enumerate(outs)
        ],
        in_specs=[spec(k, n_smem, n_hbm) for k in range(n_in)],
        out_specs=[spec(k, (), out_hbm) for k in range(len(outs))],
        scratch_shapes=list(scratch),
        compiler_params=pltpu.CompilerParams(vmem_limit_bytes=vmem << 20),
        cost_estimate=pl.CostEstimate(flops=flops, bytes_accessed=size, transcendentals=0),
    )

    def run(*args):
        return kernel(
            *[
                pltpu.with_memory_space_constraint(x, pltpu.HBM) if k in n_hbm else x
                for k, x in enumerate(args)
            ]
        )

    return run


def chunk(ref, row_block, half):
    part = ref[
        row_block * BLOCK : (row_block + 1) * BLOCK, half * HALF : (half + 1) * HALF, :
    ]
    return part.reshape(TILE, part.shape[-1])


def halves():
    return [(i, u) for i in range(2) for u in range(2)]


def rows_of(i, u):
    return slice((i * 2 + u) * TILE, (i * 2 + u + 1) * TILE)


def key_count(pat, i, b):
    return 1 + pat[i, b, 0] + pat[i, b, 1] + pat[i, b, 2] + pat[i, b, 3]


def mask_value(pat, i, b, shift):
    if abs(shift) > 2:
        return jnp.int32(0)
    if shift == 0:
        return jnp.int32(1)
    return pat[i, b, shift + 2 if shift < 0 else shift + 1]


def half_bias(count):
    bias = jnp.float32(-0.5 * math.log(64.0))
    for n in range(2, 6):
        bias = jnp.where(count == n, jnp.float32(-0.5 * math.log(64.0 * n)), bias)
    return bias


def own_bias(pat, i, u, turn):
    second_q = iota((TILE, TILE), 0) % HALF >= BLOCK
    second_k = iota((TILE, TILE), 1) % HALF >= BLOCK
    parts = []
    for qb in range(2):
        bias = half_bias(key_count(pat, i, 2 * u + qb))
        pair = [
            jnp.where(mask_value(pat, i, 2 * u + qb, 2 * turn + kb - qb) > 0, bias, MASKED)
            for kb in range(2)
        ]
        parts.append(jnp.where(second_k, pair[1], pair[0]))
    return jnp.where(second_q, parts[1], parts[0])


def start_copy(src, dst, sem):
    copy = pltpu.make_async_copy(src, dst, sem)
    copy.start()
    return copy


def halo_rows(pat_ref, u, turn, width):
    lane = iota((HALF, width), 1)
    line = iota((HALF, width), 0)
    second_k = lane % HALF >= BLOCK
    extra = jnp.zeros((HALF, width), f32)
    for i in range(2):
        for qb in range(2):
            pair = [
                mask_value(pat_ref, i, 2 * u + qb, 2 * turn + kb - qb).astype(f32)
                for kb in range(2)
            ]
            mask = jnp.where(second_k, pair[1], pair[0])
            count = key_count(pat_ref, i, 2 * u + qb).astype(f32)
            here = (line == i) & (lane >= qb * TILE) & (lane < (qb + 1) * TILE)
            there = (line == i) & (lane >= (qb + 2) * TILE) & (lane < (qb + 3) * TILE)
            extra = jnp.where(here, mask, jnp.where(there, count, extra))
    return extra.astype(bf16)


class Geometry:
    def __init__(self, slots, devs, lon_devs, lon_cols):
        self.devs, self.lon_devs = devs, lon_devs
        self.cap = (slots + devs - 1) // devs + 2
        self.full = self.cap // 8 * 8
        self.rest = self.cap - self.full
        self.shift = 4 if self.rest <= 3 else 8
        self.tail = 2 * self.shift
        self.mark = self.shift - 1
        self.rows = 2 * self.full + self.tail
        self.bulk = devs * self.full
        self.total = self.bulk + devs * self.rest
        self.lon_bits = (lon_cols * lon_devs).bit_length() - 1


def tail_picks(geo, offset):
    shape = (geo.devs, geo.devs * geo.tail)
    base = iota(shape, 1) - iota(shape, 0) * geo.tail
    return jnp.concatenate([one_hot(base == offset + r) for r in range(geo.rest)], axis=0)


def join_slots(geo, ref, feats):
    half = feats // 2
    tail = ref[:, 2 * geo.full : geo.rows, :].reshape(geo.devs * geo.tail, half)
    parts = []
    if geo.full:
        first = ref[:, 0 : geo.full, :].reshape(geo.bulk, half)
        second = ref[:, geo.full : 2 * geo.full, :].reshape(geo.bulk, half)
        parts.append(jnp.concatenate([first, second], axis=1))
    if geo.rest:
        rows = [mm(tail_picks(geo, n * geo.shift), tail) for n in range(2)]
        parts.append(jnp.concatenate(rows, axis=1).astype(bf16))
    return tail, jnp.concatenate(parts, axis=0)


def store_bulk(geo, ref, values):
    half = values.shape[1] // 2
    if geo.full:
        ref[:, 0 : geo.full, :] = values[:, 0:half].reshape(geo.devs, geo.full, half)
        ref[:, geo.full : 2 * geo.full, :] = values[:, half:].reshape(geo.devs, geo.full, half)


def slot_index(geo, owner, rank, live):
    place = jnp.where(
        rank < geo.full,
        owner * geo.full + rank,
        geo.bulk + (rank - geo.full) * geo.devs + owner,
    )
    return jnp.where(live, place, -1)


def pack_body(
    geo, pix_hbm, cnt_ref, rows_hbm, pat_hbm, cot_hbm,
    pay_hbm, slot_ref, east_hbm, west_hbm,
    pix_ref, rows_ref, pat_ref, pay_ref, east_ref, west_ref, sems,
):
    pix_copy = start_copy(pix_hbm, pix_ref, sems.at[0])
    rows_copy = start_copy(rows_hbm, rows_ref, sems.at[1])
    pat_copy = start_copy(pat_hbm, pat_ref, sems.at[2])
    lats = cot_hbm.shape[0]
    sides = ((east_ref, 1, 1), (west_ref, 0, -1))
    cot_copies = [
        start_copy(cot_hbm.at[:, u * HALF : (u + 1) * HALF, :], ref.at[0:lats], sems.at[3 + u])
        for ref, u, _ in sides
    ]
    slots = pix_ref.shape[1]
    upper = one_hot(iota((slots, slots), 0) <= iota((slots, slots), 1))
    pix_copy.wait()
    pix = pix_ref[...]
    lat = lax.shift_right_logical(pix, geo.lon_bits)
    lon = lax.bitwise_and(pix, (1 << geo.lon_bits) - 1)
    owner = lax.shift_right_logical(lat, 4) * geo.lon_devs + lax.shift_right_logical(lon, 5)
    row = lax.bitwise_and(lat, 15)
    col = lax.bitwise_and(lon, 31)
    code = (
        lax.shift_right_logical(row, 3) * (2 * TILE)
        + lax.shift_right_logical(col, 4) * TILE
        + lax.bitwise_and(row, 7) * HALF
        + lax.bitwise_and(col, 15)
        + 1
    )
    live = iota((1, slots), 1) < cnt_ref[0]
    table = (iota((geo.devs, slots), 0) == owner) & live
    table_f = jnp.where(table, 1.0, 0.0)
    table_b = table_f.astype(bf16)
    running = mm(table_b, upper)
    rank = (jnp.sum(running * table_f, axis=0, keepdims=True) - 1.0).astype(i32)
    slot = slot_index(geo, owner, rank, live)
    slot_ref[...] = slot
    high = lax.shift_right_logical(code, 5).astype(f32)
    low = lax.bitwise_and(code, 31).astype(f32)
    place = iota((128, slots), 0)
    codes = jnp.where(place == rank, high, 0.0) + jnp.where(place == rank + 64, low, 0.0)
    meta = mm(table_b, codes.astype(bf16), 1, 1)
    tails = geo.devs * geo.tail
    lift = one_hot(
        iota((tails, geo.devs), 0) == iota((tails, geo.devs), 1) * geo.tail + geo.mark
    )
    lifted = mm(lift, meta.astype(bf16))
    pat_copy.wait()
    for copy, (ref, u, turn) in zip(cot_copies, sides):
        ref[lats] = halo_rows(pat_ref, u, turn, cot_hbm.shape[2])
        copy.wait()
    outs = [
        start_copy(east_ref, east_hbm, sems.at[5]),
        start_copy(west_ref, west_hbm, sems.at[6]),
    ]
    place = iota((tails, slots), 0)
    line = jnp.where(live & (rank >= geo.full), owner * geo.tail + rank - geo.full, -geo.tail)
    first = one_hot(place == line)
    second = one_hot(place == line + geo.shift)
    rows_copy.wait()
    half = rows_ref.shape[1] // 2
    if geo.full:
        spread = one_hot(iota((geo.bulk, slots), 0) == slot)
        store_bulk(geo, pay_ref, mm(spread, rows_ref[...]).astype(bf16))
    tail = mm(first, rows_ref[:, 0:half]) + mm(second, rows_ref[:, half:]) + lifted
    pay_ref[:, 2 * geo.full : geo.rows, :] = tail.astype(bf16).reshape(geo.devs, geo.tail, half)
    outs.append(start_copy(pay_ref, pay_hbm, sems.at[7]))
    for copy in outs:
        copy.wait()


def grad_body(
    cot_hbm, west_ref, east_ref, wout_hbm,
    gm_hbm, gw_hbm, ge_hbm, bw_hbm, be_hbm,
    cot_ref, wout_ref,
    gm_ref, gw_ref, ge_ref, bw_ref, be_ref, in_sems, out_sems,
):
    wout_copy = start_copy(wout_hbm, wout_ref, in_sems.at[0])
    cot_copy = start_copy(cot_hbm, cot_ref, in_sems.at[1])
    wout_copy.wait()
    cot_copy.wait()
    wout = wout_ref[...]
    for i, u in halves():
        part = mm(chunk(cot_ref, i, u), wout, 1, 1)
        gm_ref[rows_of(i, u), :] = part.astype(bf16)
    outs = [start_copy(gm_ref, gm_hbm, out_sems.at[0])]
    second_q = iota((TILE, TILE), 0) % HALF >= BLOCK
    for n, (src, dst, bias_ref, dst_hbm, bias_hbm) in enumerate(
        (
            (west_ref, gw_ref, bw_ref, gw_hbm, bw_hbm),
            (east_ref, ge_ref, be_ref, ge_hbm, be_hbm),
        )
    ):
        rows = src.shape[0] - 1
        part = mm(src[0:rows].reshape(2 * TILE, wout.shape[0]), wout, 1, 1)
        dst[...] = part.astype(bf16)
        extra = src[rows].astype(f32)
        for i in range(2):
            line = extra[i : i + 1, :]
            mask = jnp.where(second_q, line[:, TILE : 2 * TILE], line[:, 0:TILE])
            count = jnp.where(second_q, line[:, 3 * TILE : 4 * TILE], line[:, 2 * TILE : 3 * TILE])
            bias = -0.5 * jnp.log(count * 64.0)
            bias_ref[i * TILE : (i + 1) * TILE, :] = jnp.where(mask > 0.5, bias, MASKED)
        outs += [
            start_copy(dst, dst_hbm, out_sems.at[1 + 2 * n]),
            start_copy(bias_ref, bias_hbm, out_sems.at[2 + 2 * n]),
        ]
    for copy in outs:
        copy.wait()


def state_body(geo, arr_ref, wenc_ref, bg_ref, state_ref, n_ref, n0_ref, n1_ref, inv_ref, oht_ref):
    devs, feats = geo.devs, wenc_ref.shape[0]
    tails, arr = join_slots(geo, arr_ref, feats)
    pick = one_hot(
        iota((devs, devs * geo.tail), 1) == iota((devs, devs * geo.tail), 0) * geo.tail + geo.mark
    )
    meta = mm(pick, tails).astype(bf16)
    codes = []
    if geo.full:
        shape = (devs, geo.full, devs)
        owner = one_hot(iota(shape, 0) == iota(shape, 2)).reshape(geo.bulk, devs)
        place = iota((devs, geo.full, 128), 1).reshape(geo.bulk, 128)
        lane = iota((geo.bulk, 128), 1)
        scale = jnp.where(lane == place, 32.0, 0.0) + jnp.where(lane == place + 64, 1.0, 0.0)
        codes.append(jnp.sum(mm(owner, meta) * scale, axis=1, keepdims=True))
    spare = meta.astype(f32)
    for r in range(geo.full, geo.cap):
        codes.append(spare[:, r : r + 1] * 32.0 + spare[:, 64 + r : 65 + r])
    code = jnp.concatenate(codes, axis=0).astype(i32)
    pixels = n_ref.shape[0]
    oht = one_hot(code == iota((geo.total, pixels), 1) + 1)
    oht_ref[...] = oht
    pre = mm(arr, wenc_ref[...])
    _, tangent = gelu_parts(pre)
    encoded = (0.5 * pre * (1.0 + tangent)).astype(bf16)
    obs_sum = mm(oht, encoded, 0, 0)
    number = mm(oht, jnp.ones((geo.total, 128), bf16), 0, 0)
    inverse = 1.0 / (1.0 + number)
    inv_ref[...] = inverse
    for i, u in halves():
        rows = rows_of(i, u)
        fresh = obs_sum[rows] * inverse[rows, 0:1]
        state = (chunk(bg_ref, i, u).astype(f32) + fresh).astype(bf16)
        state_ref[rows, :] = state
        wide_state = state.astype(f32)
        inv_rms = lax.rsqrt(jnp.mean(wide_state * wide_state, axis=1, keepdims=True) + norm_eps)
        normed = (wide_state * inv_rms).astype(bf16)
        n_ref[rows, :] = normed
        side = n1_ref if u else n0_ref
        side[i * TILE : (i + 1) * TILE, :] = normed


def head_lanes(shape, head, dim=1):
    return lax.shift_right_logical(iota(shape, dim), 6) == head


def split_heads(slab):
    return [jnp.where(head_lanes(slab.shape, h), slab, jnp.zeros((), slab.dtype)) for h in range(2)]


def stack_heads(slab):
    return jnp.concatenate(split_heads(slab), axis=0)


def weigh(score, grad, bias):
    weight = jnp.tanh(score + bias) + 1.0
    slope = grad * weight * (2.0 - weight)
    return weight.astype(bf16), slope.astype(bf16)


def pipeline(items, stages):
    states = [None] * len(items)
    for step in range(len(items) + len(stages) - 1):
        for lag, stage in enumerate(stages):
            n = step - lag
            if 0 <= n < len(items):
                states[n] = stage(items[n], states[n])


def project(src, wqkv_ref, q_ref, k_ref, v_ref, rows):
    chans = src.shape[1]
    queries = mm(src, wqkv_ref[:, 0:chans]).astype(bf16).astype(f32) * 0.0625
    q_ref[rows, :] = queries.astype(bf16)
    k_ref[rows, :] = mm(src, wqkv_ref[:, chans : 2 * chans]).astype(bf16)
    v_ref[rows, :] = mm(src, wqkv_ref[:, 2 * chans : 3 * chans]).astype(bf16)


def slab_lanes(s):
    return slice(s * SLAB, (s + 1) * SLAB)


def own_body(
    geo, n_ref, wqkv_ref, gm_ref, pat_hbm, arr_ref, wenc_ref, state_ref,
    q_ref, k_ref, v_ref, dq_ref, dk_ref, dv_ref, slope_ref, weight_hbm, v_hbm, state_hbm,
    pat_ref, weight_ref, sems,
):
    chans = n_ref.shape[1]
    pat_copy = start_copy(pat_hbm, pat_ref, sems.at[0])
    state_copy = start_copy(state_ref, state_hbm, sems.at[1])
    project(n_ref[...], wqkv_ref, q_ref, k_ref, v_ref, slice(0, n_ref.shape[0]))
    v_copy = start_copy(v_ref, v_hbm, sems.at[2])
    pat_copy.wait()
    biases = []
    for i in range(2):
        bias = [
            jnp.concatenate([own_bias(pat_ref, i, u, -u), own_bias(pat_ref, i, u, 1 - u)], axis=1)
            for u in range(2)
        ]
        biases.append(jnp.concatenate(bias, axis=0))

    def first(item, _):
        i, s, h = item
        keys, lanes = slice(i * 2 * TILE, (i + 1) * 2 * TILE), slab_lanes(s)
        km = split_heads(k_ref[keys, lanes])[h]
        vm = split_heads(v_ref[keys, lanes])[h]
        return km, mm(q_ref[keys, lanes], km, 1, 1), mm(gm_ref[keys, lanes], vm, 1, 1)

    def second(item, state):
        i, s, h = item
        km, score, grad = state
        weight, slope = weigh(score, grad, biases[i])
        weight_ref[i, 2 * s + h] = weight
        return km, weight, slope

    held = {}

    def third(item, state):
        i, s, h = item
        keys, lanes = slice(i * 2 * TILE, (i + 1) * 2 * TILE), slab_lanes(s)
        km, weight, slope = state
        parts = (
            mm(slope, km),
            mm(slope, q_ref[keys, lanes], 0, 0),
            mm(weight, gm_ref[keys, lanes], 0, 0),
        )
        if h == 0:
            held[i, s] = parts
            return
        before = held.pop((i, s))
        lower = iota((2 * TILE, SLAB), 1) < SLAB // 2
        dq_ref[keys, lanes] = before[0] + parts[0]
        dk_ref[keys, lanes] = jnp.where(lower, before[1], parts[1])
        dv_ref[keys, lanes] = jnp.where(lower, before[2], parts[2])

    pipeline(
        [(i, s, h) for i in range(2) for s in range(chans // SLAB) for h in range(2)],
        (first, second, third),
    )
    weight_copy = start_copy(weight_ref, weight_hbm, sems.at[3])
    pre = mm(join_slots(geo, arr_ref, wenc_ref.shape[0])[1], wenc_ref[...])
    square, tangent = gelu_parts(pre)
    slope_ref[...] = 0.5 * (1.0 + tangent) + 0.5 * pre * (1.0 - tangent * tangent) * gelu_coef * (
        1.0 + 3.0 * 0.044715 * square
    )
    for copy in (state_copy, v_copy, weight_copy):
        copy.wait()


def rim_body(
    geo, nw_ref, ne_ref, wqkv_ref, q_ref, k_ref, v_ref, gm_ref, gw_ref, ge_ref,
    bw_ref, be_ref, pat_hbm, dq_ref, dk_ref, dv_ref, state_ref, cot_ref, inv_ref,
    oht_ref, slope_ref, wenc_ref,
    v_hbm, weight_hbm, gback_hbm, reply_hbm,
    pat_ref, rim_q, rim_k, rim_v, weight_ref, gback_ref, grad_ref, reply_ref, sems,
):
    chans = q_ref.shape[1]
    pat_copy = start_copy(pat_hbm, pat_ref, sems.at[0])
    for side, src in enumerate((nw_ref, ne_ref)):
        rows = slice(side * 2 * TILE, (side + 1) * 2 * TILE)
        project(src[...], wqkv_ref, rim_q, rim_k, rim_v, rows)
    v_copy = start_copy(rim_v, v_hbm, sems.at[1])
    pat_copy.wait()
    out_bias, in_bias = {}, {}
    for i in range(2):
        for side, bias_ref in enumerate((bw_ref, be_ref)):
            bias = own_bias(pat_ref, i, side, 2 * side - 1)
            out_bias[i, side] = jnp.concatenate([bias, bias], axis=1)
            bias = bias_ref[i * TILE : (i + 1) * TILE, :]
            in_bias[i, side] = jnp.concatenate([bias, bias], axis=1)

    def where(item):
        i, side, s = item
        far = slice((side * 2 + i) * TILE, (side * 2 + i + 1) * TILE)
        near = slice(i * TILE, (i + 1) * TILE)
        return rows_of(i, side), far, near, (gw_ref, ge_ref)[side], slab_lanes(s)

    def first(item, _):
        own, far, near, gh_ref, lanes = where(item)
        km = stack_heads(rim_k[far, lanes])
        return (
            km,
            mm(q_ref[own, lanes], km, 1, 1),
            mm(gm_ref[own, lanes], stack_heads(rim_v[far, lanes]), 1, 1),
            mm(rim_q[far, lanes], stack_heads(k_ref[own, lanes]), 1, 1),
            mm(gh_ref[near, lanes], stack_heads(v_ref[own, lanes]), 1, 1),
        )

    def second(item, state):
        i, side, s = item
        km, score_out, grad_out, score_in, grad_in = state
        weight, slope_out = weigh(score_out, grad_out, out_bias[i, side])
        weight_ref[i * 2 + side, s] = weight
        weight_in, slope_in = weigh(score_in, grad_in, in_bias[i, side])
        return km, slope_out, weight_in, slope_in

    def third(item, state):
        own, far, near, gh_ref, lanes = where(item)
        km, slope_out, weight_in, slope_in = state
        grad_q = mm(slope_out, km)
        grad_k = mm(slope_in, rim_q[far, lanes], 0, 0)
        grad_v = mm(weight_in, gh_ref[near, lanes], 0, 0)
        lower = iota((TILE, SLAB), 1) < SLAB // 2
        grad_k = jnp.where(lower, grad_k[0:TILE], grad_k[TILE:])
        grad_v = jnp.where(lower, grad_v[0:TILE], grad_v[TILE:])
        for n, total in enumerate(
            (
                (dq_ref[own, lanes] + grad_q) * 0.03125,
                (dk_ref[own, lanes] + grad_k) * 0.5,
                (dv_ref[own, lanes] + grad_v) * 0.5,
            )
        ):
            spot = slice(n * chans + lanes.start, n * chans + lanes.stop)
            grad_ref[own, spot] = total.astype(bf16)

    pipeline(
        [(i, side, s) for i in range(2) for side in range(2) for s in range(chans // SLAB)],
        (first, second, third),
    )
    weight_copy = start_copy(weight_ref, weight_hbm, sems.at[2])
    scaled = []
    for i, u in halves():
        rows = rows_of(i, u)
        grad = mm(grad_ref[rows, :], wqkv_ref[...], 1, 1)
        state = state_ref[rows, :].astype(f32)
        inv_rms = lax.rsqrt(jnp.mean(state * state, axis=1, keepdims=True) + norm_eps)
        normed = state * inv_rms
        grad_state = chunk(cot_ref, i, u).astype(f32) + inv_rms * (
            grad - normed * jnp.mean(grad * normed, axis=1, keepdims=True)
        )
        gback_ref[rows, :] = grad_state.astype(bf16)
        scaled.append((grad_state * inv_ref[rows, 0:1]).astype(bf16))
    gback_copy = start_copy(gback_ref, gback_hbm, sems.at[3])
    scaled = jnp.concatenate(scaled, axis=0)
    grad_enc = mm(oht_ref[...], scaled)
    grad_pre = (grad_enc * slope_ref[...]).astype(bf16)
    reply = mm(grad_pre, wenc_ref[...], 1, 1).astype(bf16)
    store_bulk(geo, reply_ref, reply[0 : geo.bulk])
    half = reply.shape[1] // 2
    tail = jnp.zeros((geo.devs * geo.tail, half), f32)
    if geo.rest:
        for n in range(2):
            tail = tail + mm(
                tail_picks(geo, n * geo.shift), reply[geo.bulk :, n * half : (n + 1) * half], 0, 0
            )
    reply_ref[:, 2 * geo.full : geo.rows, :] = tail.astype(bf16).reshape(geo.devs, geo.tail, half)
    reply_copy = start_copy(reply_ref, reply_hbm, sems.at[4])
    for copy in (v_copy, weight_copy, gback_copy, reply_copy):
        copy.wait()


def out_body(*refs):
    hbm, (out_ref, back_ref), local, (mixed_ref, sems) = refs[:7], refs[7:9], refs[9:16], refs[16:]
    copies = [start_copy(src, dst, sems.at[n]) for n, (src, dst) in enumerate(zip(hbm, local))]
    for copy in copies:
        copy.wait()
    weight_ref, far_ref, v_ref, rim_v, wout_ref, state_ref, gback_ref = local
    chans = wout_ref.shape[0]
    for i in range(2):
        keys = slice(i * 2 * TILE, (i + 1) * 2 * TILE)
        for s in range(chans // SLAB):
            lanes = slice(s * SLAB, (s + 1) * SLAB)
            vm = split_heads(v_ref[keys, lanes])
            mixed = mm(weight_ref[i, 2 * s], vm[0]) + mm(weight_ref[i, 2 * s + 1], vm[1])
            for side in range(2):
                far = slice((side * 2 + i) * TILE, (side * 2 + i + 1) * TILE)
                total = mixed[side * TILE : (side + 1) * TILE] + mm(
                    far_ref[i * 2 + side, s], stack_heads(rim_v[far, lanes])
                )
                mixed_ref[rows_of(i, side), lanes] = (total * 0.5).astype(bf16)
    for i, u in halves():
        rows = rows_of(i, u)
        place = (slice(i * BLOCK, (i + 1) * BLOCK), slice(u * HALF, (u + 1) * HALF))
        total = state_ref[rows, :].astype(f32) + mm(mixed_ref[rows, :], wout_ref[...])
        out_ref[place[0], place[1], :] = total.astype(bf16).reshape(BLOCK, HALF, chans)
        back_ref[place[0], place[1], :] = gback_ref[rows, :].reshape(BLOCK, HALF, chans)


def unpack_body(geo, back_ref, slot_ref, out_ref):
    feats = out_ref.shape[1]
    slots = slot_ref.shape[1]
    spread = one_hot(iota((geo.total, slots), 0) == slot_ref[...])
    out_ref[...] = mm(spread, join_slots(geo, back_ref, feats)[1], 0, 0).astype(bf16)


def shards(
    background, obs_rows, obs_pixel, obs_count, block_pattern, w_enc, w_qkv, w_out, cotangent
):
    lat_rows, lon_cols, chans = background.shape
    pixels = lat_rows * lon_cols
    slots, feats = obs_rows.shape
    lon_devs = lax.axis_size("lon")
    geo = Geometry(slots, lax.axis_size("lat") * lon_devs, lon_devs, lon_cols)
    side = pixels // 2
    half = feats // 2
    up = [(i, (i + 1) % lon_devs) for i in range(lon_devs)]
    down = [(j, i) for i, j in up]

    rim = (lat_rows + 1, HALF, chans)
    wide, edge = (pixels, chans), (side, chans)
    weights_own = (2, HEADS, 2 * TILE, 2 * TILE)
    weights_far = (4, chans // SLAB, TILE, 2 * TILE)
    dma = pltpu.SemaphoreType.DMA
    pattern = pltpu.SMEM(block_pattern.shape, i32)

    def vmem(*shapes):
        return [pltpu.VMEM(shape, bf16) for shape in shapes]

    payload, slot, cot_east, cot_west = call(
        functools.partial(pack_body, geo),
        [((geo.devs, geo.rows, half), bf16), ((1, slots), i32), (rim, bf16), (rim, bf16)],
        scratch=[pltpu.VMEM((1, slots), i32), pltpu.VMEM((slots, feats), bf16), pattern]
        + vmem((geo.devs, geo.rows, half), rim, rim)
        + [dma((8,))],
        n_in=5,
        n_smem=(1,),
        n_hbm=(0, 2, 3, 4),
        out_hbm=(0, 2, 3),
        flops=400 << 20,
    )(obs_pixel.reshape(1, slots), obs_count, obs_rows, block_pattern, cotangent)
    west_cot = lax.ppermute(cot_east, "lon", up)
    east_cot = lax.ppermute(cot_west, "lon", down)
    arrived = lax.all_to_all(payload, ("lat", "lon"), split_axis=0, concat_axis=0, tiled=True)
    gm, gw, ge, bias_w, bias_e = call(
        grad_body,
        [
            (wide, bf16),
            (edge, bf16),
            (edge, bf16),
            ((side, TILE), f32),
            ((side, TILE), f32),
        ],
        scratch=vmem((lat_rows, lon_cols, chans), (chans, chans))
        + vmem(wide, edge, edge)
        + [pltpu.VMEM((side, TILE), f32)] * 2
        + [dma((2,)), dma((5,))],
        n_in=4,
        n_hbm=(0, 3),
        out_hbm=range(5),
        flops=GRAD_COST,
    )(cotangent, west_cot, east_cot, w_out)
    state, normed, n0, n1, inverse, oht = call(
        functools.partial(state_body, geo),
        [
            (wide, bf16),
            (wide, bf16),
            (edge, bf16),
            (edge, bf16),
            ((pixels, 128), f32),
            ((geo.total, pixels), bf16),
        ],
        n_in=3,
        flops=1 << 30,
    )(arrived, w_enc, background)
    n_west = lax.ppermute(n1, "lon", up)
    n_east = lax.ppermute(n0, "lon", down)
    q, k, v, dq, dk, dv, slope, weight, v_far, state_far = call(
        functools.partial(own_body, geo),
        [(wide, bf16)] * 3
        + [(wide, f32)] * 3
        + [((geo.total, chans), f32), (weights_own, bf16), (wide, bf16), (wide, bf16)],
        scratch=[pattern] + vmem(weights_own) + [dma((4,))],
        n_in=7,
        n_hbm=(3,),
        out_hbm=(7, 8, 9),
        flops=4 << 30,
    )(normed, w_qkv, gm, block_pattern, arrived, w_enc, state)
    rim_v, far, gback, reply = call(
        functools.partial(rim_body, geo),
        [(wide, bf16), (weights_far, bf16), (wide, bf16), ((geo.devs, geo.rows, half), bf16)],
        scratch=[pattern]
        + vmem(wide, wide, wide, weights_far, wide, (pixels, 3 * chans), (geo.devs, geo.rows, half))
        + [dma((5,))],
        n_in=21,
        n_hbm=(11,),
        out_hbm=(0, 1, 2, 3),
        flops=4 << 30,
    )(
        n_west, n_east, w_qkv, q, k, v, gm, gw, ge, bias_w, bias_e, block_pattern,
        dq, dk, dv, state, cotangent, inverse, oht, slope, w_enc,
    )
    returned = lax.all_to_all(reply, ("lat", "lon"), split_axis=0, concat_axis=0, tiled=True)
    updated, grad_background = call(
        out_body,
        [((lat_rows, lon_cols, chans), bf16), ((lat_rows, lon_cols, chans), bf16)],
        scratch=vmem(weights_own, weights_far, wide, wide, (chans, chans), wide, wide, wide)
        + [dma((7,))],
        n_in=7,
        n_hbm=range(7),
        flops=1 << 30,
    )(weight, far, v_far, rim_v, w_out, state_far, gback)
    (grad_obs,) = call(
        functools.partial(unpack_body, geo), [((slots, feats), bf16)], n_in=2, flops=1 << 28
    )(returned, slot)
    return (updated, grad_background, grad_obs)


def solution(mesh):
    return jax.shard_map(
        shards,
        mesh=mesh,
        in_specs=(
            P("lat", "lon", None),
            P(("lat", "lon"), None),
            P(("lat", "lon")),
            P(("lat", "lon")),
            P("lat", "lon", None),
            P(),
            P(),
            P(),
            P("lat", "lon", None),
        ),
        out_specs=(P("lat", "lon", None), P("lat", "lon", None), P(("lat", "lon"), None)),
        check_vma=False,
    )
```

```python
import functools
import math

import jax
import jax.numpy as jnp
from jax import lax
from jax.experimental import pallas as pl
from jax.experimental.pallas import tpu as pltpu
from jax.sharding import PartitionSpec as P

HEADS = 8
BLOCK = 8
HALF = 2 * BLOCK
TILE = BLOCK * HALF
SLAB = 128
MASKED = -1e30
GRAD_COST = 1 << 37
GROUPS = 4
BATCH = 2
STRIP = 32

norm_eps = 1e-06
gelu_coef = 0.7978845608028654

bf16 = jnp.bfloat16
f32 = jnp.float32
i32 = jnp.int32


def iota(shape, dim):
    return lax.broadcasted_iota(i32, shape, dim)


def mm(lhs, rhs, lhs_dim=1, rhs_dim=0):
    return lax.dot_general(
        lhs, rhs, (((lhs_dim,), (rhs_dim,)), ((), ())), preferred_element_type=f32
    )


def one_hot(cond):
    return jnp.where(cond, 1.0, 0.0).astype(bf16)


def gelu_parts(inputs):
    square = inputs * inputs
    tangent = jnp.tanh(gelu_coef * inputs * (1.0 + 0.044715 * square))
    return square, tangent


def call(
    body, outs, scratch=(), flops=0, n_smem=(), n_hbm=(), out_hbm=(), n_in=0, size=1 << 20, vmem=16
):
    def spec(k, smem, hbm):
        if k in hbm:
            return pl.BlockSpec(memory_space=pltpu.HBM)
        return pl.BlockSpec(memory_space=pltpu.SMEM if k in smem else pltpu.VMEM)

    kernel = pl.pallas_call(
        body,
        out_shape=[
            pltpu.HBM(s, d) if k in out_hbm else jax.ShapeDtypeStruct(s, d)
            for k, (s, d) in enumerate(outs)
        ],
        in_specs=[spec(k, n_smem, n_hbm) for k in range(n_in)],
        out_specs=[spec(k, (), out_hbm) for k in range(len(outs))],
        scratch_shapes=list(scratch),
        compiler_params=pltpu.CompilerParams(vmem_limit_bytes=vmem << 20),
        cost_estimate=pl.CostEstimate(flops=flops, bytes_accessed=size, transcendentals=0),
    )

    def run(*args):
        return kernel(
            *[
                pltpu.with_memory_space_constraint(x, pltpu.HBM) if k in n_hbm else x
                for k, x in enumerate(args)
            ]
        )

    return run


def chunk(ref, row_block, half):
    part = ref[
        row_block * BLOCK : (row_block + 1) * BLOCK, half * HALF : (half + 1) * HALF, :
    ]
    return part.reshape(TILE, part.shape[-1])


def halves():
    return [(i, u) for i in range(2) for u in range(2)]


def rows_of(i, u):
    return slice((i * 2 + u) * TILE, (i * 2 + u + 1) * TILE)


def key_count(pat, i, b):
    return 1 + pat[i, b, 0] + pat[i, b, 1] + pat[i, b, 2] + pat[i, b, 3]


def mask_value(pat, i, b, shift):
    if abs(shift) > 2:
        return jnp.int32(0)
    if shift == 0:
        return jnp.int32(1)
    return pat[i, b, shift + 2 if shift < 0 else shift + 1]


def half_bias(count):
    bias = jnp.float32(-0.5 * math.log(64.0))
    for n in range(2, 6):
        bias = jnp.where(count == n, jnp.float32(-0.5 * math.log(64.0 * n)), bias)
    return bias


def own_bias(pat, i, u, turn):
    second_q = iota((TILE, TILE), 0) % HALF >= BLOCK
    second_k = iota((TILE, TILE), 1) % HALF >= BLOCK
    parts = []
    for qb in range(2):
        bias = half_bias(key_count(pat, i, 2 * u + qb))
        pair = [
            jnp.where(mask_value(pat, i, 2 * u + qb, 2 * turn + kb - qb) > 0, bias, MASKED)
            for kb in range(2)
        ]
        parts.append(jnp.where(second_k, pair[1], pair[0]))
    return jnp.where(second_q, parts[1], parts[0])


def start_copy(src, dst, sem):
    copy = pltpu.make_async_copy(src, dst, sem)
    copy.start()
    return copy


def halo_rows(pat_ref, u, turn, width):
    lane = iota((HALF, width), 1)
    line = iota((HALF, width), 0)
    second_k = lane % HALF >= BLOCK
    extra = jnp.zeros((HALF, width), f32)
    for i in range(2):
        for qb in range(2):
            pair = [
                mask_value(pat_ref, i, 2 * u + qb, 2 * turn + kb - qb).astype(f32)
                for kb in range(2)
            ]
            mask = jnp.where(second_k, pair[1], pair[0])
            count = key_count(pat_ref, i, 2 * u + qb).astype(f32)
            here = (line == i) & (lane >= qb * TILE) & (lane < (qb + 1) * TILE)
            there = (line == i) & (lane >= (qb + 2) * TILE) & (lane < (qb + 3) * TILE)
            extra = jnp.where(here, mask, jnp.where(there, count, extra))
    return extra.astype(bf16)


def pipeline(items, stages, extra=None):
    states = [None] * len(items)
    extra = extra or {}
    for step in range(max([len(items) + len(stages) - 1] + [n + 1 for n in extra])):
        for lag, stage in enumerate(stages):
            n = step - lag
            if 0 <= n < len(items):
                states[n] = stage(items[n], states[n])
        for task in extra.get(step, ()):
            task()


def batch(items, stages, size):
    groups = [items[n : n + size] for n in range(0, len(items), size)]

    def lift(stage):
        return lambda group, states: [
            stage(item, state) for item, state in zip(group, states or [None] * len(group))
        ]

    return groups, tuple(lift(stage) for stage in stages)


class Geometry:
    def __init__(self, slots, devs, lon_devs, lon_cols):
        self.devs, self.lon_devs = devs, lon_devs
        self.cap = (slots + devs - 1) // devs + 2
        self.full = self.cap // 8 * 8
        self.rest = self.cap - self.full
        self.shift = 4 if self.rest <= 3 else 8
        self.tail = 2 * self.shift
        self.mark = self.shift - 1
        self.rows = 2 * self.full + self.tail
        self.bulk = devs * self.full
        self.total = self.bulk + devs * self.rest
        self.lon_bits = (lon_cols * lon_devs).bit_length() - 1


def tail_picks(geo, offset):
    shape = (geo.devs, geo.devs * geo.tail)
    base = iota(shape, 1) - iota(shape, 0) * geo.tail
    return jnp.concatenate([one_hot(base == offset + r) for r in range(geo.rest)], axis=0)


def join_slots(geo, ref, feats):
    half = feats // 2
    tail = ref[:, 2 * geo.full : geo.rows, :].reshape(geo.devs * geo.tail, half)
    parts = []
    if geo.full:
        first = ref[:, 0 : geo.full, :].reshape(geo.bulk, half)
        second = ref[:, geo.full : 2 * geo.full, :].reshape(geo.bulk, half)
        parts.append(jnp.concatenate([first, second], axis=1))
    if geo.rest:
        rows = [mm(tail_picks(geo, n * geo.shift), tail) for n in range(2)]
        parts.append(jnp.concatenate(rows, axis=1).astype(bf16))
    return tail, jnp.concatenate(parts, axis=0)


def send_groups(geo, ref, hbm, sems, base, stages):
    copies = []
    if not geo.full:
        copies.append(start_copy(ref, hbm, sems.at[base]))
        return copies
    step = geo.devs // GROUPS

    def store(item, values):
        n, lo, hi = item
        half = values.shape[1] // 2
        values = values.astype(bf16)
        ref[lo:hi, 0 : geo.full, :] = values[:, 0:half].reshape(hi - lo, geo.full, half)
        ref[lo:hi, geo.full : 2 * geo.full, :] = values[:, half:].reshape(hi - lo, geo.full, half)
        copies.append(start_copy(ref.at[lo:hi], hbm.at[lo:hi], sems.at[base + n]))

    pipeline([(n, n * step, (n + 1) * step) for n in range(GROUPS)], tuple(stages) + (store,))
    return copies


def slot_index(geo, owner, rank, live):
    place = jnp.where(
        rank < geo.full,
        owner * geo.full + rank,
        geo.bulk + (rank - geo.full) * geo.devs + owner,
    )
    return jnp.where(live, place, -1)


def pack_body(
    geo, pix_hbm, cnt_ref, rows_hbm, pat_hbm, cot_hbm,
    pay_hbm, slot_ref, east_hbm, west_hbm,
    pix_ref, rows_ref, pat_ref, pay_ref, east_ref, west_ref, sems,
):
    pix_copy = start_copy(pix_hbm, pix_ref, sems.at[0])
    rows_copy = start_copy(rows_hbm, rows_ref, sems.at[1])
    pat_copy = start_copy(pat_hbm, pat_ref, sems.at[2])
    lats = cot_hbm.shape[0]
    sides = ((east_ref, 1, 1), (west_ref, 0, -1))
    cot_copies = [
        start_copy(cot_hbm.at[:, u * HALF : (u + 1) * HALF, :], ref.at[0:lats], sems.at[3 + u])
        for ref, u, _ in sides
    ]
    slots = pix_ref.shape[1]
    upper = one_hot(iota((slots, slots), 0) <= iota((slots, slots), 1))
    pix_copy.wait()
    pix = pix_ref[...]
    lat = lax.shift_right_logical(pix, geo.lon_bits)
    lon = lax.bitwise_and(pix, (1 << geo.lon_bits) - 1)
    owner = lax.shift_right_logical(lat, 4) * geo.lon_devs + lax.shift_right_logical(lon, 5)
    row = lax.bitwise_and(lat, 15)
    col = lax.bitwise_and(lon, 31)
    code = (
        lax.shift_right_logical(row, 3) * (2 * TILE)
        + lax.shift_right_logical(col, 4) * TILE
        + lax.bitwise_and(row, 7) * HALF
        + lax.bitwise_and(col, 15)
        + 1
    )
    live = iota((1, slots), 1) < cnt_ref[0]
    table = (iota((geo.devs, slots), 0) == owner) & live
    table_f = jnp.where(table, 1.0, 0.0)
    table_b = table_f.astype(bf16)
    running = mm(table_b, upper)
    rank = (jnp.sum(running * table_f, axis=0, keepdims=True) - 1.0).astype(i32)
    slot = slot_index(geo, owner, rank, live)
    slot_ref[...] = slot
    high = lax.shift_right_logical(code, 5).astype(f32)
    low = lax.bitwise_and(code, 31).astype(f32)
    place = iota((128, slots), 0)
    codes = jnp.where(place == rank, high, 0.0) + jnp.where(place == rank + 64, low, 0.0)
    meta = mm(table_b, codes.astype(bf16), 1, 1)
    tails = geo.devs * geo.tail
    lift = one_hot(
        iota((tails, geo.devs), 0) == iota((tails, geo.devs), 1) * geo.tail + geo.mark
    )
    lifted = mm(lift, meta.astype(bf16))
    pat_copy.wait()
    for copy, (ref, u, turn) in zip(cot_copies, sides):
        ref[lats] = halo_rows(pat_ref, u, turn, cot_hbm.shape[2])
        copy.wait()
    outs = [
        start_copy(east_ref, east_hbm, sems.at[5]),
        start_copy(west_ref, west_hbm, sems.at[6]),
    ]
    place = iota((tails, slots), 0)
    line = jnp.where(live & (rank >= geo.full), owner * geo.tail + rank - geo.full, -geo.tail)
    first = one_hot(place == line)
    second = one_hot(place == line + geo.shift)
    rows_copy.wait()
    half = rows_ref.shape[1] // 2
    tail = mm(first, rows_ref[:, 0:half]) + mm(second, rows_ref[:, half:]) + lifted
    pay_ref[:, 2 * geo.full : geo.rows, :] = tail.astype(bf16).reshape(geo.devs, geo.tail, half)

    def spread(item, _):
        base = item[1] * geo.full
        hot = one_hot(iota(((item[2] - item[1]) * geo.full, slots), 0) + base == slot)
        return mm(hot, rows_ref[...])

    outs += send_groups(geo, pay_ref, pay_hbm, sems, 7, (spread,))
    for copy in outs:
        copy.wait()


def grad_body(
    cot_hbm, west_ref, east_ref, wout_hbm,
    gm_hbm, gw_hbm, ge_hbm, bw_hbm, be_hbm,
    cot_ref, wout_ref,
    gm_ref, gw_ref, ge_ref, bw_ref, be_ref, in_sems, out_sems,
):
    wout_copy = start_copy(wout_hbm, wout_ref, in_sems.at[0])
    cot_copy = start_copy(cot_hbm, cot_ref, in_sems.at[1])
    wout_copy.wait()
    cot_copy.wait()
    wout = wout_ref[...]
    for i, u in halves():
        part = mm(chunk(cot_ref, i, u), wout, 1, 1)
        gm_ref[rows_of(i, u), :] = part.astype(bf16)
    outs = [start_copy(gm_ref, gm_hbm, out_sems.at[0])]
    second_q = iota((TILE, TILE), 0) % HALF >= BLOCK
    for n, (src, dst, bias_ref, dst_hbm, bias_hbm) in enumerate(
        (
            (west_ref, gw_ref, bw_ref, gw_hbm, bw_hbm),
            (east_ref, ge_ref, be_ref, ge_hbm, be_hbm),
        )
    ):
        rows = src.shape[0] - 1
        part = mm(src[0:rows].reshape(2 * TILE, wout.shape[0]), wout, 1, 1)
        dst[...] = part.astype(bf16)
        extra = src[rows].astype(f32)
        for i in range(2):
            line = extra[i : i + 1, :]
            mask = jnp.where(second_q, line[:, TILE : 2 * TILE], line[:, 0:TILE])
            count = jnp.where(second_q, line[:, 3 * TILE : 4 * TILE], line[:, 2 * TILE : 3 * TILE])
            bias = -0.5 * jnp.log(count * 64.0)
            bias_ref[i * TILE : (i + 1) * TILE, :] = jnp.where(mask > 0.5, bias, MASKED)
        outs += [
            start_copy(dst, dst_hbm, out_sems.at[1 + 2 * n]),
            start_copy(bias_ref, bias_hbm, out_sems.at[2 + 2 * n]),
        ]
    for copy in outs:
        copy.wait()


def slot_table(geo, tails, pixels):
    pick = one_hot(
        iota((geo.devs, geo.devs * geo.tail), 1) == iota((geo.devs, geo.devs * geo.tail), 0) * geo.tail + geo.mark
    )
    meta = mm(pick, tails).astype(bf16)
    codes = []
    if geo.full:
        shape = (geo.devs, geo.full, geo.devs)
        owner = one_hot(iota(shape, 0) == iota(shape, 2)).reshape(geo.bulk, geo.devs)
        place = iota((geo.devs, geo.full, 128), 1).reshape(geo.bulk, 128)
        lane = iota((geo.bulk, 128), 1)
        scale = jnp.where(lane == place, 32.0, 0.0) + jnp.where(lane == place + 64, 1.0, 0.0)
        codes.append(jnp.sum(mm(owner, meta) * scale, axis=1, keepdims=True))
    spare = meta.astype(f32)
    for r in range(geo.full, geo.cap):
        codes.append(spare[:, r : r + 1] * 32.0 + spare[:, 64 + r : 65 + r])
    code = jnp.concatenate(codes, axis=0).astype(i32)
    return one_hot(code == iota((geo.total, pixels), 1) + 1)


def state_body(geo, arr_ref, wenc_ref, bg_ref, state_ref, n_ref, n0_ref, n1_ref, inv_ref, rms_ref, oht_ref):
    feats = wenc_ref.shape[0]
    tails, arr = join_slots(geo, arr_ref, feats)
    oht = slot_table(geo, tails, n_ref.shape[0])
    oht_ref[...] = oht
    pre = mm(arr, wenc_ref[...])
    _, tangent = gelu_parts(pre)
    encoded = (0.5 * pre * (1.0 + tangent)).astype(bf16)
    obs_sum = mm(oht, encoded, 0, 0)
    number = mm(oht, jnp.ones((geo.total, 128), bf16), 0, 0)
    inverse = 1.0 / (1.0 + number)
    inv_ref[...] = inverse
    for i, u in halves():
        rows = rows_of(i, u)
        fresh = obs_sum[rows] * inverse[rows, 0:1]
        state = (chunk(bg_ref, i, u).astype(f32) + fresh).astype(bf16)
        state_ref[rows, :] = state
        wide_state = state.astype(f32)
        inv_rms = lax.rsqrt(jnp.mean(wide_state * wide_state, axis=1, keepdims=True) + norm_eps)
        rms_ref[rows, :] = jnp.broadcast_to(inv_rms, (TILE, 128))
        normed = (wide_state * inv_rms).astype(bf16)
        n_ref[rows, :] = normed
        side = n1_ref if u else n0_ref
        side[i * TILE : (i + 1) * TILE, :] = normed


def head_lanes(shape, head, dim=1):
    return lax.shift_right_logical(iota(shape, dim), 6) == head


def split_heads(slab):
    return [jnp.where(head_lanes(slab.shape, h), slab, jnp.zeros((), slab.dtype)) for h in range(2)]


def across(lanes, width):
    return jnp.concatenate([lanes] * (width // lanes.shape[1]), axis=1)


def stack_heads(slab):
    return jnp.concatenate(split_heads(slab), axis=0)


def weigh(score, grad, bias):
    weight = jnp.tanh(score + bias) + 1.0
    slope = grad * weight * (2.0 - weight)
    return weight.astype(bf16), slope.astype(bf16)


def project(src, wqkv_ref, q_ref, k_ref, v_ref, rows):
    chans = src.shape[1]
    q_ref[rows, :] = (mm(src, wqkv_ref[:, 0:chans]) * 0.0625).astype(bf16)
    k_ref[rows, :] = mm(src, wqkv_ref[:, chans : 2 * chans]).astype(bf16)
    v_ref[rows, :] = mm(src, wqkv_ref[:, 2 * chans : 3 * chans]).astype(bf16)


def slab_lanes(s):
    return slice(s * SLAB, (s + 1) * SLAB)


def own_body(
    geo, n_ref, wqkv_ref, gm_ref, pat_hbm, arr_ref, wenc_ref, state_ref,
    q_ref, k_ref, v_ref, dq_ref, dk_ref, dv_ref, slope_ref, weight_hbm, v_hbm, state_hbm,
    pat_ref, weight_ref, sems,
):
    chans = n_ref.shape[1]
    pat_copy = start_copy(pat_hbm, pat_ref, sems.at[0])
    state_copy = start_copy(state_ref, state_hbm, sems.at[1])
    project(n_ref[...], wqkv_ref, q_ref, k_ref, v_ref, slice(0, n_ref.shape[0]))
    v_copy = start_copy(v_ref, v_hbm, sems.at[2])
    pat_copy.wait()
    biases = []
    for i in range(2):
        bias = [
            jnp.concatenate([own_bias(pat_ref, i, u, -u), own_bias(pat_ref, i, u, 1 - u)], axis=1)
            for u in range(2)
        ]
        biases.append(jnp.concatenate(bias, axis=0))

    def first(item, _):
        i, s, h = item
        keys, lanes = slice(i * 2 * TILE, (i + 1) * 2 * TILE), slab_lanes(s)
        km = split_heads(k_ref[keys, lanes])[h]
        vm = split_heads(v_ref[keys, lanes])[h]
        return km, mm(q_ref[keys, lanes], km, 1, 1), mm(gm_ref[keys, lanes], vm, 1, 1)

    def second(item, state):
        i, s, h = item
        km, score, grad = state
        weight, slope = weigh(score, grad, biases[i])
        weight_ref[i, 2 * s + h] = weight
        return km, weight, slope

    held, weight_copies = {}, []

    def third(item, state):
        i, s, h = item
        keys, lanes = slice(i * 2 * TILE, (i + 1) * 2 * TILE), slab_lanes(s)
        km, weight, slope = state
        parts = (
            mm(slope, km),
            mm(slope, q_ref[keys, lanes], 0, 0),
            mm(weight, gm_ref[keys, lanes], 0, 0),
        )
        if h == 0:
            held[i, s] = parts
            return
        before = held.pop((i, s))
        lower = iota((2 * TILE, SLAB), 1) < SLAB // 2
        dq_ref[keys, lanes] = before[0] + parts[0]
        dk_ref[keys, lanes] = jnp.where(lower, before[1], parts[1])
        dv_ref[keys, lanes] = jnp.where(lower, before[2], parts[2])
        pair = (i, slice(2 * s, 2 * s + 2))
        sem = sems.at[3 + i * (chans // SLAB) + s]
        weight_copies.append(start_copy(weight_ref.at[pair], weight_hbm.at[pair], sem))

    pipeline(
        [(i, s, h) for i in range(2) for s in range(chans // SLAB) for h in range(2)],
        (first, second, third),
    )
    arr = join_slots(geo, arr_ref, wenc_ref.shape[0])[1]
    pre = mm(arr, wenc_ref[...])
    square, tangent = gelu_parts(pre)
    slope_ref[...] = 0.5 * (1.0 + tangent) + 0.5 * pre * (1.0 - tangent * tangent) * gelu_coef * (
        1.0 + 3.0 * 0.044715 * square
    )
    for copy in [state_copy, v_copy] + weight_copies:
        copy.wait()


def rim_body(
    geo, nw_ref, ne_ref, wqkv_ref, q_ref, k_ref, v_ref, gm_ref, gw_ref, ge_ref,
    bw_ref, be_ref, pat_hbm, dq_ref, dk_ref, dv_ref, state_ref, rms_ref, cot_ref, inv_ref,
    oht_ref, slope_ref, wenc_ref,
    v_hbm, weight_hbm, gback_hbm, reply_hbm,
    pat_ref, rim_q, rim_k, rim_v, weight_ref, gback_ref, scaled_ref, grad_ref, reply_ref, tail_ref, sems,
):
    chans = q_ref.shape[1]
    pat_copy = start_copy(pat_hbm, pat_ref, sems.at[0])
    far_rows = [slice(side * 2 * TILE, (side + 1) * 2 * TILE) for side in range(2)]
    project(nw_ref[...], wqkv_ref, rim_q, rim_k, rim_v, far_rows[0])
    pat_copy.wait()
    out_bias, in_bias = {}, {}
    for i in range(2):
        for side, bias_ref in enumerate((bw_ref, be_ref)):
            bias = own_bias(pat_ref, i, side, 2 * side - 1)
            out_bias[i, side] = jnp.concatenate([bias, bias], axis=1)
            bias = bias_ref[i * TILE : (i + 1) * TILE, :]
            in_bias[i, side] = jnp.concatenate([bias, bias], axis=1)

    def where(item):
        i, side, s = item
        far = slice((side * 2 + i) * TILE, (side * 2 + i + 1) * TILE)
        near = slice(i * TILE, (i + 1) * TILE)
        return rows_of(i, side), far, near, (gw_ref, ge_ref)[side], slab_lanes(s)

    def first(item, _):
        own, far, near, gh_ref, lanes = where(item)
        km = stack_heads(rim_k[far, lanes])
        return (
            km,
            mm(q_ref[own, lanes], km, 1, 1),
            mm(gm_ref[own, lanes], stack_heads(rim_v[far, lanes]), 1, 1),
            mm(rim_q[far, lanes], stack_heads(k_ref[own, lanes]), 1, 1),
            mm(gh_ref[near, lanes], stack_heads(v_ref[own, lanes]), 1, 1),
        )

    def second(item, state):
        i, side, s = item
        km, score_out, grad_out, score_in, grad_in = state
        weight, slope_out = weigh(score_out, grad_out, out_bias[i, side])
        weight_ref[i * 2 + side, s] = weight
        weight_in, slope_in = weigh(score_in, grad_in, in_bias[i, side])
        return km, slope_out, weight_in, slope_in

    def third(item, state):
        own, far, near, gh_ref, lanes = where(item)
        km, slope_out, weight_in, slope_in = state
        grad_q = mm(slope_out, km)
        grad_k = mm(slope_in, rim_q[far, lanes], 0, 0)
        grad_v = mm(weight_in, gh_ref[near, lanes], 0, 0)
        lower = iota((TILE, SLAB), 1) < SLAB // 2
        grad_k = jnp.where(lower, grad_k[0:TILE], grad_k[TILE:])
        grad_v = jnp.where(lower, grad_v[0:TILE], grad_v[TILE:])
        for n, total in enumerate(
            (
                (dq_ref[own, lanes] + grad_q) * 0.03125,
                (dk_ref[own, lanes] + grad_k) * 0.5,
                (dv_ref[own, lanes] + grad_v) * 0.5,
            )
        ):
            spot = slice(n * chans + lanes.start, n * chans + lanes.stop)
            grad_ref[own, spot] = total.astype(bf16)

    back = {}

    def project_back(group):
        back[group] = mm(grad_ref[rows_of(*group), :], wqkv_ref[...], 1, 1)

    def norm_back(item):
        i, u = item
        total = back.pop(item)
        cot = chunk(cot_ref, i, u)
        for n in range(0, TILE, STRIP):
            base = rows_of(i, u).start + n
            rows = slice(base, base + STRIP)
            inv_rms = across(rms_ref[rows, :], chans)
            normed = state_ref[rows, :].astype(f32) * inv_rms
            grad = total[n : n + STRIP]
            grad_state = cot[n : n + STRIP].astype(f32) + inv_rms * (
                grad - normed * jnp.mean(grad * normed, axis=1, keepdims=True)
            )
            gback_ref[rows, :] = grad_state.astype(bf16)
            scaled_ref[rows, :] = (grad_state * across(inv_ref[rows, :], chans)).astype(bf16)

    slabs = chans // SLAB
    groups = [(i, side) for side in range(2) for i in range(2)]
    extra = {
        1: [lambda: project(ne_ref[...], wqkv_ref, rim_q, rim_k, rim_v, far_rows[1])],
    }
    for n, group in enumerate(groups):
        ready = slabs * (n + 1) // BATCH + 1
        extra.setdefault(ready, []).append(functools.partial(project_back, group))
        extra.setdefault(ready + 1, []).append(functools.partial(norm_back, group))
    items = [(i, side, s) for i, side in groups for s in range(slabs)]
    pipeline(*batch(items, (first, second, third), BATCH), extra)
    v_copy = start_copy(rim_v, v_hbm, sems.at[1])
    weight_copy = start_copy(weight_ref, weight_hbm, sems.at[2])
    gback_copy = start_copy(gback_ref, gback_hbm, sems.at[3])

    def pre_grad(lo, hi):
        return (mm(oht_ref[lo:hi, :], scaled_ref[...]) * slope_ref[lo:hi, :]).astype(bf16)

    half = wenc_ref.shape[0] // 2
    tail_ref[...] = jnp.zeros(tail_ref.shape, f32)
    if geo.rest:
        spare = mm(pre_grad(geo.bulk, geo.total), wenc_ref[...], 1, 1)
        for n in range(2):
            for r in range(geo.rest):
                part = spare[r * geo.devs : (r + 1) * geo.devs, n * half : (n + 1) * half]
                tail_ref[:, n * geo.shift + r, :] = part
    reply_ref[:, 2 * geo.full : geo.rows, :] = tail_ref[...].astype(bf16)
    replies = send_groups(
        geo, reply_ref, reply_hbm, sems, 4,
        (
            lambda item, _: pre_grad(item[1] * geo.full, item[2] * geo.full),
            lambda item, rows: mm(rows, wenc_ref[...], 1, 1),
        ),
    )
    for copy in [v_copy, weight_copy, gback_copy] + replies:
        copy.wait()


def out_body(*refs):
    hbm, (out_ref, back_ref), local, (mixed_ref, sems) = refs[:7], refs[7:9], refs[9:16], refs[16:]
    copies = [start_copy(src, dst, sems.at[n]) for n, (src, dst) in enumerate(zip(hbm, local))]
    for copy in copies:
        copy.wait()
    weight_ref, far_ref, v_ref, rim_v, wout_ref, state_ref, gback_ref = local
    chans = wout_ref.shape[0]
    for i in range(2):
        keys = slice(i * 2 * TILE, (i + 1) * 2 * TILE)
        for s in range(chans // SLAB):
            lanes = slice(s * SLAB, (s + 1) * SLAB)
            vm = split_heads(v_ref[keys, lanes])
            mixed = mm(weight_ref[i, 2 * s], vm[0]) + mm(weight_ref[i, 2 * s + 1], vm[1])
            for side in range(2):
                far = slice((side * 2 + i) * TILE, (side * 2 + i + 1) * TILE)
                total = mixed[side * TILE : (side + 1) * TILE] + mm(
                    far_ref[i * 2 + side, s], stack_heads(rim_v[far, lanes])
                )
                mixed_ref[rows_of(i, side), lanes] = (total * 0.5).astype(bf16)
    for i, u in halves():
        rows = rows_of(i, u)
        place = (slice(i * BLOCK, (i + 1) * BLOCK), slice(u * HALF, (u + 1) * HALF))
        total = state_ref[rows, :].astype(f32) + mm(mixed_ref[rows, :], wout_ref[...])
        out_ref[place[0], place[1], :] = total.astype(bf16).reshape(BLOCK, HALF, chans)
        back_ref[place[0], place[1], :] = gback_ref[rows, :].reshape(BLOCK, HALF, chans)


def unpack_body(geo, back_ref, slot_ref, out_hbm, out_ref, sems):
    slots, feats = out_ref.shape
    rows = join_slots(geo, back_ref, feats)[1]
    step = slots // GROUPS
    copies = []
    for n in range(GROUPS):
        part = slice(n * step, (n + 1) * step)
        spread = one_hot(iota((geo.total, step), 0) == slot_ref[:, part])
        out_ref[part, :] = mm(spread, rows, 0, 0).astype(bf16)
        copies.append(start_copy(out_ref.at[part], out_hbm.at[part], sems.at[n]))
    for copy in copies:
        copy.wait()


def shards(
    background, obs_rows, obs_pixel, obs_count, block_pattern, w_enc, w_qkv, w_out, cotangent
):
    lat_rows, lon_cols, chans = background.shape
    pixels = lat_rows * lon_cols
    slots, feats = obs_rows.shape
    lon_devs = lax.axis_size("lon")
    geo = Geometry(slots, lax.axis_size("lat") * lon_devs, lon_devs, lon_cols)
    side = pixels // 2
    half = feats // 2
    up = [(i, (i + 1) % lon_devs) for i in range(lon_devs)]
    down = [(j, i) for i, j in up]

    rim = (lat_rows + 1, HALF, chans)
    wide, edge = (pixels, chans), (side, chans)
    weights_own = (2, HEADS, 2 * TILE, 2 * TILE)
    weights_far = (4, chans // SLAB, TILE, 2 * TILE)
    dma = pltpu.SemaphoreType.DMA
    pattern = pltpu.SMEM(block_pattern.shape, i32)

    def vmem(*shapes):
        return [pltpu.VMEM(shape, bf16) for shape in shapes]

    payload, slot, cot_east, cot_west = call(
        functools.partial(pack_body, geo),
        [((geo.devs, geo.rows, half), bf16), ((1, slots), i32), (rim, bf16), (rim, bf16)],
        scratch=[pltpu.VMEM((1, slots), i32), pltpu.VMEM((slots, feats), bf16), pattern]
        + vmem((geo.devs, geo.rows, half), rim, rim)
        + [dma((7 + GROUPS,))],
        n_in=5,
        n_smem=(1,),
        n_hbm=(0, 2, 3, 4),
        out_hbm=(0, 2, 3),
        flops=400 << 20,
    )(obs_pixel.reshape(1, slots), obs_count, obs_rows, block_pattern, cotangent)
    west_cot = lax.ppermute(cot_east, "lon", up)
    east_cot = lax.ppermute(cot_west, "lon", down)
    arrived = lax.all_to_all(payload, ("lat", "lon"), split_axis=0, concat_axis=0, tiled=True)
    gm, gw, ge, bias_w, bias_e = call(
        grad_body,
        [
            (wide, bf16),
            (edge, bf16),
            (edge, bf16),
            ((side, TILE), f32),
            ((side, TILE), f32),
        ],
        scratch=vmem((lat_rows, lon_cols, chans), (chans, chans))
        + vmem(wide, edge, edge)
        + [pltpu.VMEM((side, TILE), f32)] * 2
        + [dma((2,)), dma((5,))],
        n_in=4,
        n_hbm=(0, 3),
        out_hbm=range(5),
        flops=GRAD_COST,
    )(cotangent, west_cot, east_cot, w_out)
    state, normed, n0, n1, inverse, inv_rms, oht = call(
        functools.partial(state_body, geo),
        [
            (wide, bf16),
            (wide, bf16),
            (edge, bf16),
            (edge, bf16),
            ((pixels, 128), f32),
            ((pixels, 128), f32),
            ((geo.total, pixels), bf16),
        ],
        n_in=3,
        flops=1 << 30,
    )(arrived, w_enc, background)
    n_west = lax.ppermute(n1, "lon", up)
    n_east = lax.ppermute(n0, "lon", down)
    q, k, v, dq, dk, dv, slope, weight, v_far, state_far = call(
        functools.partial(own_body, geo),
        [(wide, bf16)] * 3
        + [(wide, f32)] * 3
        + [((geo.total, chans), f32), (weights_own, bf16), (wide, bf16), (wide, bf16)],
        scratch=[pattern] + vmem(weights_own) + [dma((3 + HEADS,))],
        n_in=7,
        n_hbm=(3,),
        out_hbm=(7, 8, 9),
        flops=4 << 30,
    )(normed, w_qkv, gm, block_pattern, arrived, w_enc, state)
    rim_v, far, gback, reply = call(
        functools.partial(rim_body, geo),
        [(wide, bf16), (weights_far, bf16), (wide, bf16), ((geo.devs, geo.rows, half), bf16)],
        scratch=[pattern]
        + vmem(wide, wide, wide, weights_far, wide, wide, (pixels, 3 * chans), (geo.devs, geo.rows, half))
        + [pltpu.VMEM((geo.devs, geo.tail, half), f32), dma((4 + GROUPS,))],
        n_in=22,
        n_hbm=(11,),
        out_hbm=(0, 1, 2, 3),
        flops=4 << 30,
    )(
        n_west, n_east, w_qkv, q, k, v, gm, gw, ge, bias_w, bias_e, block_pattern,
        dq, dk, dv, state, inv_rms, cotangent, inverse, oht, slope, w_enc,
    )
    returned = lax.all_to_all(reply, ("lat", "lon"), split_axis=0, concat_axis=0, tiled=True)
    updated, grad_background = call(
        out_body,
        [((lat_rows, lon_cols, chans), bf16), ((lat_rows, lon_cols, chans), bf16)],
        scratch=vmem(weights_own, weights_far, wide, wide, (chans, chans), wide, wide, wide)
        + [dma((7,))],
        n_in=7,
        n_hbm=range(7),
        flops=1 << 30,
    )(weight, far, v_far, rim_v, w_out, state_far, gback)
    (grad_obs,) = call(
        functools.partial(unpack_body, geo),
        [((slots, feats), bf16)],
        scratch=vmem((slots, feats)) + [dma((GROUPS,))],
        n_in=2,
        out_hbm=(0,),
        flops=1 << 28,
    )(returned, slot)
    return (updated, grad_background, grad_obs)


def solution(mesh):
    return jax.shard_map(
        shards,
        mesh=mesh,
        in_specs=(
            P("lat", "lon", None),
            P(("lat", "lon"), None),
            P(("lat", "lon")),
            P(("lat", "lon")),
            P("lat", "lon", None),
            P(),
            P(),
            P(),
            P("lat", "lon", None),
        ),
        out_specs=(P("lat", "lon", None), P("lat", "lon", None), P(("lat", "lon"), None)),
        check_vma=False,
    )
```

```python
import functools
import math

import jax
import jax.numpy as jnp
from jax import lax
from jax.experimental import pallas as pl
from jax.experimental.pallas import tpu as pltpu
from jax.sharding import PartitionSpec as P

HEADS = 8
BLOCK = 8
HALF = 2 * BLOCK
TILE = BLOCK * HALF
SLAB = 128
MASKED = -1e30
GRAD_COST = 1 << 37
GROUPS = 4
BATCH = 4
ORDER = {1: (0,), 2: (1, 0), 3: (1, 0, 2)}
STRIP = 32

norm_eps = 1e-06
gelu_coef = 0.7978845608028654

bf16 = jnp.bfloat16
f32 = jnp.float32
i32 = jnp.int32


def iota(shape, dim):
    return lax.broadcasted_iota(i32, shape, dim)


def mm(lhs, rhs, lhs_dim=1, rhs_dim=0):
    return lax.dot_general(
        lhs, rhs, (((lhs_dim,), (rhs_dim,)), ((), ())), preferred_element_type=f32
    )


def one_hot(cond):
    return jnp.where(cond, 1.0, 0.0).astype(bf16)


def gelu_parts(inputs):
    square = inputs * inputs
    tangent = jnp.tanh(gelu_coef * inputs * (1.0 + 0.044715 * square))
    return square, tangent


def call(
    body, outs, scratch=(), flops=0, n_smem=(), n_hbm=(), out_hbm=(), n_in=0, size=1 << 20, vmem=16
):
    def spec(k, smem, hbm):
        if k in hbm:
            return pl.BlockSpec(memory_space=pltpu.HBM)
        return pl.BlockSpec(memory_space=pltpu.SMEM if k in smem else pltpu.VMEM)

    kernel = pl.pallas_call(
        body,
        out_shape=[
            pltpu.HBM(s, d) if k in out_hbm else jax.ShapeDtypeStruct(s, d)
            for k, (s, d) in enumerate(outs)
        ],
        in_specs=[spec(k, n_smem, n_hbm) for k in range(n_in)],
        out_specs=[spec(k, (), out_hbm) for k in range(len(outs))],
        scratch_shapes=list(scratch),
        compiler_params=pltpu.CompilerParams(vmem_limit_bytes=vmem << 20),
        cost_estimate=pl.CostEstimate(flops=flops, bytes_accessed=size, transcendentals=0),
    )

    def run(*args):
        return kernel(
            *[
                pltpu.with_memory_space_constraint(x, pltpu.HBM) if k in n_hbm else x
                for k, x in enumerate(args)
            ]
        )

    return run


def chunk(ref, row_block, half):
    part = ref[
        row_block * BLOCK : (row_block + 1) * BLOCK, half * HALF : (half + 1) * HALF, :
    ]
    return part.reshape(TILE, part.shape[-1])


def halves():
    return [(i, u) for i in range(2) for u in range(2)]


def rows_of(i, u):
    return slice((i * 2 + u) * TILE, (i * 2 + u + 1) * TILE)


def key_count(pat, i, b):
    return 1 + pat[i, b, 0] + pat[i, b, 1] + pat[i, b, 2] + pat[i, b, 3]


def mask_value(pat, i, b, shift):
    if abs(shift) > 2:
        return jnp.int32(0)
    if shift == 0:
        return jnp.int32(1)
    return pat[i, b, shift + 2 if shift < 0 else shift + 1]


def half_bias(count):
    bias = jnp.float32(-0.5 * math.log(64.0))
    for n in range(2, 6):
        bias = jnp.where(count == n, jnp.float32(-0.5 * math.log(64.0 * n)), bias)
    return bias


def own_bias(pat, i, u, turn):
    second_q = iota((TILE, TILE), 0) % HALF >= BLOCK
    second_k = iota((TILE, TILE), 1) % HALF >= BLOCK
    parts = []
    for qb in range(2):
        bias = half_bias(key_count(pat, i, 2 * u + qb))
        pair = [
            jnp.where(mask_value(pat, i, 2 * u + qb, 2 * turn + kb - qb) > 0, bias, MASKED)
            for kb in range(2)
        ]
        parts.append(jnp.where(second_k, pair[1], pair[0]))
    return jnp.where(second_q, parts[1], parts[0])


def start_copy(src, dst, sem):
    copy = pltpu.make_async_copy(src, dst, sem)
    copy.start()
    return copy


def halo_rows(pat_ref, u, turn, width):
    lane = iota((HALF, width), 1)
    line = iota((HALF, width), 0)
    second_k = lane % HALF >= BLOCK
    extra = jnp.zeros((HALF, width), f32)
    for i in range(2):
        for qb in range(2):
            pair = [
                mask_value(pat_ref, i, 2 * u + qb, 2 * turn + kb - qb).astype(f32)
                for kb in range(2)
            ]
            mask = jnp.where(second_k, pair[1], pair[0])
            count = key_count(pat_ref, i, 2 * u + qb).astype(f32)
            here = (line == i) & (lane >= qb * TILE) & (lane < (qb + 1) * TILE)
            there = (line == i) & (lane >= (qb + 2) * TILE) & (lane < (qb + 3) * TILE)
            extra = jnp.where(here, mask, jnp.where(there, count, extra))
    return extra.astype(bf16)


def pipeline(items, stages, extra=None):
    states = [None] * len(items)
    extra = extra or {}
    for step in range(max([len(items) + len(stages) - 1] + [n + 1 for n in extra])):
        for lag in ORDER[len(stages)]:
            stage = stages[lag]
            n = step - lag
            if 0 <= n < len(items):
                states[n] = stage(items[n], states[n])
        for task in extra.get(step, ()):
            task()


def batch(items, stages, size):
    groups = [items[n : n + size] for n in range(0, len(items), size)]

    def lift(stage):
        return lambda group, states: [
            stage(item, state) for item, state in zip(group, states or [None] * len(group))
        ]

    return groups, tuple(lift(stage) for stage in stages)


class Geometry:
    def __init__(self, slots, devs, lon_devs, lon_cols):
        self.devs, self.lon_devs = devs, lon_devs
        self.cap = (slots + devs - 1) // devs + 2
        self.full = self.cap // 8 * 8
        self.rest = self.cap - self.full
        self.shift = 4 if self.rest <= 3 else 8
        self.tail = 2 * self.shift
        self.mark = self.shift - 1
        self.rows = 2 * self.full + self.tail
        self.bulk = devs * self.full
        self.total = self.bulk + devs * self.rest
        self.lon_bits = (lon_cols * lon_devs).bit_length() - 1


def tail_picks(geo, offset):
    shape = (geo.devs, geo.devs * geo.tail)
    base = iota(shape, 1) - iota(shape, 0) * geo.tail
    return jnp.concatenate([one_hot(base == offset + r) for r in range(geo.rest)], axis=0)


def join_slots(geo, ref, feats):
    half = feats // 2
    tail = ref[:, 2 * geo.full : geo.rows, :].reshape(geo.devs * geo.tail, half)
    parts = []
    if geo.full:
        first = ref[:, 0 : geo.full, :].reshape(geo.bulk, half)
        second = ref[:, geo.full : 2 * geo.full, :].reshape(geo.bulk, half)
        parts.append(jnp.concatenate([first, second], axis=1))
    if geo.rest:
        rows = [mm(tail_picks(geo, n * geo.shift), tail) for n in range(2)]
        parts.append(jnp.concatenate(rows, axis=1).astype(bf16))
    return tail, jnp.concatenate(parts, axis=0)


def send_groups(geo, ref, hbm, sems, base, stages):
    copies = []
    if not geo.full:
        copies.append(start_copy(ref, hbm, sems.at[base]))
        return copies
    step = geo.devs // GROUPS

    def store(item, values):
        n, lo, hi = item
        half = values.shape[1] // 2
        values = values.astype(bf16)
        ref[lo:hi, 0 : geo.full, :] = values[:, 0:half].reshape(hi - lo, geo.full, half)
        ref[lo:hi, geo.full : 2 * geo.full, :] = values[:, half:].reshape(hi - lo, geo.full, half)
        copies.append(start_copy(ref.at[lo:hi], hbm.at[lo:hi], sems.at[base + n]))

    pipeline([(n, n * step, (n + 1) * step) for n in range(GROUPS)], tuple(stages) + (store,))
    return copies


def slot_index(geo, owner, rank, live):
    place = jnp.where(
        rank < geo.full,
        owner * geo.full + rank,
        geo.bulk + (rank - geo.full) * geo.devs + owner,
    )
    return jnp.where(live, place, -1)


def pack_body(
    geo, pix_hbm, cnt_ref, rows_hbm, pat_hbm, cot_hbm,
    pay_hbm, slot_ref, east_hbm, west_hbm,
    pix_ref, rows_ref, pat_ref, pay_ref, east_ref, west_ref, sems,
):
    pix_copy = start_copy(pix_hbm, pix_ref, sems.at[0])
    rows_copy = start_copy(rows_hbm, rows_ref, sems.at[1])
    pat_copy = start_copy(pat_hbm, pat_ref, sems.at[2])
    lats = cot_hbm.shape[0]
    sides = ((east_ref, 1, 1), (west_ref, 0, -1))
    cot_copies = [
        start_copy(cot_hbm.at[:, u * HALF : (u + 1) * HALF, :], ref.at[0:lats], sems.at[3 + u])
        for ref, u, _ in sides
    ]
    slots = pix_ref.shape[1]
    upper = one_hot(iota((slots, slots), 0) <= iota((slots, slots), 1))
    pix_copy.wait()
    pix = pix_ref[...]
    lat = lax.shift_right_logical(pix, geo.lon_bits)
    lon = lax.bitwise_and(pix, (1 << geo.lon_bits) - 1)
    owner = lax.shift_right_logical(lat, 4) * geo.lon_devs + lax.shift_right_logical(lon, 5)
    row = lax.bitwise_and(lat, 15)
    col = lax.bitwise_and(lon, 31)
    code = (
        lax.shift_right_logical(row, 3) * (2 * TILE)
        + lax.shift_right_logical(col, 4) * TILE
        + lax.bitwise_and(row, 7) * HALF
        + lax.bitwise_and(col, 15)
        + 1
    )
    live = iota((1, slots), 1) < cnt_ref[0]
    table = (iota((geo.devs, slots), 0) == owner) & live
    table_f = jnp.where(table, 1.0, 0.0)
    table_b = table_f.astype(bf16)
    running = mm(table_b, upper)
    rank = (jnp.sum(running * table_f, axis=0, keepdims=True) - 1.0).astype(i32)
    slot = slot_index(geo, owner, rank, live)
    slot_ref[...] = slot
    high = lax.shift_right_logical(code, 5).astype(f32)
    low = lax.bitwise_and(code, 31).astype(f32)
    place = iota((128, slots), 0)
    codes = jnp.where(place == rank, high, 0.0) + jnp.where(place == rank + 64, low, 0.0)
    meta = mm(table_b, codes.astype(bf16), 1, 1)
    tails = geo.devs * geo.tail
    lift = one_hot(
        iota((tails, geo.devs), 0) == iota((tails, geo.devs), 1) * geo.tail + geo.mark
    )
    lifted = mm(lift, meta.astype(bf16))
    pat_copy.wait()
    for copy, (ref, u, turn) in zip(cot_copies, sides):
        ref[lats] = halo_rows(pat_ref, u, turn, cot_hbm.shape[2])
        copy.wait()
    outs = [
        start_copy(east_ref, east_hbm, sems.at[5]),
        start_copy(west_ref, west_hbm, sems.at[6]),
    ]
    place = iota((tails, slots), 0)
    line = jnp.where(live & (rank >= geo.full), owner * geo.tail + rank - geo.full, -geo.tail)
    first = one_hot(place == line)
    second = one_hot(place == line + geo.shift)
    rows_copy.wait()
    half = rows_ref.shape[1] // 2
    tail = mm(first, rows_ref[:, 0:half]) + mm(second, rows_ref[:, half:]) + lifted
    pay_ref[:, 2 * geo.full : geo.rows, :] = tail.astype(bf16).reshape(geo.devs, geo.tail, half)

    def spread(item, _):
        base = item[1] * geo.full
        hot = one_hot(iota(((item[2] - item[1]) * geo.full, slots), 0) + base == slot)
        return mm(hot, rows_ref[...])

    outs += send_groups(geo, pay_ref, pay_hbm, sems, 7, (spread,))
    for copy in outs:
        copy.wait()


def grad_body(
    cot_hbm, west_ref, east_ref, wout_hbm,
    gm_hbm, gw_hbm, ge_hbm, bw_hbm, be_hbm,
    cot_ref, wout_ref,
    gm_ref, gw_ref, ge_ref, bw_ref, be_ref, in_sems, out_sems,
):
    wout_copy = start_copy(wout_hbm, wout_ref, in_sems.at[0])
    cot_copy = start_copy(cot_hbm, cot_ref, in_sems.at[1])
    wout_copy.wait()
    cot_copy.wait()
    wout = wout_ref[...]
    for i, u in halves():
        part = mm(chunk(cot_ref, i, u), wout, 1, 1)
        gm_ref[rows_of(i, u), :] = part.astype(bf16)
    outs = [start_copy(gm_ref, gm_hbm, out_sems.at[0])]
    second_q = iota((TILE, TILE), 0) % HALF >= BLOCK
    for n, (src, dst, bias_ref, dst_hbm, bias_hbm) in enumerate(
        (
            (west_ref, gw_ref, bw_ref, gw_hbm, bw_hbm),
            (east_ref, ge_ref, be_ref, ge_hbm, be_hbm),
        )
    ):
        rows = src.shape[0] - 1
        part = mm(src[0:rows].reshape(2 * TILE, wout.shape[0]), wout, 1, 1)
        dst[...] = part.astype(bf16)
        extra = src[rows].astype(f32)
        for i in range(2):
            line = extra[i : i + 1, :]
            mask = jnp.where(second_q, line[:, TILE : 2 * TILE], line[:, 0:TILE])
            count = jnp.where(second_q, line[:, 3 * TILE : 4 * TILE], line[:, 2 * TILE : 3 * TILE])
            bias = -0.5 * jnp.log(count * 64.0)
            bias_ref[i * TILE : (i + 1) * TILE, :] = jnp.where(mask > 0.5, bias, MASKED)
        outs += [
            start_copy(dst, dst_hbm, out_sems.at[1 + 2 * n]),
            start_copy(bias_ref, bias_hbm, out_sems.at[2 + 2 * n]),
        ]
    for copy in outs:
        copy.wait()


def slot_table(geo, tails, pixels):
    pick = one_hot(
        iota((geo.devs, geo.devs * geo.tail), 1) == iota((geo.devs, geo.devs * geo.tail), 0) * geo.tail + geo.mark
    )
    meta = mm(pick, tails).astype(bf16)
    codes = []
    if geo.full:
        shape = (geo.devs, geo.full, geo.devs)
        owner = one_hot(iota(shape, 0) == iota(shape, 2)).reshape(geo.bulk, geo.devs)
        place = iota((geo.devs, geo.full, 128), 1).reshape(geo.bulk, 128)
        lane = iota((geo.bulk, 128), 1)
        scale = jnp.where(lane == place, 32.0, 0.0) + jnp.where(lane == place + 64, 1.0, 0.0)
        codes.append(jnp.sum(mm(owner, meta) * scale, axis=1, keepdims=True))
    spare = meta.astype(f32)
    for r in range(geo.full, geo.cap):
        codes.append(spare[:, r : r + 1] * 32.0 + spare[:, 64 + r : 65 + r])
    code = jnp.concatenate(codes, axis=0).astype(i32)
    return one_hot(code == iota((geo.total, pixels), 1) + 1)


def state_body(geo, arr_ref, wenc_ref, bg_ref, state_ref, n_ref, n0_ref, n1_ref, inv_ref, rms_ref, oht_ref):
    feats = wenc_ref.shape[0]
    tails, arr = join_slots(geo, arr_ref, feats)
    oht = slot_table(geo, tails, n_ref.shape[0])
    oht_ref[...] = oht
    pre = mm(arr, wenc_ref[...])
    _, tangent = gelu_parts(pre)
    encoded = (0.5 * pre * (1.0 + tangent)).astype(bf16)
    obs_sum = mm(oht, encoded, 0, 0)
    number = mm(oht, jnp.ones((geo.total, 128), bf16), 0, 0)
    inverse = 1.0 / (1.0 + number)
    inv_ref[...] = inverse
    for i, u in halves():
        rows = rows_of(i, u)
        fresh = obs_sum[rows] * inverse[rows, 0:1]
        state = (chunk(bg_ref, i, u).astype(f32) + fresh).astype(bf16)
        state_ref[rows, :] = state
        wide_state = state.astype(f32)
        inv_rms = lax.rsqrt(jnp.mean(wide_state * wide_state, axis=1, keepdims=True) + norm_eps)
        rms_ref[rows, :] = jnp.broadcast_to(inv_rms, (TILE, 128))
        normed = (wide_state * inv_rms).astype(bf16)
        n_ref[rows, :] = normed
        side = n1_ref if u else n0_ref
        side[i * TILE : (i + 1) * TILE, :] = normed


def head_lanes(shape, head, dim=1):
    return lax.shift_right_logical(iota(shape, dim), 6) == head


def split_heads(slab):
    return [jnp.where(head_lanes(slab.shape, h), slab, jnp.zeros((), slab.dtype)) for h in range(2)]


def across(lanes, width):
    return jnp.concatenate([lanes] * (width // lanes.shape[1]), axis=1)


def stack_heads(slab):
    return jnp.concatenate(split_heads(slab), axis=0)


def weigh(score, grad, bias):
    weight = jnp.tanh(score + bias) + 1.0
    slope = grad * weight * (2.0 - weight)
    return weight.astype(bf16), slope.astype(bf16)


def project(src, wqkv_ref, q_ref, k_ref, v_ref, rows):
    chans = src.shape[1]
    q_ref[rows, :] = (mm(src, wqkv_ref[:, 0:chans]) * 0.0625).astype(bf16)
    k_ref[rows, :] = mm(src, wqkv_ref[:, chans : 2 * chans]).astype(bf16)
    v_ref[rows, :] = mm(src, wqkv_ref[:, 2 * chans : 3 * chans]).astype(bf16)


def slab_lanes(s):
    return slice(s * SLAB, (s + 1) * SLAB)


def own_body(
    geo, n_ref, wqkv_ref, gm_ref, pat_hbm, arr_ref, wenc_ref, state_ref,
    q_ref, k_ref, v_ref, dq_ref, dk_ref, dv_ref, slope_ref, weight_hbm, v_hbm, state_hbm,
    pat_ref, weight_ref, sems,
):
    chans = n_ref.shape[1]
    pat_copy = start_copy(pat_hbm, pat_ref, sems.at[0])
    state_copy = start_copy(state_ref, state_hbm, sems.at[1])
    project(n_ref[...], wqkv_ref, q_ref, k_ref, v_ref, slice(0, n_ref.shape[0]))
    v_copy = start_copy(v_ref, v_hbm, sems.at[2])
    pat_copy.wait()
    biases = []
    for i in range(2):
        bias = [
            jnp.concatenate([own_bias(pat_ref, i, u, -u), own_bias(pat_ref, i, u, 1 - u)], axis=1)
            for u in range(2)
        ]
        biases.append(jnp.concatenate(bias, axis=0))

    def first(item, _):
        i, s, h = item
        keys, lanes = slice(i * 2 * TILE, (i + 1) * 2 * TILE), slab_lanes(s)
        km = split_heads(k_ref[keys, lanes])[h]
        vm = split_heads(v_ref[keys, lanes])[h]
        return km, mm(q_ref[keys, lanes], km, 1, 1), mm(gm_ref[keys, lanes], vm, 1, 1)

    def second(item, state):
        i, s, h = item
        km, score, grad = state
        weight, slope = weigh(score, grad, biases[i])
        weight_ref[i, 2 * s + h] = weight
        return km, weight, slope

    held, weight_copies = {}, []

    def third(item, state):
        i, s, h = item
        keys, lanes = slice(i * 2 * TILE, (i + 1) * 2 * TILE), slab_lanes(s)
        km, weight, slope = state
        parts = (
            mm(slope, km),
            mm(slope, q_ref[keys, lanes], 0, 0),
            mm(weight, gm_ref[keys, lanes], 0, 0),
        )
        if h == 0:
            held[i, s] = parts
            return
        before = held.pop((i, s))
        lower = iota((2 * TILE, SLAB), 1) < SLAB // 2
        dq_ref[keys, lanes] = before[0] + parts[0]
        dk_ref[keys, lanes] = jnp.where(lower, before[1], parts[1])
        dv_ref[keys, lanes] = jnp.where(lower, before[2], parts[2])
        pair = (i, slice(2 * s, 2 * s + 2))
        sem = sems.at[3 + i * (chans // SLAB) + s]
        weight_copies.append(start_copy(weight_ref.at[pair], weight_hbm.at[pair], sem))

    pipeline(
        [(i, s, h) for i in range(2) for s in range(chans // SLAB) for h in range(2)],
        (first, second, third),
    )
    arr = join_slots(geo, arr_ref, wenc_ref.shape[0])[1]
    pre = mm(arr, wenc_ref[...])
    square, tangent = gelu_parts(pre)
    slope_ref[...] = 0.5 * (1.0 + tangent) + 0.5 * pre * (1.0 - tangent * tangent) * gelu_coef * (
        1.0 + 3.0 * 0.044715 * square
    )
    for copy in [state_copy, v_copy] + weight_copies:
        copy.wait()


def rim_body(
    geo, nw_ref, ne_ref, wqkv_ref, q_ref, k_ref, v_ref, gm_ref, gw_ref, ge_ref,
    bw_ref, be_ref, pat_hbm, dq_ref, dk_ref, dv_ref, state_ref, rms_ref, cot_ref, inv_ref,
    oht_ref, slope_ref, wenc_ref,
    v_hbm, weight_hbm, gback_hbm, reply_hbm,
    pat_ref, rim_q, rim_k, rim_v, weight_ref, gback_ref, scaled_ref, grad_ref, reply_ref, tail_ref, sems,
):
    chans = q_ref.shape[1]
    pat_copy = start_copy(pat_hbm, pat_ref, sems.at[0])
    far_rows = [slice(side * 2 * TILE, (side + 1) * 2 * TILE) for side in range(2)]
    project(nw_ref[...], wqkv_ref, rim_q, rim_k, rim_v, far_rows[0])
    pat_copy.wait()
    out_bias, in_bias = {}, {}
    for i in range(2):
        for side, bias_ref in enumerate((bw_ref, be_ref)):
            bias = own_bias(pat_ref, i, side, 2 * side - 1)
            out_bias[i, side] = jnp.concatenate([bias, bias], axis=1)
            bias = bias_ref[i * TILE : (i + 1) * TILE, :]
            in_bias[i, side] = jnp.concatenate([bias, bias], axis=1)

    def where(item):
        i, side, s = item
        far = slice((side * 2 + i) * TILE, (side * 2 + i + 1) * TILE)
        near = slice(i * TILE, (i + 1) * TILE)
        return rows_of(i, side), far, near, (gw_ref, ge_ref)[side], slab_lanes(s)

    def first(item, _):
        own, far, near, gh_ref, lanes = where(item)
        km = stack_heads(rim_k[far, lanes])
        return (
            km,
            mm(q_ref[own, lanes], km, 1, 1),
            mm(gm_ref[own, lanes], stack_heads(rim_v[far, lanes]), 1, 1),
            mm(rim_q[far, lanes], stack_heads(k_ref[own, lanes]), 1, 1),
            mm(gh_ref[near, lanes], stack_heads(v_ref[own, lanes]), 1, 1),
        )

    def second(item, state):
        i, side, s = item
        km, score_out, grad_out, score_in, grad_in = state
        weight, slope_out = weigh(score_out, grad_out, out_bias[i, side])
        weight_ref[i * 2 + side, s] = weight
        weight_in, slope_in = weigh(score_in, grad_in, in_bias[i, side])
        return km, slope_out, weight_in, slope_in

    def third(item, state):
        own, far, near, gh_ref, lanes = where(item)
        km, slope_out, weight_in, slope_in = state
        grad_q = mm(slope_out, km)
        grad_k = mm(slope_in, rim_q[far, lanes], 0, 0)
        grad_v = mm(weight_in, gh_ref[near, lanes], 0, 0)
        lower = iota((TILE, SLAB), 1) < SLAB // 2
        grad_k = jnp.where(lower, grad_k[0:TILE], grad_k[TILE:])
        grad_v = jnp.where(lower, grad_v[0:TILE], grad_v[TILE:])
        for n, total in enumerate(
            (
                (dq_ref[own, lanes] + grad_q) * 0.03125,
                (dk_ref[own, lanes] + grad_k) * 0.5,
                (dv_ref[own, lanes] + grad_v) * 0.5,
            )
        ):
            spot = slice(n * chans + lanes.start, n * chans + lanes.stop)
            grad_ref[own, spot] = total.astype(bf16)

    back = {}

    def project_back(group):
        back[group] = mm(grad_ref[rows_of(*group), :], wqkv_ref[...], 1, 1)

    def norm_back(item):
        i, u = item
        total = back.pop(item)
        cot = chunk(cot_ref, i, u)
        for n in range(0, TILE, STRIP):
            base = rows_of(i, u).start + n
            rows = slice(base, base + STRIP)
            inv_rms = across(rms_ref[rows, :], chans)
            normed = state_ref[rows, :].astype(f32) * inv_rms
            grad = total[n : n + STRIP]
            grad_state = cot[n : n + STRIP].astype(f32) + inv_rms * (
                grad - normed * jnp.mean(grad * normed, axis=1, keepdims=True)
            )
            gback_ref[rows, :] = grad_state.astype(bf16)
            scaled_ref[rows, :] = (grad_state * across(inv_ref[rows, :], chans)).astype(bf16)

    slabs = chans // SLAB
    groups = [(i, side) for side in range(2) for i in range(2)]
    extra = {
        1: [lambda: project(ne_ref[...], wqkv_ref, rim_q, rim_k, rim_v, far_rows[1])],
    }
    for n, group in enumerate(groups):
        ready = slabs * (n + 1) // BATCH + 1
        extra.setdefault(ready, []).append(functools.partial(project_back, group))
        extra.setdefault(ready + 1, []).append(functools.partial(norm_back, group))
    items = [(i, side, s) for i, side in groups for s in range(slabs)]
    pipeline(*batch(items, (first, second, third), BATCH), extra)
    v_copy = start_copy(rim_v, v_hbm, sems.at[1])
    weight_copy = start_copy(weight_ref, weight_hbm, sems.at[2])
    gback_copy = start_copy(gback_ref, gback_hbm, sems.at[3])

    def pre_grad(lo, hi):
        return (mm(oht_ref[lo:hi, :], scaled_ref[...]) * slope_ref[lo:hi, :]).astype(bf16)

    half = wenc_ref.shape[0] // 2
    tail_ref[...] = jnp.zeros(tail_ref.shape, f32)
    if geo.rest:
        spare = mm(pre_grad(geo.bulk, geo.total), wenc_ref[...], 1, 1)
        for n in range(2):
            for r in range(geo.rest):
                part = spare[r * geo.devs : (r + 1) * geo.devs, n * half : (n + 1) * half]
                tail_ref[:, n * geo.shift + r, :] = part
    reply_ref[:, 2 * geo.full : geo.rows, :] = tail_ref[...].astype(bf16)
    replies = send_groups(
        geo, reply_ref, reply_hbm, sems, 4,
        (
            lambda item, _: pre_grad(item[1] * geo.full, item[2] * geo.full),
            lambda item, rows: mm(rows, wenc_ref[...], 1, 1),
        ),
    )
    for copy in [v_copy, weight_copy, gback_copy] + replies:
        copy.wait()


def out_body(*refs):
    hbm, (out_ref, back_ref), local, (mixed_ref, sems) = refs[:7], refs[7:9], refs[9:16], refs[16:]
    copies = [start_copy(src, dst, sems.at[n]) for n, (src, dst) in enumerate(zip(hbm, local))]
    for copy in copies:
        copy.wait()
    weight_ref, far_ref, v_ref, rim_v, wout_ref, state_ref, gback_ref = local
    chans = wout_ref.shape[0]
    for i in range(2):
        keys = slice(i * 2 * TILE, (i + 1) * 2 * TILE)
        for s in range(chans // SLAB):
            lanes = slice(s * SLAB, (s + 1) * SLAB)
            vm = split_heads(v_ref[keys, lanes])
            mixed = mm(weight_ref[i, 2 * s], vm[0]) + mm(weight_ref[i, 2 * s + 1], vm[1])
            for side in range(2):
                far = slice((side * 2 + i) * TILE, (side * 2 + i + 1) * TILE)
                total = mixed[side * TILE : (side + 1) * TILE] + mm(
                    far_ref[i * 2 + side, s], stack_heads(rim_v[far, lanes])
                )
                mixed_ref[rows_of(i, side), lanes] = (total * 0.5).astype(bf16)
    for i, u in halves():
        rows = rows_of(i, u)
        place = (slice(i * BLOCK, (i + 1) * BLOCK), slice(u * HALF, (u + 1) * HALF))
        total = state_ref[rows, :].astype(f32) + mm(mixed_ref[rows, :], wout_ref[...])
        out_ref[place[0], place[1], :] = total.astype(bf16).reshape(BLOCK, HALF, chans)
        back_ref[place[0], place[1], :] = gback_ref[rows, :].reshape(BLOCK, HALF, chans)


def unpack_body(geo, back_ref, slot_ref, out_hbm, out_ref, sems):
    slots, feats = out_ref.shape
    rows = join_slots(geo, back_ref, feats)[1]
    step = slots // GROUPS
    copies = []
    for n in range(GROUPS):
        part = slice(n * step, (n + 1) * step)
        spread = one_hot(iota((geo.total, step), 0) == slot_ref[:, part])
        out_ref[part, :] = mm(spread, rows, 0, 0).astype(bf16)
        copies.append(start_copy(out_ref.at[part], out_hbm.at[part], sems.at[n]))
    for copy in copies:
        copy.wait()


def shards(
    background, obs_rows, obs_pixel, obs_count, block_pattern, w_enc, w_qkv, w_out, cotangent
):
    lat_rows, lon_cols, chans = background.shape
    pixels = lat_rows * lon_cols
    slots, feats = obs_rows.shape
    lon_devs = lax.axis_size("lon")
    geo = Geometry(slots, lax.axis_size("lat") * lon_devs, lon_devs, lon_cols)
    side = pixels // 2
    half = feats // 2
    up = [(i, (i + 1) % lon_devs) for i in range(lon_devs)]
    down = [(j, i) for i, j in up]

    rim = (lat_rows + 1, HALF, chans)
    wide, edge = (pixels, chans), (side, chans)
    weights_own = (2, HEADS, 2 * TILE, 2 * TILE)
    weights_far = (4, chans // SLAB, TILE, 2 * TILE)
    dma = pltpu.SemaphoreType.DMA
    pattern = pltpu.SMEM(block_pattern.shape, i32)

    def vmem(*shapes):
        return [pltpu.VMEM(shape, bf16) for shape in shapes]

    payload, slot, cot_east, cot_west = call(
        functools.partial(pack_body, geo),
        [((geo.devs, geo.rows, half), bf16), ((1, slots), i32), (rim, bf16), (rim, bf16)],
        scratch=[pltpu.VMEM((1, slots), i32), pltpu.VMEM((slots, feats), bf16), pattern]
        + vmem((geo.devs, geo.rows, half), rim, rim)
        + [dma((7 + GROUPS,))],
        n_in=5,
        n_smem=(1,),
        n_hbm=(0, 2, 3, 4),
        out_hbm=(0, 2, 3),
        flops=400 << 20,
    )(obs_pixel.reshape(1, slots), obs_count, obs_rows, block_pattern, cotangent)
    west_cot = lax.ppermute(cot_east, "lon", up)
    east_cot = lax.ppermute(cot_west, "lon", down)
    arrived = lax.all_to_all(payload, ("lat", "lon"), split_axis=0, concat_axis=0, tiled=True)
    gm, gw, ge, bias_w, bias_e = call(
        grad_body,
        [
            (wide, bf16),
            (edge, bf16),
            (edge, bf16),
            ((side, TILE), f32),
            ((side, TILE), f32),
        ],
        scratch=vmem((lat_rows, lon_cols, chans), (chans, chans))
        + vmem(wide, edge, edge)
        + [pltpu.VMEM((side, TILE), f32)] * 2
        + [dma((2,)), dma((5,))],
        n_in=4,
        n_hbm=(0, 3),
        out_hbm=range(5),
        flops=GRAD_COST,
    )(cotangent, west_cot, east_cot, w_out)
    state, normed, n0, n1, inverse, inv_rms, oht = call(
        functools.partial(state_body, geo),
        [
            (wide, bf16),
            (wide, bf16),
            (edge, bf16),
            (edge, bf16),
            ((pixels, 128), f32),
            ((pixels, 128), f32),
            ((geo.total, pixels), bf16),
        ],
        n_in=3,
        flops=1 << 30,
    )(arrived, w_enc, background)
    n_west = lax.ppermute(n1, "lon", up)
    n_east = lax.ppermute(n0, "lon", down)
    q, k, v, dq, dk, dv, slope, weight, v_far, state_far = call(
        functools.partial(own_body, geo),
        [(wide, bf16)] * 3
        + [(wide, f32)] * 3
        + [((geo.total, chans), f32), (weights_own, bf16), (wide, bf16), (wide, bf16)],
        scratch=[pattern] + vmem(weights_own) + [dma((3 + HEADS,))],
        n_in=7,
        n_hbm=(3,),
        out_hbm=(7, 8, 9),
        flops=4 << 30,
    )(normed, w_qkv, gm, block_pattern, arrived, w_enc, state)
    rim_v, far, gback, reply = call(
        functools.partial(rim_body, geo),
        [(wide, bf16), (weights_far, bf16), (wide, bf16), ((geo.devs, geo.rows, half), bf16)],
        scratch=[pattern]
        + vmem(wide, wide, wide, weights_far, wide, wide, (pixels, 3 * chans), (geo.devs, geo.rows, half))
        + [pltpu.VMEM((geo.devs, geo.tail, half), f32), dma((4 + GROUPS,))],
        n_in=22,
        n_hbm=(11,),
        out_hbm=(0, 1, 2, 3),
        flops=4 << 30,
    )(
        n_west, n_east, w_qkv, q, k, v, gm, gw, ge, bias_w, bias_e, block_pattern,
        dq, dk, dv, state, inv_rms, cotangent, inverse, oht, slope, w_enc,
    )
    returned = lax.all_to_all(reply, ("lat", "lon"), split_axis=0, concat_axis=0, tiled=True)
    updated, grad_background = call(
        out_body,
        [((lat_rows, lon_cols, chans), bf16), ((lat_rows, lon_cols, chans), bf16)],
        scratch=vmem(weights_own, weights_far, wide, wide, (chans, chans), wide, wide, wide)
        + [dma((7,))],
        n_in=7,
        n_hbm=range(7),
        flops=1 << 30,
    )(weight, far, v_far, rim_v, w_out, state_far, gback)
    (grad_obs,) = call(
        functools.partial(unpack_body, geo),
        [((slots, feats), bf16)],
        scratch=vmem((slots, feats)) + [dma((GROUPS,))],
        n_in=2,
        out_hbm=(0,),
        flops=1 << 28,
    )(returned, slot)
    return (updated, grad_background, grad_obs)


def solution(mesh):
    return jax.shard_map(
        shards,
        mesh=mesh,
        in_specs=(
            P("lat", "lon", None),
            P(("lat", "lon"), None),
            P(("lat", "lon")),
            P(("lat", "lon")),
            P("lat", "lon", None),
            P(),
            P(),
            P(),
            P("lat", "lon", None),
        ),
        out_specs=(P("lat", "lon", None), P("lat", "lon", None), P(("lat", "lon"), None)),
        check_vma=False,
    )
```

```python
import functools
import math

import jax
import jax.numpy as jnp
from jax import lax
from jax.experimental import pallas as pl
from jax.experimental.pallas import tpu as pltpu
from jax.sharding import PartitionSpec as P

HEADS = 8
BLOCK = 8
HALF = 2 * BLOCK
TILE = BLOCK * HALF
SLAB = 128
MASKED = -1e30
GRAD_COST = 1 << 37
GROUPS = 4
BATCH = 4
STRIP = 32

norm_eps = 1e-06
gelu_coef = 0.7978845608028654

bf16 = jnp.bfloat16
f32 = jnp.float32
i32 = jnp.int32


def iota(shape, dim):
    return lax.broadcasted_iota(i32, shape, dim)


def mm(lhs, rhs, lhs_dim=1, rhs_dim=0):
    return lax.dot_general(
        lhs, rhs, (((lhs_dim,), (rhs_dim,)), ((), ())), preferred_element_type=f32
    )


def one_hot(cond):
    return jnp.where(cond, 1.0, 0.0).astype(bf16)


def gelu_parts(inputs):
    square = inputs * inputs
    tangent = jnp.tanh(gelu_coef * inputs * (1.0 + 0.044715 * square))
    return square, tangent


def call(
    body, outs, scratch=(), flops=0, n_smem=(), n_hbm=(), out_hbm=(), n_in=0, size=1 << 20, vmem=16
):
    def spec(k, smem, hbm):
        if k in hbm:
            return pl.BlockSpec(memory_space=pltpu.HBM)
        return pl.BlockSpec(memory_space=pltpu.SMEM if k in smem else pltpu.VMEM)

    kernel = pl.pallas_call(
        body,
        out_shape=[
            pltpu.HBM(s, d) if k in out_hbm else jax.ShapeDtypeStruct(s, d)
            for k, (s, d) in enumerate(outs)
        ],
        in_specs=[spec(k, n_smem, n_hbm) for k in range(n_in)],
        out_specs=[spec(k, (), out_hbm) for k in range(len(outs))],
        scratch_shapes=list(scratch),
        compiler_params=pltpu.CompilerParams(vmem_limit_bytes=vmem << 20),
        cost_estimate=pl.CostEstimate(flops=flops, bytes_accessed=size, transcendentals=0),
    )

    def run(*args):
        return kernel(
            *[
                pltpu.with_memory_space_constraint(x, pltpu.HBM) if k in n_hbm else x
                for k, x in enumerate(args)
            ]
        )

    return run


def chunk(ref, row_block, half):
    part = ref[
        row_block * BLOCK : (row_block + 1) * BLOCK, half * HALF : (half + 1) * HALF, :
    ]
    return part.reshape(TILE, part.shape[-1])


def halves():
    return [(i, u) for i in range(2) for u in range(2)]


def rows_of(i, u):
    return slice((i * 2 + u) * TILE, (i * 2 + u + 1) * TILE)


def key_count(pat, i, b):
    return 1 + pat[i, b, 0] + pat[i, b, 1] + pat[i, b, 2] + pat[i, b, 3]


def mask_value(pat, i, b, shift):
    if abs(shift) > 2:
        return jnp.int32(0)
    if shift == 0:
        return jnp.int32(1)
    return pat[i, b, shift + 2 if shift < 0 else shift + 1]


def half_bias(count):
    bias = jnp.float32(-0.5 * math.log(64.0))
    for n in range(2, 6):
        bias = jnp.where(count == n, jnp.float32(-0.5 * math.log(64.0 * n)), bias)
    return bias


def own_bias(pat, i, u, turn):
    second_q = iota((TILE, TILE), 0) % HALF >= BLOCK
    second_k = iota((TILE, TILE), 1) % HALF >= BLOCK
    parts = []
    for qb in range(2):
        bias = half_bias(key_count(pat, i, 2 * u + qb))
        pair = [
            jnp.where(mask_value(pat, i, 2 * u + qb, 2 * turn + kb - qb) > 0, bias, MASKED)
            for kb in range(2)
        ]
        parts.append(jnp.where(second_k, pair[1], pair[0]))
    return jnp.where(second_q, parts[1], parts[0])


def start_copy(src, dst, sem):
    copy = pltpu.make_async_copy(src, dst, sem)
    copy.start()
    return copy


def halo_rows(pat_ref, u, turn, width):
    lane = iota((HALF, width), 1)
    line = iota((HALF, width), 0)
    second_k = lane % HALF >= BLOCK
    extra = jnp.zeros((HALF, width), f32)
    for i in range(2):
        for qb in range(2):
            pair = [
                mask_value(pat_ref, i, 2 * u + qb, 2 * turn + kb - qb).astype(f32)
                for kb in range(2)
            ]
            mask = jnp.where(second_k, pair[1], pair[0])
            count = key_count(pat_ref, i, 2 * u + qb).astype(f32)
            here = (line == i) & (lane >= qb * TILE) & (lane < (qb + 1) * TILE)
            there = (line == i) & (lane >= (qb + 2) * TILE) & (lane < (qb + 3) * TILE)
            extra = jnp.where(here, mask, jnp.where(there, count, extra))
    return extra.astype(bf16)


def pipeline(items, stages, extra=None):
    states = [None] * len(items)
    extra = extra or {}
    for step in range(max([len(items) + len(stages) - 1] + [n + 1 for n in extra])):
        for lag, stage in enumerate(stages):
            n = step - lag
            if 0 <= n < len(items):
                states[n] = stage(items[n], states[n])
        for task in extra.get(step, ()):
            task()


def batch(items, stages, size):
    groups = [items[n : n + size] for n in range(0, len(items), size)]

    def lift(stage):
        return lambda group, states: [
            stage(item, state) for item, state in zip(group, states or [None] * len(group))
        ]

    return groups, tuple(lift(stage) for stage in stages)


class Geometry:
    def __init__(self, slots, devs, lon_devs, lon_cols):
        self.devs, self.lon_devs = devs, lon_devs
        self.cap = (slots + devs - 1) // devs + 2
        self.full = self.cap // 8 * 8
        self.rest = self.cap - self.full
        self.shift = 4 if self.rest <= 3 else 8
        self.tail = 2 * self.shift
        self.mark = self.shift - 1
        self.rows = 2 * self.full + self.tail
        self.bulk = devs * self.full
        self.total = self.bulk + devs * self.rest
        self.lon_bits = (lon_cols * lon_devs).bit_length() - 1


def tail_picks(geo, offset):
    shape = (geo.devs, geo.devs * geo.tail)
    base = iota(shape, 1) - iota(shape, 0) * geo.tail
    return jnp.concatenate([one_hot(base == offset + r) for r in range(geo.rest)], axis=0)


def join_slots(geo, ref, feats):
    half = feats // 2
    tail = ref[:, 2 * geo.full : geo.rows, :].reshape(geo.devs * geo.tail, half)
    parts = []
    if geo.full:
        first = ref[:, 0 : geo.full, :].reshape(geo.bulk, half)
        second = ref[:, geo.full : 2 * geo.full, :].reshape(geo.bulk, half)
        parts.append(jnp.concatenate([first, second], axis=1))
    if geo.rest:
        rows = [mm(tail_picks(geo, n * geo.shift), tail) for n in range(2)]
        parts.append(jnp.concatenate(rows, axis=1).astype(bf16))
    return tail, jnp.concatenate(parts, axis=0)


def send_groups(geo, ref, hbm, sems, base, stages):
    copies = []
    if not geo.full:
        copies.append(start_copy(ref, hbm, sems.at[base]))
        return copies
    step = geo.devs // GROUPS

    def store(item, values):
        n, lo, hi = item
        half = values.shape[1] // 2
        values = values.astype(bf16)
        ref[lo:hi, 0 : geo.full, :] = values[:, 0:half].reshape(hi - lo, geo.full, half)
        ref[lo:hi, geo.full : 2 * geo.full, :] = values[:, half:].reshape(hi - lo, geo.full, half)
        copies.append(start_copy(ref.at[lo:hi], hbm.at[lo:hi], sems.at[base + n]))

    pipeline([(n, n * step, (n + 1) * step) for n in range(GROUPS)], tuple(stages) + (store,))
    return copies


def slot_index(geo, owner, rank, live):
    place = jnp.where(
        rank < geo.full,
        owner * geo.full + rank,
        geo.bulk + (rank - geo.full) * geo.devs + owner,
    )
    return jnp.where(live, place, -1)


def pack_body(
    geo, pix_hbm, cnt_ref, rows_hbm, pat_hbm, cot_hbm,
    pay_hbm, slot_ref, east_hbm, west_hbm,
    pix_ref, rows_ref, pat_ref, pay_ref, east_ref, west_ref, sems,
):
    pix_copy = start_copy(pix_hbm, pix_ref, sems.at[0])
    rows_copy = start_copy(rows_hbm, rows_ref, sems.at[1])
    pat_copy = start_copy(pat_hbm, pat_ref, sems.at[2])
    lats = cot_hbm.shape[0]
    sides = ((east_ref, 1, 1), (west_ref, 0, -1))
    cot_copies = [
        start_copy(cot_hbm.at[:, u * HALF : (u + 1) * HALF, :], ref.at[0:lats], sems.at[3 + u])
        for ref, u, _ in sides
    ]
    slots = pix_ref.shape[1]
    upper = one_hot(iota((slots, slots), 0) <= iota((slots, slots), 1))
    pix_copy.wait()
    pix = pix_ref[...]
    lat = lax.shift_right_logical(pix, geo.lon_bits)
    lon = lax.bitwise_and(pix, (1 << geo.lon_bits) - 1)
    owner = lax.shift_right_logical(lat, 4) * geo.lon_devs + lax.shift_right_logical(lon, 5)
    row = lax.bitwise_and(lat, 15)
    col = lax.bitwise_and(lon, 31)
    code = (
        lax.shift_right_logical(row, 3) * (2 * TILE)
        + lax.shift_right_logical(col, 4) * TILE
        + lax.bitwise_and(row, 7) * HALF
        + lax.bitwise_and(col, 15)
        + 1
    )
    live = iota((1, slots), 1) < cnt_ref[0]
    table = (iota((geo.devs, slots), 0) == owner) & live
    table_f = jnp.where(table, 1.0, 0.0)
    table_b = table_f.astype(bf16)
    running = mm(table_b, upper)
    rank = (jnp.sum(running * table_f, axis=0, keepdims=True) - 1.0).astype(i32)
    slot = slot_index(geo, owner, rank, live)
    slot_ref[...] = slot
    high = lax.shift_right_logical(code, 5).astype(f32)
    low = lax.bitwise_and(code, 31).astype(f32)
    place = iota((128, slots), 0)
    codes = jnp.where(place == rank, high, 0.0) + jnp.where(place == rank + 64, low, 0.0)
    meta = mm(table_b, codes.astype(bf16), 1, 1)
    tails = geo.devs * geo.tail
    lift = one_hot(
        iota((tails, geo.devs), 0) == iota((tails, geo.devs), 1) * geo.tail + geo.mark
    )
    lifted = mm(lift, meta.astype(bf16))
    pat_copy.wait()
    for copy, (ref, u, turn) in zip(cot_copies, sides):
        ref[lats] = halo_rows(pat_ref, u, turn, cot_hbm.shape[2])
        copy.wait()
    outs = [
        start_copy(east_ref, east_hbm, sems.at[5]),
        start_copy(west_ref, west_hbm, sems.at[6]),
    ]
    place = iota((tails, slots), 0)
    line = jnp.where(live & (rank >= geo.full), owner * geo.tail + rank - geo.full, -geo.tail)
    first = one_hot(place == line)
    second = one_hot(place == line + geo.shift)
    rows_copy.wait()
    half = rows_ref.shape[1] // 2
    tail = mm(first, rows_ref[:, 0:half]) + mm(second, rows_ref[:, half:]) + lifted
    pay_ref[:, 2 * geo.full : geo.rows, :] = tail.astype(bf16).reshape(geo.devs, geo.tail, half)

    def spread(item, _):
        base = item[1] * geo.full
        hot = one_hot(iota(((item[2] - item[1]) * geo.full, slots), 0) + base == slot)
        return mm(hot, rows_ref[...])

    outs += send_groups(geo, pay_ref, pay_hbm, sems, 7, (spread,))
    for copy in outs:
        copy.wait()


def grad_body(
    cot_hbm, west_ref, east_ref, wout_hbm,
    gm_hbm, gw_hbm, ge_hbm, bw_hbm, be_hbm,
    cot_ref, wout_ref,
    gm_ref, gw_ref, ge_ref, bw_ref, be_ref, in_sems, out_sems,
):
    wout_copy = start_copy(wout_hbm, wout_ref, in_sems.at[0])
    cot_copy = start_copy(cot_hbm, cot_ref, in_sems.at[1])
    wout_copy.wait()
    cot_copy.wait()
    wout = wout_ref[...]
    for i, u in halves():
        part = mm(chunk(cot_ref, i, u), wout, 1, 1)
        gm_ref[rows_of(i, u), :] = part.astype(bf16)
    outs = [start_copy(gm_ref, gm_hbm, out_sems.at[0])]
    second_q = iota((TILE, TILE), 0) % HALF >= BLOCK
    for n, (src, dst, bias_ref, dst_hbm, bias_hbm) in enumerate(
        (
            (west_ref, gw_ref, bw_ref, gw_hbm, bw_hbm),
            (east_ref, ge_ref, be_ref, ge_hbm, be_hbm),
        )
    ):
        rows = src.shape[0] - 1
        part = mm(src[0:rows].reshape(2 * TILE, wout.shape[0]), wout, 1, 1)
        dst[...] = part.astype(bf16)
        extra = src[rows].astype(f32)
        for i in range(2):
            line = extra[i : i + 1, :]
            mask = jnp.where(second_q, line[:, TILE : 2 * TILE], line[:, 0:TILE])
            count = jnp.where(second_q, line[:, 3 * TILE : 4 * TILE], line[:, 2 * TILE : 3 * TILE])
            bias = -0.5 * jnp.log(count * 64.0)
            bias_ref[i * TILE : (i + 1) * TILE, :] = jnp.where(mask > 0.5, bias, MASKED)
        outs += [
            start_copy(dst, dst_hbm, out_sems.at[1 + 2 * n]),
            start_copy(bias_ref, bias_hbm, out_sems.at[2 + 2 * n]),
        ]
    for copy in outs:
        copy.wait()


def slot_table(geo, tails, pixels):
    pick = one_hot(
        iota((geo.devs, geo.devs * geo.tail), 1) == iota((geo.devs, geo.devs * geo.tail), 0) * geo.tail + geo.mark
    )
    meta = mm(pick, tails).astype(bf16)
    codes = []
    if geo.full:
        shape = (geo.devs, geo.full, geo.devs)
        owner = one_hot(iota(shape, 0) == iota(shape, 2)).reshape(geo.bulk, geo.devs)
        place = iota((geo.devs, geo.full, 128), 1).reshape(geo.bulk, 128)
        lane = iota((geo.bulk, 128), 1)
        scale = jnp.where(lane == place, 32.0, 0.0) + jnp.where(lane == place + 64, 1.0, 0.0)
        codes.append(jnp.sum(mm(owner, meta) * scale, axis=1, keepdims=True))
    spare = meta.astype(f32)
    for r in range(geo.full, geo.cap):
        codes.append(spare[:, r : r + 1] * 32.0 + spare[:, 64 + r : 65 + r])
    code = jnp.concatenate(codes, axis=0).astype(i32)
    return one_hot(code == iota((geo.total, pixels), 1) + 1)


def state_body(geo, arr_ref, wenc_ref, bg_ref, state_ref, n_ref, n0_ref, n1_ref, inv_ref, rms_ref, oht_ref):
    feats = wenc_ref.shape[0]
    tails, arr = join_slots(geo, arr_ref, feats)
    oht = slot_table(geo, tails, n_ref.shape[0])
    oht_ref[...] = oht
    pre = mm(arr, wenc_ref[...])
    _, tangent = gelu_parts(pre)
    encoded = (0.5 * pre * (1.0 + tangent)).astype(bf16)
    obs_sum = mm(oht, encoded, 0, 0)
    number = mm(oht, jnp.ones((geo.total, 128), bf16), 0, 0)
    inverse = 1.0 / (1.0 + number)
    inv_ref[...] = inverse
    for i, u in halves():
        rows = rows_of(i, u)
        fresh = obs_sum[rows] * inverse[rows, 0:1]
        state = (chunk(bg_ref, i, u).astype(f32) + fresh).astype(bf16)
        state_ref[rows, :] = state
        wide_state = state.astype(f32)
        inv_rms = lax.rsqrt(jnp.mean(wide_state * wide_state, axis=1, keepdims=True) + norm_eps)
        rms_ref[rows, :] = jnp.broadcast_to(inv_rms, (TILE, 128))
        normed = (wide_state * inv_rms).astype(bf16)
        n_ref[rows, :] = normed
        side = n1_ref if u else n0_ref
        side[i * TILE : (i + 1) * TILE, :] = normed


def head_lanes(shape, head, dim=1):
    return lax.shift_right_logical(iota(shape, dim), 6) == head


def split_heads(slab):
    return [jnp.where(head_lanes(slab.shape, h), slab, jnp.zeros((), slab.dtype)) for h in range(2)]


def across(lanes, width):
    return jnp.concatenate([lanes] * (width // lanes.shape[1]), axis=1)


def stack_heads(slab):
    return jnp.concatenate(split_heads(slab), axis=0)


def weigh(score, grad, bias):
    weight = jnp.tanh(score + bias) + 1.0
    slope = grad * weight * (2.0 - weight)
    return weight.astype(bf16), slope.astype(bf16)


def project(src, wqkv_ref, q_ref, k_ref, v_ref, rows):
    chans = src.shape[1]
    q_ref[rows, :] = (mm(src, wqkv_ref[:, 0:chans]) * 0.0625).astype(bf16)
    k_ref[rows, :] = mm(src, wqkv_ref[:, chans : 2 * chans]).astype(bf16)
    v_ref[rows, :] = mm(src, wqkv_ref[:, 2 * chans : 3 * chans]).astype(bf16)


def slab_lanes(s):
    return slice(s * SLAB, (s + 1) * SLAB)


def own_body(
    geo, n_ref, wqkv_ref, gm_ref, pat_hbm, arr_ref, wenc_ref, state_ref,
    q_ref, k_ref, v_ref, dq_ref, dk_ref, dv_ref, slope_ref, weight_hbm, v_hbm, state_hbm,
    pat_ref, weight_ref, sems,
):
    chans = n_ref.shape[1]
    pat_copy = start_copy(pat_hbm, pat_ref, sems.at[0])
    state_copy = start_copy(state_ref, state_hbm, sems.at[1])
    project(n_ref[...], wqkv_ref, q_ref, k_ref, v_ref, slice(0, n_ref.shape[0]))
    v_copy = start_copy(v_ref, v_hbm, sems.at[2])
    pat_copy.wait()
    biases = []
    for i in range(2):
        bias = [
            jnp.concatenate([own_bias(pat_ref, i, u, -u), own_bias(pat_ref, i, u, 1 - u)], axis=1)
            for u in range(2)
        ]
        biases.append(jnp.concatenate(bias, axis=0))

    def first(item, _):
        i, s, h = item
        keys, lanes = slice(i * 2 * TILE, (i + 1) * 2 * TILE), slab_lanes(s)
        km = split_heads(k_ref[keys, lanes])[h]
        vm = split_heads(v_ref[keys, lanes])[h]
        return km, mm(q_ref[keys, lanes], km, 1, 1), mm(gm_ref[keys, lanes], vm, 1, 1)

    def second(item, state):
        i, s, h = item
        km, score, grad = state
        weight, slope = weigh(score, grad, biases[i])
        weight_ref[i, 2 * s + h] = weight
        return km, weight, slope

    held, weight_copies = {}, []

    def third(item, state):
        i, s, h = item
        keys, lanes = slice(i * 2 * TILE, (i + 1) * 2 * TILE), slab_lanes(s)
        km, weight, slope = state
        parts = (
            mm(slope, km),
            mm(slope, q_ref[keys, lanes], 0, 0),
            mm(weight, gm_ref[keys, lanes], 0, 0),
        )
        if h == 0:
            held[i, s] = parts
            return
        before = held.pop((i, s))
        lower = iota((2 * TILE, SLAB), 1) < SLAB // 2
        dq_ref[keys, lanes] = before[0] + parts[0]
        dk_ref[keys, lanes] = jnp.where(lower, before[1], parts[1])
        dv_ref[keys, lanes] = jnp.where(lower, before[2], parts[2])
        pair = (i, slice(2 * s, 2 * s + 2))
        sem = sems.at[3 + i * (chans // SLAB) + s]
        weight_copies.append(start_copy(weight_ref.at[pair], weight_hbm.at[pair], sem))

    pipeline(
        [(i, s, h) for i in range(2) for s in range(chans // SLAB) for h in range(2)],
        (first, second, third),
    )
    arr = join_slots(geo, arr_ref, wenc_ref.shape[0])[1]
    pre = mm(arr, wenc_ref[...])
    square, tangent = gelu_parts(pre)
    slope_ref[...] = 0.5 * (1.0 + tangent) + 0.5 * pre * (1.0 - tangent * tangent) * gelu_coef * (
        1.0 + 3.0 * 0.044715 * square
    )
    for copy in [state_copy, v_copy] + weight_copies:
        copy.wait()


def rim_body(
    geo, nw_ref, ne_ref, wqkv_ref, q_ref, k_ref, v_ref, gm_ref, gw_ref, ge_ref,
    bw_ref, be_ref, pat_hbm, dq_ref, dk_ref, dv_ref, state_ref, rms_ref, cot_ref, inv_ref,
    oht_ref, slope_ref, wenc_ref,
    v_hbm, weight_hbm, gback_hbm, reply_hbm,
    pat_ref, rim_q, rim_k, rim_v, weight_ref, gback_ref, scaled_ref, grad_ref, reply_ref, tail_ref, sems,
):
    chans = q_ref.shape[1]
    pat_copy = start_copy(pat_hbm, pat_ref, sems.at[0])
    far_rows = [slice(side * 2 * TILE, (side + 1) * 2 * TILE) for side in range(2)]
    project(nw_ref[...], wqkv_ref, rim_q, rim_k, rim_v, far_rows[0])
    pat_copy.wait()
    out_bias, in_bias = {}, {}
    for i in range(2):
        for side, bias_ref in enumerate((bw_ref, be_ref)):
            bias = own_bias(pat_ref, i, side, 2 * side - 1)
            out_bias[i, side] = jnp.concatenate([bias, bias], axis=1)
            bias = bias_ref[i * TILE : (i + 1) * TILE, :]
            in_bias[i, side] = jnp.concatenate([bias, bias], axis=1)

    def where(item):
        i, side, s = item
        far = slice((side * 2 + i) * TILE, (side * 2 + i + 1) * TILE)
        near = slice(i * TILE, (i + 1) * TILE)
        return rows_of(i, side), far, near, (gw_ref, ge_ref)[side], slab_lanes(s)

    def first(item, _):
        own, far, near, gh_ref, lanes = where(item)
        km = stack_heads(rim_k[far, lanes])
        return (
            km,
            mm(q_ref[own, lanes], km, 1, 1),
            mm(gm_ref[own, lanes], stack_heads(rim_v[far, lanes]), 1, 1),
            mm(rim_q[far, lanes], stack_heads(k_ref[own, lanes]), 1, 1),
            mm(gh_ref[near, lanes], stack_heads(v_ref[own, lanes]), 1, 1),
        )

    def second(item, state):
        i, side, s = item
        km, score_out, grad_out, score_in, grad_in = state
        weight, slope_out = weigh(score_out, grad_out, out_bias[i, side])
        weight_ref[i * 2 + side, s] = weight
        weight_in, slope_in = weigh(score_in, grad_in, in_bias[i, side])
        return km, slope_out, weight_in, slope_in

    def third(item, state):
        own, far, near, gh_ref, lanes = where(item)
        km, slope_out, weight_in, slope_in = state
        grad_q = mm(slope_out, km)
        grad_k = mm(slope_in, rim_q[far, lanes], 0, 0)
        grad_v = mm(weight_in, gh_ref[near, lanes], 0, 0)
        lower = iota((TILE, SLAB), 1) < SLAB // 2
        grad_k = jnp.where(lower, grad_k[0:TILE], grad_k[TILE:])
        grad_v = jnp.where(lower, grad_v[0:TILE], grad_v[TILE:])
        for n, total in enumerate(
            (
                (dq_ref[own, lanes] + grad_q) * 0.03125,
                (dk_ref[own, lanes] + grad_k) * 0.5,
                (dv_ref[own, lanes] + grad_v) * 0.5,
            )
        ):
            spot = slice(n * chans + lanes.start, n * chans + lanes.stop)
            grad_ref[own, spot] = total.astype(bf16)

    back = {}

    def project_back(group):
        back[group] = mm(grad_ref[rows_of(*group), :], wqkv_ref[...], 1, 1)

    def norm_back(item):
        i, u = item
        total = back.pop(item)
        cot = chunk(cot_ref, i, u)
        for n in range(0, TILE, STRIP):
            base = rows_of(i, u).start + n
            rows = slice(base, base + STRIP)
            inv_rms = across(rms_ref[rows, :], chans)
            normed = state_ref[rows, :].astype(f32) * inv_rms
            grad = total[n : n + STRIP]
            grad_state = cot[n : n + STRIP].astype(f32) + inv_rms * (
                grad - normed * jnp.mean(grad * normed, axis=1, keepdims=True)
            )
            gback_ref[rows, :] = grad_state.astype(bf16)
            scaled_ref[rows, :] = (grad_state * across(inv_ref[rows, :], chans)).astype(bf16)

    slabs = chans // SLAB
    groups = [(i, side) for side in range(2) for i in range(2)]
    extra = {
        1: [lambda: project(ne_ref[...], wqkv_ref, rim_q, rim_k, rim_v, far_rows[1])],
    }
    for n, group in enumerate(groups):
        ready = slabs * (n + 1) // BATCH + 1
        extra.setdefault(ready, []).append(functools.partial(project_back, group))
        extra.setdefault(ready + 1, []).append(functools.partial(norm_back, group))
    items = [(i, side, s) for i, side in groups for s in range(slabs)]
    pipeline(*batch(items, (first, second, third), BATCH), extra)
    v_copy = start_copy(rim_v, v_hbm, sems.at[1])
    weight_copy = start_copy(weight_ref, weight_hbm, sems.at[2])
    gback_copy = start_copy(gback_ref, gback_hbm, sems.at[3])

    def pre_grad(lo, hi):
        return (mm(oht_ref[lo:hi, :], scaled_ref[...]) * slope_ref[lo:hi, :]).astype(bf16)

    half = wenc_ref.shape[0] // 2
    tail_ref[...] = jnp.zeros(tail_ref.shape, f32)
    if geo.rest:
        spare = mm(pre_grad(geo.bulk, geo.total), wenc_ref[...], 1, 1)
        for n in range(2):
            for r in range(geo.rest):
                part = spare[r * geo.devs : (r + 1) * geo.devs, n * half : (n + 1) * half]
                tail_ref[:, n * geo.shift + r, :] = part
    reply_ref[:, 2 * geo.full : geo.rows, :] = tail_ref[...].astype(bf16)
    replies = send_groups(
        geo, reply_ref, reply_hbm, sems, 4,
        (
            lambda item, _: pre_grad(item[1] * geo.full, item[2] * geo.full),
            lambda item, rows: mm(rows, wenc_ref[...], 1, 1),
        ),
    )
    for copy in [v_copy, weight_copy, gback_copy] + replies:
        copy.wait()


def out_body(*refs):
    hbm, (out_ref, back_ref), local, (mixed_ref, sems) = refs[:7], refs[7:9], refs[9:16], refs[16:]
    copies = [start_copy(src, dst, sems.at[n]) for n, (src, dst) in enumerate(zip(hbm, local))]
    for copy in copies:
        copy.wait()
    weight_ref, far_ref, v_ref, rim_v, wout_ref, state_ref, gback_ref = local
    chans = wout_ref.shape[0]
    for i in range(2):
        keys = slice(i * 2 * TILE, (i + 1) * 2 * TILE)
        for s in range(chans // SLAB):
            lanes = slice(s * SLAB, (s + 1) * SLAB)
            vm = split_heads(v_ref[keys, lanes])
            mixed = mm(weight_ref[i, 2 * s], vm[0]) + mm(weight_ref[i, 2 * s + 1], vm[1])
            for side in range(2):
                far = slice((side * 2 + i) * TILE, (side * 2 + i + 1) * TILE)
                total = mixed[side * TILE : (side + 1) * TILE] + mm(
                    far_ref[i * 2 + side, s], stack_heads(rim_v[far, lanes])
                )
                mixed_ref[rows_of(i, side), lanes] = (total * 0.5).astype(bf16)
    for i, u in halves():
        rows = rows_of(i, u)
        place = (slice(i * BLOCK, (i + 1) * BLOCK), slice(u * HALF, (u + 1) * HALF))
        total = state_ref[rows, :].astype(f32) + mm(mixed_ref[rows, :], wout_ref[...])
        out_ref[place[0], place[1], :] = total.astype(bf16).reshape(BLOCK, HALF, chans)
        back_ref[place[0], place[1], :] = gback_ref[rows, :].reshape(BLOCK, HALF, chans)


def unpack_body(geo, back_ref, slot_ref, out_hbm, out_ref, sems):
    slots, feats = out_ref.shape
    rows = join_slots(geo, back_ref, feats)[1]
    step = slots // GROUPS
    copies = []
    for n in range(GROUPS):
        part = slice(n * step, (n + 1) * step)
        spread = one_hot(iota((geo.total, step), 0) == slot_ref[:, part])
        out_ref[part, :] = mm(spread, rows, 0, 0).astype(bf16)
        copies.append(start_copy(out_ref.at[part], out_hbm.at[part], sems.at[n]))
    for copy in copies:
        copy.wait()


def shards(
    background, obs_rows, obs_pixel, obs_count, block_pattern, w_enc, w_qkv, w_out, cotangent
):
    lat_rows, lon_cols, chans = background.shape
    pixels = lat_rows * lon_cols
    slots, feats = obs_rows.shape
    lon_devs = lax.axis_size("lon")
    geo = Geometry(slots, lax.axis_size("lat") * lon_devs, lon_devs, lon_cols)
    side = pixels // 2
    half = feats // 2
    up = [(i, (i + 1) % lon_devs) for i in range(lon_devs)]
    down = [(j, i) for i, j in up]

    rim = (lat_rows + 1, HALF, chans)
    wide, edge = (pixels, chans), (side, chans)
    weights_own = (2, HEADS, 2 * TILE, 2 * TILE)
    weights_far = (4, chans // SLAB, TILE, 2 * TILE)
    dma = pltpu.SemaphoreType.DMA
    pattern = pltpu.SMEM(block_pattern.shape, i32)

    def vmem(*shapes):
        return [pltpu.VMEM(shape, bf16) for shape in shapes]

    payload, slot, cot_east, cot_west = call(
        functools.partial(pack_body, geo),
        [((geo.devs, geo.rows, half), bf16), ((1, slots), i32), (rim, bf16), (rim, bf16)],
        scratch=[pltpu.VMEM((1, slots), i32), pltpu.VMEM((slots, feats), bf16), pattern]
        + vmem((geo.devs, geo.rows, half), rim, rim)
        + [dma((7 + GROUPS,))],
        n_in=5,
        n_smem=(1,),
        n_hbm=(0, 2, 3, 4),
        out_hbm=(0, 2, 3),
        flops=400 << 20,
    )(obs_pixel.reshape(1, slots), obs_count, obs_rows, block_pattern, cotangent)
    west_cot = lax.ppermute(cot_east, "lon", up)
    east_cot = lax.ppermute(cot_west, "lon", down)
    arrived = lax.all_to_all(payload, ("lat", "lon"), split_axis=0, concat_axis=0, tiled=True)
    gm, gw, ge, bias_w, bias_e = call(
        grad_body,
        [
            (wide, bf16),
            (edge, bf16),
            (edge, bf16),
            ((side, TILE), f32),
            ((side, TILE), f32),
        ],
        scratch=vmem((lat_rows, lon_cols, chans), (chans, chans))
        + vmem(wide, edge, edge)
        + [pltpu.VMEM((side, TILE), f32)] * 2
        + [dma((2,)), dma((5,))],
        n_in=4,
        n_hbm=(0, 3),
        out_hbm=range(5),
        flops=GRAD_COST,
    )(cotangent, west_cot, east_cot, w_out)
    state, normed, n0, n1, inverse, inv_rms, oht = call(
        functools.partial(state_body, geo),
        [
            (wide, bf16),
            (wide, bf16),
            (edge, bf16),
            (edge, bf16),
            ((pixels, 128), f32),
            ((pixels, 128), f32),
            ((geo.total, pixels), bf16),
        ],
        n_in=3,
        flops=1 << 30,
    )(arrived, w_enc, background)
    n_west = lax.ppermute(n1, "lon", up)
    n_east = lax.ppermute(n0, "lon", down)
    q, k, v, dq, dk, dv, slope, weight, v_far, state_far = call(
        functools.partial(own_body, geo),
        [(wide, bf16)] * 3
        + [(wide, f32)] * 3
        + [((geo.total, chans), f32), (weights_own, bf16), (wide, bf16), (wide, bf16)],
        scratch=[pattern] + vmem(weights_own) + [dma((3 + HEADS,))],
        n_in=7,
        n_hbm=(3,),
        out_hbm=(7, 8, 9),
        flops=4 << 30,
    )(normed, w_qkv, gm, block_pattern, arrived, w_enc, state)
    rim_v, far, gback, reply = call(
        functools.partial(rim_body, geo),
        [(wide, bf16), (weights_far, bf16), (wide, bf16), ((geo.devs, geo.rows, half), bf16)],
        scratch=[pattern]
        + vmem(wide, wide, wide, weights_far, wide, wide, (pixels, 3 * chans), (geo.devs, geo.rows, half))
        + [pltpu.VMEM((geo.devs, geo.tail, half), f32), dma((4 + GROUPS,))],
        n_in=22,
        n_hbm=(11,),
        out_hbm=(0, 1, 2, 3),
        flops=4 << 30,
    )(
        n_west, n_east, w_qkv, q, k, v, gm, gw, ge, bias_w, bias_e, block_pattern,
        dq, dk, dv, state, inv_rms, cotangent, inverse, oht, slope, w_enc,
    )
    returned = lax.all_to_all(reply, ("lat", "lon"), split_axis=0, concat_axis=0, tiled=True)
    updated, grad_background = call(
        out_body,
        [((lat_rows, lon_cols, chans), bf16), ((lat_rows, lon_cols, chans), bf16)],
        scratch=vmem(weights_own, weights_far, wide, wide, (chans, chans), wide, wide, wide)
        + [dma((7,))],
        n_in=7,
        n_hbm=range(7),
        flops=1 << 30,
    )(weight, far, v_far, rim_v, w_out, state_far, gback)
    (grad_obs,) = call(
        functools.partial(unpack_body, geo),
        [((slots, feats), bf16)],
        scratch=vmem((slots, feats)) + [dma((GROUPS,))],
        n_in=2,
        out_hbm=(0,),
        flops=1 << 28,
    )(returned, slot)
    return (updated, grad_background, grad_obs)


def solution(mesh):
    return jax.shard_map(
        shards,
        mesh=mesh,
        in_specs=(
            P("lat", "lon", None),
            P(("lat", "lon"), None),
            P(("lat", "lon")),
            P(("lat", "lon")),
            P("lat", "lon", None),
            P(),
            P(),
            P(),
            P("lat", "lon", None),
        ),
        out_specs=(P("lat", "lon", None), P("lat", "lon", None), P(("lat", "lon"), None)),
        check_vma=False,
    )
```
